512 devices in a mesh: space: 16 (over y_hi, x, core), term: 32 (over y_lo, z).
Axes of the slice: x: 4, y: 4 (y_hi: 2, y_lo: 2; y = y_hi * 2 + y_lo), z: 16, core: 2. Of those that a mesh axis runs over, the one named last changes fastest.
Arguments:
- chaos_field: bfloat16 [256, 2, 8192], P('term', None, 'space'), may hold values from -6 to 6
- stiff_blocks: bfloat16 [64, 32, 6, 256, 256], P('term', 'space'), may hold values from -0.15625 to 0.15625
- stiff_offsets: int32 [64, 32, 6], P('term', 'space'), may hold values from -2 to 2
- triple_blocks: bfloat16 [64, 24, 32, 32], P('term'), may hold values from -0.078125 to 0.078125
- triple_pattern: int32 [64, 24, 2], P('term'), may hold values from 0 to 7, as said below
Outputs:
- applied: float32 [256, 2, 8192], P('term', None, 'space')
The draws below stay inside these ranges and needn't reach their ends.
Inputs may be any that keep to these rules, and one draw needn't show every extreme that they name: `triple_pattern`: within one term the 24 pairs of block row and block column are distinct.
All inputs are finite; a program needn't handle non-finite values.
Results may differ from the reference program's by a relative error of at most 0.0029.
Values may be sent and summed in bfloat16 or wider, within the bound.
A program may use at most 64 MiB of HBM per device.

```python
import jax
import jax.numpy as jnp
from jax import lax

P_SIZE = 256
KL = 64
BS = 32
NNZ = 24
SB = 256
SBAND = 6
LOADS = 2
N = 8192
NB = 32


def draw_triple_pattern(key, part):
    block_count = P_SIZE // BS
    keys = jax.random.split(jax.random.fold_in(key, 11), KL)

    def one_term(term_key):
        chosen = jax.random.permutation(term_key, block_count * block_count)[:NNZ]
        return jnp.stack([chosen // block_count, chosen % block_count], axis=-1)
    return jax.vmap(one_term)(keys).astype(jnp.int32)


def touch_ends(entries, key, low, top_value):
    longest = entries.shape.index(max(entries.shape))
    spots = []
    for shift in (0, 1):
        where = [jax.random.randint(jax.random.fold_in(key, axis), (), 0, length) for axis, length in enumerate(entries.shape)]
        where[longest] = (where[longest] + shift) % entries.shape[longest]
        spots.append(tuple(where))
    return entries.at[spots[0]].set(low).at[spots[1]].set(top_value)


def block_scale(own_key, dims, shards, low, high):
    def one(dim, parts):
        steps = jax.random.uniform(jax.random.fold_in(jax.random.fold_in(own_key, 6), dim), (parts,), jnp.float32, low / len(shards), high / len(shards))
        return jnp.repeat(jnp.exp(steps), dims[dim] // parts).reshape((-1,) + (1,) * (len(dims) - dim - 1))

    loudness = one(*shards[0])
    for cut in shards[1:]:
        loudness = loudness * one(*cut)
    return loudness


def noise(key, dims, deviation, limit, shards=(), kind=jnp.bfloat16):
    values = jax.random.normal(key, dims, jnp.float32) * deviation
    if len(shards) > 0:
        values = block_scale(key, dims, shards, -0.22, 0.18) * values
    return jnp.clip(values, min=-limit, max=limit).astype(kind)


def setup_inputs(seed: int = 0) -> dict:
    splits = jax.random.split(jax.random.key(seed), 6)
    return {
        "chaos_field": noise(splits[0], (P_SIZE, LOADS, N), 1.0, 6.0, ((0, 32), (2, 16))),
        "stiff_blocks": noise(splits[1], (KL, NB, SBAND, SB, SB), (SBAND * SB) ** -0.5, 0.15625, ((0, 32), (1, 16))),
        "stiff_offsets": touch_ends(jax.random.randint(splits[2], (KL, NB, SBAND), -2, 3), jax.random.fold_in(splits[2], 1), -2, 2).astype(jnp.int32),
        "triple_blocks": noise(splits[3], (KL, NNZ, BS, BS), (KL * NNZ * BS // (P_SIZE // BS)) ** -0.5, 0.078125, ((0, 32),)),
        "triple_pattern": draw_triple_pattern(jax.random.fold_in(splits[5], 71), 0),
    }


def reference(chaos_field, stiff_blocks, stiff_offsets, triple_blocks, triple_pattern):
    grid_panel = chaos_field.astype(jnp.float32).reshape(P_SIZE, LOADS, NB, SB)
    grid_panel = jnp.pad(grid_panel, ((0, 0), (0, 0), (2, 2), (0, 0)))
    block_index = jnp.arange(NB, dtype=jnp.int32)[:, None]
    levels = jnp.arange(P_SIZE // BS, dtype=jnp.int32)

    def one_term(total, inputs):
        blocks, offsets, values, pattern = inputs
        picked = jnp.take(grid_panel, block_index + 2 + offsets.astype(jnp.int32), axis=2)
        image = jnp.einsum("bsdc,prbsc->prbd", blocks.astype(jnp.float32), picked).astype(jnp.bfloat16)
        image = lax.optimization_barrier(image)
        row_hot = (pattern[:, 0:1] == levels).astype(jnp.float32)
        col_hot = (pattern[:, 1:2] == levels).astype(jnp.float32)
        dense = jnp.einsum("na,nb,nxy->axby", row_hot, col_hot, values.astype(jnp.float32)).reshape(P_SIZE, P_SIZE)
        total = total + jnp.dot(dense, image.astype(jnp.float32).reshape(P_SIZE, LOADS * NB * SB))
        return total, None

    start_total = jnp.zeros((P_SIZE, LOADS * NB * SB), jnp.float32)
    total, unused = lax.scan(one_term, start_total, (stiff_blocks, stiff_offsets, triple_blocks, triple_pattern))
    return total.reshape(P_SIZE, LOADS, NB * SB)
```

```python
import jax
import jax.numpy as jnp
from jax import lax
from jax.experimental import pallas as pl
from jax.experimental.pallas import tpu as pltpu
from jax.sharding import PartitionSpec as P

MESH_ID = pl.DeviceIdType.MESH


def greet_peers(count):
    me = lax.axis_index("term")
    row = lax.axis_index("space")
    barrier = pltpu.get_barrier_semaphore()

    def greet(step, carry):
        peer = lax.rem(me + step, count)
        pl.semaphore_signal(barrier, 1, device_id=(row, peer), device_id_type=MESH_ID)
        return carry

    lax.fori_loop(1, count, greet, 0)
    pl.semaphore_wait(barrier, count - 1)
    return me, row


def gather_kernel(block_ref, out_ref, send_sems, recv_sems):
    count = out_ref.shape[0]
    me, row = greet_peers(count)

    def outgoing(step):
        peer = lax.rem(me + step, count)
        return pltpu.make_async_remote_copy(
            block_ref, out_ref.at[me], send_sems.at[step], recv_sems.at[me],
            device_id=(row, peer), device_id_type=MESH_ID,
        )

    def incoming(step):
        source = lax.rem(me + count - step, count)
        return pltpu.make_async_remote_copy(
            block_ref, out_ref.at[source], send_sems.at[step], recv_sems.at[source],
            device_id=(row, source), device_id_type=MESH_ID,
        )

    def start(step, carry):
        outgoing(step).start()
        return carry

    lax.fori_loop(1, count, start, 0)
    out_ref[me] = block_ref[...]

    def finish(step, carry):
        outgoing(step).wait_send()
        incoming(step).wait_recv()
        return carry

    lax.fori_loop(1, count, finish, 0)


def gather_term(block):
    count = lax.axis_size("term")
    return pl.pallas_call(
        gather_kernel,
        out_shape=jax.ShapeDtypeStruct((count,) + block.shape, block.dtype),
        in_specs=[pl.BlockSpec(memory_space=pltpu.VMEM)],
        out_specs=pl.BlockSpec(memory_space=pltpu.VMEM),
        scratch_shapes=[pltpu.SemaphoreType.DMA((count,)), pltpu.SemaphoreType.DMA((count,))],
        compiler_params=pltpu.CompilerParams(collective_id=0, has_side_effects=True),
    )(block)


def scatter_kernel(part_ref, out_ref, slots, send_sems, recv_sems):
    count = part_ref.shape[0]
    me, row = greet_peers(count)

    def outgoing(step):
        peer = lax.rem(me + step, count)
        return pltpu.make_async_remote_copy(
            part_ref.at[peer], slots.at[me], send_sems.at[step], recv_sems.at[me],
            device_id=(row, peer), device_id_type=MESH_ID,
        )

    def incoming(step):
        source = lax.rem(me + count - step, count)
        return pltpu.make_async_remote_copy(
            part_ref.at[source], slots.at[source], send_sems.at[step], recv_sems.at[source],
            device_id=(row, source), device_id_type=MESH_ID,
        )

    def start(step, carry):
        outgoing(step).start()
        return carry

    lax.fori_loop(1, count, start, 0)

    def finish(step, total):
        outgoing(step).wait_send()
        incoming(step).wait_recv()
        source = lax.rem(me + count - step, count)
        return total + slots[source]

    out_ref[...] = lax.fori_loop(1, count, finish, part_ref[me])


def scatter_term(parts):
    count = parts.shape[0]
    return pl.pallas_call(
        scatter_kernel,
        out_shape=jax.ShapeDtypeStruct(parts.shape[1:], parts.dtype),
        in_specs=[pl.BlockSpec(memory_space=pltpu.VMEM)],
        out_specs=pl.BlockSpec(memory_space=pltpu.VMEM),
        scratch_shapes=[
            pltpu.VMEM(parts.shape, parts.dtype),
            pltpu.SemaphoreType.DMA((count,)),
            pltpu.SemaphoreType.DMA((count,)),
        ],
        compiler_params=pltpu.CompilerParams(collective_id=1, has_side_effects=True),
    )(parts)


def with_halo(block, sides, width):
    for axis, dim in sides:
        count = lax.axis_size(axis)
        forward = [(i, i + 1) for i in range(count - 1)]
        backward = [(target, source) for source, target in forward]
        low = lax.ppermute(
            lax.slice_in_dim(block, block.shape[dim] - width, None, axis=dim), axis, forward
        )
        high = lax.ppermute(lax.slice_in_dim(block, 0, width, axis=dim), axis, backward)
        block = jnp.concatenate([low, block, high], axis=dim)
    return block


def per_device(chaos_field, stiff_blocks, stiff_offsets, triple_blocks, triple_pattern):
    local_rows = chaos_field.shape[0]
    load_count = chaos_field.shape[1]
    cell_count = chaos_field.shape[2]
    term_count = stiff_blocks.shape[0]
    block_width = stiff_blocks.shape[3]
    block_rows = cell_count // block_width
    groups = lax.axis_size("term")
    total_rows = local_rows * groups
    rim_cells = 2 * block_width
    gathered = gather_term(chaos_field.reshape(local_rows * load_count, cell_count))
    gathered = gathered.reshape(total_rows, load_count, cell_count)
    extended = with_halo(gathered, (("space", 2),), rim_cells)
    row_count = extended.shape[0]
    grid_panel = extended.reshape(row_count, load_count, block_rows + 4, block_width)
    base_index = jnp.arange(block_rows, dtype=jnp.int32)[:, None] + 2
    found_images = []
    for term_slot in range(term_count):
        picked = jnp.take(grid_panel, base_index + stiff_offsets[term_slot], axis=2)
        product = jnp.einsum(
            "bsdc,prbsc->prbd", stiff_blocks[term_slot], picked, preferred_element_type=jnp.float32
        )
        found_images.append(product.astype(jnp.bfloat16))
    images = jnp.stack(found_images).reshape(term_count, row_count, load_count, cell_count)
    block_size = triple_blocks.shape[2]
    levels = jnp.arange(total_rows // block_size, dtype=jnp.int32)
    row_hot = (triple_pattern[:, :, 0:1] == levels).astype(jnp.float32)
    col_hot = (triple_pattern[:, :, 1:2] == levels).astype(jnp.float32)
    dense = jnp.einsum("kna,knb,knxy->kaxby", row_hot, col_hot, triple_blocks.astype(jnp.float32))
    dense = dense.reshape(term_count, total_rows, total_rows).astype(jnp.bfloat16)
    flat_images = images.reshape(term_count, total_rows, load_count * cell_count)
    partial = jnp.einsum("kij,kjm->im", dense, flat_images, preferred_element_type=jnp.float32)
    summed = scatter_term(partial.reshape(groups, local_rows, load_count * cell_count))
    return summed.reshape(local_rows, load_count, cell_count)


def solution(mesh):
    return jax.shard_map(
        per_device,
        mesh=mesh,
        in_specs=(
            P("term", None, "space"),
            P("term", "space", None, None, None),
            P("term", "space", None),
            P("term", None, None, None),
            P("term", None, None),
        ),
        out_specs=P("term", None, "space"),
        check_vma=False,
    )
```

```python
import jax
import jax.numpy as jnp
from jax import lax
from jax.experimental import pallas as pl
from jax.experimental.pallas import tpu as pltpu
from jax.sharding import PartitionSpec as P

MESH_ID = pl.DeviceIdType.MESH


def greet_peers(count):
    me = lax.axis_index("term")
    row = lax.axis_index("space")
    barrier = pltpu.get_barrier_semaphore()

    def greet(step, carry):
        peer = lax.rem(me + step, count)
        pl.semaphore_signal(barrier, 1, device_id=(row, peer), device_id_type=MESH_ID)
        return carry

    lax.fori_loop(1, count, greet, 0)
    pl.semaphore_wait(barrier, count - 1)
    return me, row


def gather_kernel(block_ref, out_ref, send_sems, recv_sems):
    count = out_ref.shape[0]
    me, row = greet_peers(count)

    def outgoing(step):
        peer = lax.rem(me + step, count)
        return pltpu.make_async_remote_copy(
            block_ref, out_ref.at[me], send_sems.at[step], recv_sems.at[me],
            device_id=(row, peer), device_id_type=MESH_ID,
        )

    def incoming(step):
        source = lax.rem(me + count - step, count)
        return pltpu.make_async_remote_copy(
            block_ref, out_ref.at[source], send_sems.at[step], recv_sems.at[source],
            device_id=(row, source), device_id_type=MESH_ID,
        )

    def start(step, carry):
        outgoing(step).start()
        return carry

    lax.fori_loop(1, count, start, 0)
    out_ref[me] = block_ref[...]

    def finish(step, carry):
        outgoing(step).wait_send()
        incoming(step).wait_recv()
        return carry

    lax.fori_loop(1, count, finish, 0)


def gather_term(block):
    count = lax.axis_size("term")
    return pl.pallas_call(
        gather_kernel,
        out_shape=jax.ShapeDtypeStruct((count,) + block.shape, block.dtype),
        in_specs=[pl.BlockSpec(memory_space=pltpu.VMEM)],
        out_specs=pl.BlockSpec(memory_space=pltpu.VMEM),
        scratch_shapes=[pltpu.SemaphoreType.DMA((count,)), pltpu.SemaphoreType.DMA((count,))],
        compiler_params=pltpu.CompilerParams(collective_id=0, has_side_effects=True),
    )(block)


def scatter_kernel(part_ref, own_ref, out_ref, slots, send_sems, recv_sems):
    count = part_ref.shape[0]
    me, row = greet_peers(count)

    def outgoing(step):
        peer = lax.rem(me + step, count)
        return pltpu.make_async_remote_copy(
            part_ref.at[peer], slots.at[me], send_sems.at[step], recv_sems.at[me],
            device_id=(row, peer), device_id_type=MESH_ID,
        )

    def incoming(step):
        source = lax.rem(me + count - step, count)
        return pltpu.make_async_remote_copy(
            part_ref.at[source], slots.at[source], send_sems.at[step], recv_sems.at[source],
            device_id=(row, source), device_id_type=MESH_ID,
        )

    def start(step, carry):
        outgoing(step).start()
        return carry

    lax.fori_loop(1, count, start, 0)

    def finish(step, total):
        outgoing(step).wait_send()
        incoming(step).wait_recv()
        source = lax.rem(me + count - step, count)
        return total + slots[source].astype(jnp.float32)

    out_ref[...] = lax.fori_loop(1, count, finish, own_ref[me])


def scatter_term(parts):
    count = parts.shape[0]
    sent = parts.astype(jnp.bfloat16)
    return pl.pallas_call(
        scatter_kernel,
        out_shape=jax.ShapeDtypeStruct(parts.shape[1:], parts.dtype),
        in_specs=[pl.BlockSpec(memory_space=pltpu.VMEM)] * 2,
        out_specs=pl.BlockSpec(memory_space=pltpu.VMEM),
        scratch_shapes=[
            pltpu.VMEM(sent.shape, sent.dtype),
            pltpu.SemaphoreType.DMA((count,)),
            pltpu.SemaphoreType.DMA((count,)),
        ],
        compiler_params=pltpu.CompilerParams(collective_id=1, has_side_effects=True),
    )(sent, parts)


def with_halo(block, sides, width):
    for axis, dim in sides:
        count = lax.axis_size(axis)
        forward = [(i, i + 1) for i in range(count - 1)]
        backward = [(target, source) for source, target in forward]
        low = lax.ppermute(
            lax.slice_in_dim(block, block.shape[dim] - width, None, axis=dim), axis, forward
        )
        high = lax.ppermute(lax.slice_in_dim(block, 0, width, axis=dim), axis, backward)
        block = jnp.concatenate([low, block, high], axis=dim)
    return block


def per_device(chaos_field, stiff_blocks, stiff_offsets, triple_blocks, triple_pattern):
    local_rows = chaos_field.shape[0]
    load_count = chaos_field.shape[1]
    cell_count = chaos_field.shape[2]
    term_count = stiff_blocks.shape[0]
    block_width = stiff_blocks.shape[3]
    block_rows = cell_count // block_width
    groups = lax.axis_size("term")
    total_rows = local_rows * groups
    rim_cells = 2 * block_width
    gathered = gather_term(chaos_field.reshape(local_rows * load_count, cell_count))
    gathered = gathered.reshape(total_rows, load_count, cell_count)
    extended = with_halo(gathered, (("space", 2),), rim_cells)
    row_count = extended.shape[0]
    grid_panel = extended.reshape(row_count, load_count, block_rows + 4, block_width)
    base_index = jnp.arange(block_rows, dtype=jnp.int32)[:, None] + 2
    found_images = []
    for term_slot in range(term_count):
        picked = jnp.take(grid_panel, base_index + stiff_offsets[term_slot], axis=2)
        product = jnp.einsum(
            "bsdc,prbsc->prbd", stiff_blocks[term_slot], picked, preferred_element_type=jnp.float32
        )
        found_images.append(product.astype(jnp.bfloat16))
    images = jnp.stack(found_images).reshape(term_count, row_count, load_count, cell_count)
    block_size = triple_blocks.shape[2]
    levels = jnp.arange(total_rows // block_size, dtype=jnp.int32)
    row_hot = (triple_pattern[:, :, 0:1] == levels).astype(jnp.float32)
    col_hot = (triple_pattern[:, :, 1:2] == levels).astype(jnp.float32)
    dense = jnp.einsum("kna,knb,knxy->kaxby", row_hot, col_hot, triple_blocks.astype(jnp.float32))
    dense = dense.reshape(term_count, total_rows, total_rows).astype(jnp.bfloat16)
    flat_images = images.reshape(term_count, total_rows, load_count * cell_count)
    partial = jnp.einsum("kij,kjm->im", dense, flat_images, preferred_element_type=jnp.float32)
    summed = scatter_term(partial.reshape(groups, local_rows, load_count * cell_count))
    return summed.reshape(local_rows, load_count, cell_count)


def solution(mesh):
    return jax.shard_map(
        per_device,
        mesh=mesh,
        in_specs=(
            P("term", None, "space"),
            P("term", "space", None, None, None),
            P("term", "space", None),
            P("term", None, None, None),
            P("term", None, None),
        ),
        out_specs=P("term", None, "space"),
        check_vma=False,
    )
```

```python
import jax
import jax.numpy as jnp
from jax import lax
from jax.experimental import pallas as pl
from jax.experimental.pallas import tpu as pltpu
from jax.sharding import PartitionSpec as P

MESH_ID = pl.DeviceIdType.MESH


def greet_peers(count):
    me = lax.axis_index("term")
    row = lax.axis_index("space")
    barrier = pltpu.get_barrier_semaphore()

    def greet(step, carry):
        peer = lax.rem(me + step, count)
        pl.semaphore_signal(barrier, 1, device_id=(row, peer), device_id_type=MESH_ID)
        return carry

    lax.fori_loop(1, count, greet, 0)
    pl.semaphore_wait(barrier, count - 1)
    return me, row


def gather_kernel(block_ref, out_ref, send_sems, recv_sems):
    count = out_ref.shape[0]
    me, row = greet_peers(count)

    def outgoing(step):
        peer = lax.rem(me + step, count)
        return pltpu.make_async_remote_copy(
            block_ref, out_ref.at[me], send_sems.at[step], recv_sems.at[me],
            device_id=(row, peer), device_id_type=MESH_ID,
        )

    def incoming(step):
        source = lax.rem(me + count - step, count)
        return pltpu.make_async_remote_copy(
            block_ref, out_ref.at[source], send_sems.at[step], recv_sems.at[source],
            device_id=(row, source), device_id_type=MESH_ID,
        )

    def start(step, carry):
        outgoing(step).start()
        return carry

    lax.fori_loop(1, count, start, 0)
    out_ref[me] = block_ref[...]

    def finish(step, carry):
        outgoing(step).wait_send()
        incoming(step).wait_recv()
        return carry

    lax.fori_loop(1, count, finish, 0)


def gather_term(block):
    count = lax.axis_size("term")
    return pl.pallas_call(
        gather_kernel,
        out_shape=jax.ShapeDtypeStruct((count,) + block.shape, block.dtype),
        in_specs=[pl.BlockSpec(memory_space=pltpu.VMEM)],
        out_specs=pl.BlockSpec(memory_space=pltpu.VMEM),
        scratch_shapes=[pltpu.SemaphoreType.DMA((count,)), pltpu.SemaphoreType.DMA((count,))],
        compiler_params=pltpu.CompilerParams(collective_id=0, has_side_effects=True),
    )(block)


def scatter_kernel(part_ref, own_ref, out_ref, slots, send_sems, recv_sems):
    count = part_ref.shape[0]
    me, row = greet_peers(count)

    def outgoing(step):
        peer = lax.rem(me + step, count)
        return pltpu.make_async_remote_copy(
            part_ref.at[peer], slots.at[me], send_sems.at[step], recv_sems.at[me],
            device_id=(row, peer), device_id_type=MESH_ID,
        )

    def incoming(step):
        source = lax.rem(me + count - step, count)
        return pltpu.make_async_remote_copy(
            part_ref.at[source], slots.at[source], send_sems.at[step], recv_sems.at[source],
            device_id=(row, source), device_id_type=MESH_ID,
        )

    def start(step, carry):
        outgoing(step).start()
        return carry

    lax.fori_loop(1, count, start, 0)

    def finish(step, total):
        outgoing(step).wait_send()
        incoming(step).wait_recv()
        source = lax.rem(me + count - step, count)
        return total + slots[source].astype(jnp.float32)

    out_ref[...] = lax.fori_loop(1, count, finish, own_ref[me])


def scatter_term(parts):
    count = parts.shape[0]
    sent = parts.astype(jnp.bfloat16)
    return pl.pallas_call(
        scatter_kernel,
        out_shape=jax.ShapeDtypeStruct(parts.shape[1:], parts.dtype),
        in_specs=[pl.BlockSpec(memory_space=pltpu.VMEM)] * 2,
        out_specs=pl.BlockSpec(memory_space=pltpu.VMEM),
        scratch_shapes=[
            pltpu.VMEM(sent.shape, sent.dtype),
            pltpu.SemaphoreType.DMA((count,)),
            pltpu.SemaphoreType.DMA((count,)),
        ],
        compiler_params=pltpu.CompilerParams(collective_id=1, has_side_effects=True),
    )(sent, parts)


def image_kernel(offs_ref, panel_ref, stiff_ref, triple_ref, out_ref):
    term = pl.program_id(0)
    block = pl.program_id(1)
    block_rows = pl.num_programs(1)
    band = stiff_ref.shape[2]
    width = stiff_ref.shape[-1]
    loads, rows, span = panel_ref.shape
    rim = (span // width - block_rows) // 2

    @pl.when((term == 0) & (block == 0))
    def _():
        out_ref[...] = jnp.zeros_like(out_ref)

    for load in range(loads):
        total = jnp.zeros((rows, width), jnp.float32)
        for slot in range(band):
            place = block + rim + offs_ref[(term * block_rows + block) * band + slot]
            start = pl.multiple_of(place * width, width)
            total += lax.dot_general(
                panel_ref[load, :, pl.ds(start, width)], stiff_ref[0, 0, slot],
                (((1,), (1,)), ((), ())), preferred_element_type=jnp.float32,
            )
        image = total.astype(jnp.bfloat16)
        column = pl.multiple_of((load * block_rows + block) * width, width)
        out_ref[:, pl.ds(column, width)] += jnp.dot(
            triple_ref[0], image, preferred_element_type=jnp.float32
        )


def image_contract(offsets, panel, stiff_blocks, dense):
    term_count, block_rows, band, width, _ = stiff_blocks.shape
    loads, rows, span = panel.shape
    return pl.pallas_call(
        image_kernel,
        out_shape=jax.ShapeDtypeStruct((rows, loads * block_rows * width), jnp.float32),
        grid_spec=pltpu.PrefetchScalarGridSpec(
            num_scalar_prefetch=1,
            grid=(term_count, block_rows),
            in_specs=[
                pl.BlockSpec((loads, rows, span), lambda k, b, offs: (0, 0, 0)),
                pl.BlockSpec((1, 1, band, width, width), lambda k, b, offs: (k, b, 0, 0, 0)),
                pl.BlockSpec((1, rows, rows), lambda k, b, offs: (k, 0, 0)),
            ],
            out_specs=pl.BlockSpec((rows, loads * block_rows * width), lambda k, b, offs: (0, 0)),
        ),
    )(offsets.reshape(-1), panel, stiff_blocks, dense)


def with_halo(block, sides, width):
    for axis, dim in sides:
        count = lax.axis_size(axis)
        forward = [(i, i + 1) for i in range(count - 1)]
        backward = [(target, source) for source, target in forward]
        low = lax.ppermute(
            lax.slice_in_dim(block, block.shape[dim] - width, None, axis=dim), axis, forward
        )
        high = lax.ppermute(lax.slice_in_dim(block, 0, width, axis=dim), axis, backward)
        block = jnp.concatenate([low, block, high], axis=dim)
    return block


def per_device(chaos_field, stiff_blocks, stiff_offsets, triple_blocks, triple_pattern):
    local_rows = chaos_field.shape[0]
    load_count = chaos_field.shape[1]
    cell_count = chaos_field.shape[2]
    term_count = stiff_blocks.shape[0]
    block_width = stiff_blocks.shape[3]
    block_rows = cell_count // block_width
    groups = lax.axis_size("term")
    total_rows = local_rows * groups
    rim_cells = 2 * block_width
    gathered = gather_term(chaos_field.reshape(local_rows * load_count, cell_count))
    panel = gathered.reshape(groups, local_rows, load_count, cell_count).transpose(2, 0, 1, 3)
    panel = panel.reshape(load_count, total_rows, cell_count)
    extended = with_halo(panel, (("space", 2),), rim_cells)
    block_size = triple_blocks.shape[2]
    levels = jnp.arange(total_rows // block_size, dtype=jnp.int32)
    row_hot = (triple_pattern[:, :, 0:1] == levels).astype(jnp.float32)
    col_hot = (triple_pattern[:, :, 1:2] == levels).astype(jnp.float32)
    dense = jnp.einsum("kna,knb,knxy->kaxby", row_hot, col_hot, triple_blocks.astype(jnp.float32))
    dense = dense.reshape(term_count, total_rows, total_rows).astype(jnp.bfloat16)
    partial = image_contract(stiff_offsets, extended, stiff_blocks, dense)
    summed = scatter_term(partial.reshape(groups, local_rows, load_count * cell_count))
    return summed.reshape(local_rows, load_count, cell_count)


def solution(mesh):
    return jax.shard_map(
        per_device,
        mesh=mesh,
        in_specs=(
            P("term", None, "space"),
            P("term", "space", None, None, None),
            P("term", "space", None),
            P("term", None, None, None),
            P("term", None, None),
        ),
        out_specs=P("term", None, "space"),
        check_vma=False,
    )
```

```python
import jax
import jax.numpy as jnp
from jax import lax
from jax.experimental import pallas as pl
from jax.experimental.pallas import tpu as pltpu
from jax.sharding import PartitionSpec as P

MESH_ID = pl.DeviceIdType.MESH


def greet_peers(count):
    me = lax.axis_index("term")
    row = lax.axis_index("space")
    barrier = pltpu.get_barrier_semaphore()

    def greet(step, carry):
        peer = lax.rem(me + step, count)
        pl.semaphore_signal(barrier, 1, device_id=(row, peer), device_id_type=MESH_ID)
        return carry

    lax.fori_loop(1, count, greet, 0)
    pl.semaphore_wait(barrier, count - 1)
    return me, row


CLASSES = 4


def gather_kernel(block_ref, out_ref, local_sem, send_near, recv_near, send_far, recv_far):
    count = out_ref.shape[0]
    chunk = count // CLASSES
    me = lax.axis_index("term")
    row = lax.axis_index("space")
    stride, lane = me // CLASSES, me % CLASSES
    barrier = pltpu.get_barrier_semaphore()

    def far_peer(step):
        return lax.rem(stride + step, chunk) * CLASSES + lane

    def near_peer(step):
        return stride * CLASSES + lax.rem(lane + step, CLASSES)

    def greet_far(step, carry):
        pl.semaphore_signal(barrier, 1, device_id=(row, far_peer(step)), device_id_type=MESH_ID)
        return carry

    def greet_near(step, carry):
        pl.semaphore_signal(barrier, 1, device_id=(row, near_peer(step)), device_id_type=MESH_ID)
        return carry

    lax.fori_loop(1, chunk, greet_far, 0)
    lax.fori_loop(1, CLASSES, greet_near, 0)
    pl.semaphore_wait(barrier, chunk + CLASSES - 2)

    mine = lane * chunk + stride
    local = pltpu.make_async_copy(block_ref, out_ref.at[mine], local_sem)
    local.start()

    def far_out(step):
        return pltpu.make_async_remote_copy(
            block_ref, out_ref.at[mine], send_far.at[step], recv_far.at[stride],
            device_id=(row, far_peer(step)), device_id_type=MESH_ID,
        )

    def far_in(step):
        source = lax.rem(stride + chunk - step, chunk)
        return pltpu.make_async_remote_copy(
            block_ref, out_ref.at[lane * chunk + source], send_far.at[step], recv_far.at[source],
            device_id=(row, source * CLASSES + lane), device_id_type=MESH_ID,
        )

    def far_start(step, carry):
        far_out(step).start()
        return carry

    def far_finish(step, carry):
        far_out(step).wait_send()
        far_in(step).wait_recv()
        return carry

    lax.fori_loop(1, chunk, far_start, 0)
    local.wait()
    lax.fori_loop(1, chunk, far_finish, 0)

    own = out_ref.at[pl.ds(lane * chunk, chunk)]

    def near_out(step):
        return pltpu.make_async_remote_copy(
            own, own, send_near.at[step], recv_near.at[lane],
            device_id=(row, near_peer(step)), device_id_type=MESH_ID,
        )

    def near_in(step):
        source = lax.rem(lane + CLASSES - step, CLASSES)
        theirs = out_ref.at[pl.ds(source * chunk, chunk)]
        return pltpu.make_async_remote_copy(
            theirs, theirs, send_near.at[step], recv_near.at[source],
            device_id=(row, stride * CLASSES + source), device_id_type=MESH_ID,
        )

    def near_start(step, carry):
        near_out(step).start()
        return carry

    def near_finish(step, carry):
        near_out(step).wait_send()
        near_in(step).wait_recv()
        return carry

    lax.fori_loop(1, CLASSES, near_start, 0)
    lax.fori_loop(1, CLASSES, near_finish, 0)


def gather_term(block):
    count = lax.axis_size("term")
    return pl.pallas_call(
        gather_kernel,
        out_shape=jax.ShapeDtypeStruct((count,) + block.shape, block.dtype),
        in_specs=[pl.BlockSpec(memory_space=pltpu.VMEM)],
        out_specs=pl.BlockSpec(memory_space=pltpu.VMEM),
        scratch_shapes=[
            pltpu.SemaphoreType.DMA(()),
            pltpu.SemaphoreType.DMA((CLASSES,)),
            pltpu.SemaphoreType.DMA((CLASSES,)),
            pltpu.SemaphoreType.DMA((count // CLASSES,)),
            pltpu.SemaphoreType.DMA((count // CLASSES,)),
        ],
        compiler_params=pltpu.CompilerParams(collective_id=0, has_side_effects=True),
    )(block)


def scatter_kernel(part_ref, own_ref, out_ref, slots, send_sems, recv_sems):
    count = part_ref.shape[0]
    me, row = greet_peers(count)

    def outgoing(step):
        peer = lax.rem(me + step, count)
        return pltpu.make_async_remote_copy(
            part_ref.at[peer], slots.at[me], send_sems.at[step], recv_sems.at[me],
            device_id=(row, peer), device_id_type=MESH_ID,
        )

    def incoming(step):
        source = lax.rem(me + count - step, count)
        return pltpu.make_async_remote_copy(
            part_ref.at[source], slots.at[source], send_sems.at[step], recv_sems.at[source],
            device_id=(row, source), device_id_type=MESH_ID,
        )

    def start(step, carry):
        outgoing(step).start()
        return carry

    lax.fori_loop(1, count, start, 0)

    def finish(step, total):
        outgoing(step).wait_send()
        incoming(step).wait_recv()
        source = lax.rem(me + count - step, count)
        return total + slots[source].astype(jnp.float32)

    out_ref[...] = lax.fori_loop(1, count, finish, own_ref[me])


def scatter_term(parts):
    count = parts.shape[0]
    sent = parts.astype(jnp.bfloat16)
    return pl.pallas_call(
        scatter_kernel,
        out_shape=jax.ShapeDtypeStruct(parts.shape[1:], parts.dtype),
        in_specs=[pl.BlockSpec(memory_space=pltpu.VMEM)] * 2,
        out_specs=pl.BlockSpec(memory_space=pltpu.VMEM),
        scratch_shapes=[
            pltpu.VMEM(sent.shape, sent.dtype),
            pltpu.SemaphoreType.DMA((count,)),
            pltpu.SemaphoreType.DMA((count,)),
        ],
        compiler_params=pltpu.CompilerParams(collective_id=1, has_side_effects=True),
    )(sent, parts)


def image_kernel(offs_ref, panel_ref, stiff_ref, triple_ref, out_ref):
    term = pl.program_id(0)
    block = pl.program_id(1)
    block_rows = pl.num_programs(1)
    band = stiff_ref.shape[2]
    width = stiff_ref.shape[-1]
    loads, rows, span = panel_ref.shape
    rim = (span // width - block_rows) // 2

    @pl.when((term == 0) & (block == 0))
    def _():
        out_ref[...] = jnp.zeros_like(out_ref)

    for load in range(loads):
        total = jnp.zeros((rows, width), jnp.float32)
        for slot in range(band):
            place = block + rim + offs_ref[(term * block_rows + block) * band + slot]
            start = pl.multiple_of(place * width, width)
            total += lax.dot_general(
                panel_ref[load, :, pl.ds(start, width)], stiff_ref[0, 0, slot],
                (((1,), (1,)), ((), ())), preferred_element_type=jnp.float32,
            )
        image = total.astype(jnp.bfloat16)
        column = pl.multiple_of((load * block_rows + block) * width, width)
        out_ref[:, pl.ds(column, width)] += jnp.dot(
            triple_ref[0], image, preferred_element_type=jnp.float32
        )


def image_contract(offsets, panel, stiff_blocks, dense):
    term_count, block_rows, band, width, _ = stiff_blocks.shape
    loads, rows, span = panel.shape
    return pl.pallas_call(
        image_kernel,
        out_shape=jax.ShapeDtypeStruct((rows, loads * block_rows * width), jnp.float32),
        grid_spec=pltpu.PrefetchScalarGridSpec(
            num_scalar_prefetch=1,
            grid=(term_count, block_rows),
            in_specs=[
                pl.BlockSpec((loads, rows, span), lambda k, b, offs: (0, 0, 0)),
                pl.BlockSpec((1, 1, band, width, width), lambda k, b, offs: (k, b, 0, 0, 0)),
                pl.BlockSpec((1, rows, rows), lambda k, b, offs: (k, 0, 0)),
            ],
            out_specs=pl.BlockSpec((rows, loads * block_rows * width), lambda k, b, offs: (0, 0)),
        ),
    )(offsets.reshape(-1), panel, stiff_blocks, dense)


def with_halo(block, sides, width):
    for axis, dim in sides:
        count = lax.axis_size(axis)
        forward = [(i, i + 1) for i in range(count - 1)]
        backward = [(target, source) for source, target in forward]
        low = lax.ppermute(
            lax.slice_in_dim(block, block.shape[dim] - width, None, axis=dim), axis, forward
        )
        high = lax.ppermute(lax.slice_in_dim(block, 0, width, axis=dim), axis, backward)
        block = jnp.concatenate([low, block, high], axis=dim)
    return block


def per_device(chaos_field, stiff_blocks, stiff_offsets, triple_blocks, triple_pattern):
    local_rows = chaos_field.shape[0]
    load_count = chaos_field.shape[1]
    cell_count = chaos_field.shape[2]
    term_count = stiff_blocks.shape[0]
    block_width = stiff_blocks.shape[3]
    block_rows = cell_count // block_width
    groups = lax.axis_size("term")
    total_rows = local_rows * groups
    rim_cells = 2 * block_width
    gathered = gather_term(chaos_field.reshape(local_rows * load_count, cell_count))
    panel = gathered.reshape(groups, local_rows, load_count, cell_count).transpose(2, 0, 1, 3)
    panel = panel.reshape(load_count, total_rows, cell_count)
    extended = with_halo(panel, (("space", 2),), rim_cells)
    block_size = triple_blocks.shape[2]
    levels = jnp.arange(total_rows // block_size, dtype=jnp.int32)
    row_hot = (triple_pattern[:, :, 0:1] == levels).astype(jnp.float32)
    col_hot = (triple_pattern[:, :, 1:2] == levels).astype(jnp.float32)
    dense = jnp.einsum("kna,knb,knxy->kaxby", row_hot, col_hot, triple_blocks.astype(jnp.float32))
    dense = dense.reshape(term_count, total_rows, groups // CLASSES, CLASSES, local_rows)
    dense = dense.transpose(0, 1, 3, 2, 4).reshape(term_count, total_rows, total_rows)
    dense = dense.astype(jnp.bfloat16)
    partial = image_contract(stiff_offsets, extended, stiff_blocks, dense)
    summed = scatter_term(partial.reshape(groups, local_rows, load_count * cell_count))
    return summed.reshape(local_rows, load_count, cell_count)


def solution(mesh):
    return jax.shard_map(
        per_device,
        mesh=mesh,
        in_specs=(
            P("term", None, "space"),
            P("term", "space", None, None, None),
            P("term", "space", None),
            P("term", None, None, None),
            P("term", None, None),
        ),
        out_specs=P("term", None, "space"),
        check_vma=False,
    )
```

```python
import jax
import jax.numpy as jnp
from jax import lax
from jax.experimental import pallas as pl
from jax.experimental.pallas import tpu as pltpu
from jax.sharding import PartitionSpec as P

MESH_ID = pl.DeviceIdType.MESH


def greet_peers(count):
    me = lax.axis_index("term")
    row = lax.axis_index("space")
    barrier = pltpu.get_barrier_semaphore()

    def greet(step, carry):
        peer = lax.rem(me + step, count)
        pl.semaphore_signal(barrier, 1, device_id=(row, peer), device_id_type=MESH_ID)
        return carry

    lax.fori_loop(1, count, greet, 0)
    pl.semaphore_wait(barrier, count - 1)
    return me, row


CLASSES = 4


def gather_kernel(block_ref, out_ref, local_sem, send_near, recv_near, send_far, recv_far):
    count = out_ref.shape[0]
    chunk = count // CLASSES
    me = lax.axis_index("term")
    row = lax.axis_index("space")
    stride, lane = me // CLASSES, me % CLASSES
    barrier = pltpu.get_barrier_semaphore()

    def far_peer(step):
        return lax.rem(stride + step, chunk) * CLASSES + lane

    def near_peer(step):
        return stride * CLASSES + lax.rem(lane + step, CLASSES)

    def greet_far(step, carry):
        pl.semaphore_signal(barrier, 1, device_id=(row, far_peer(step)), device_id_type=MESH_ID)
        return carry

    def greet_near(step, carry):
        pl.semaphore_signal(barrier, 1, device_id=(row, near_peer(step)), device_id_type=MESH_ID)
        return carry

    lax.fori_loop(1, chunk, greet_far, 0)
    lax.fori_loop(1, CLASSES, greet_near, 0)
    pl.semaphore_wait(barrier, chunk + CLASSES - 2)

    mine = lane * chunk + stride
    local = pltpu.make_async_copy(block_ref, out_ref.at[mine], local_sem)
    local.start()

    def far_out(step):
        return pltpu.make_async_remote_copy(
            block_ref, out_ref.at[mine], send_far.at[step], recv_far.at[stride],
            device_id=(row, far_peer(step)), device_id_type=MESH_ID,
        )

    def far_in(step):
        source = lax.rem(stride + chunk - step, chunk)
        return pltpu.make_async_remote_copy(
            block_ref, out_ref.at[lane * chunk + source], send_far.at[step], recv_far.at[source],
            device_id=(row, source * CLASSES + lane), device_id_type=MESH_ID,
        )

    def far_start(step, carry):
        far_out(step).start()
        return carry

    def far_finish(step, carry):
        far_out(step).wait_send()
        far_in(step).wait_recv()
        return carry

    lax.fori_loop(1, chunk, far_start, 0)
    local.wait()
    lax.fori_loop(1, chunk, far_finish, 0)

    own = out_ref.at[pl.ds(lane * chunk, chunk)]

    def near_out(step):
        return pltpu.make_async_remote_copy(
            own, own, send_near.at[step], recv_near.at[lane],
            device_id=(row, near_peer(step)), device_id_type=MESH_ID,
        )

    def near_in(step):
        source = lax.rem(lane + CLASSES - step, CLASSES)
        theirs = out_ref.at[pl.ds(source * chunk, chunk)]
        return pltpu.make_async_remote_copy(
            theirs, theirs, send_near.at[step], recv_near.at[source],
            device_id=(row, stride * CLASSES + source), device_id_type=MESH_ID,
        )

    def near_start(step, carry):
        near_out(step).start()
        return carry

    def near_finish(step, carry):
        near_out(step).wait_send()
        near_in(step).wait_recv()
        return carry

    lax.fori_loop(1, CLASSES, near_start, 0)
    lax.fori_loop(1, CLASSES, near_finish, 0)


def gather_term(block):
    count = lax.axis_size("term")
    return pl.pallas_call(
        gather_kernel,
        out_shape=jax.ShapeDtypeStruct((count,) + block.shape, block.dtype),
        in_specs=[pl.BlockSpec(memory_space=pltpu.VMEM)],
        out_specs=pl.BlockSpec(memory_space=pltpu.VMEM),
        scratch_shapes=[
            pltpu.SemaphoreType.DMA(()),
            pltpu.SemaphoreType.DMA((CLASSES,)),
            pltpu.SemaphoreType.DMA((CLASSES,)),
            pltpu.SemaphoreType.DMA((count // CLASSES,)),
            pltpu.SemaphoreType.DMA((count // CLASSES,)),
        ],
        compiler_params=pltpu.CompilerParams(collective_id=0, has_side_effects=True),
    )(block)


def scatter_kernel(part_ref, own_ref, out_ref, near_slots, class_sum, far_slots,
                   send_near, recv_near, send_far, recv_far):
    classes, chunk = part_ref.shape[0], part_ref.shape[1]
    me = lax.axis_index("term")
    row = lax.axis_index("space")
    stride, lane = me // classes, me % classes
    barrier = pltpu.get_barrier_semaphore()

    def far_peer(step):
        return lax.rem(stride + step, chunk) * classes + lane

    def near_peer(step):
        return stride * classes + lax.rem(lane + step, classes)

    def greet_far(step, carry):
        pl.semaphore_signal(barrier, 1, device_id=(row, far_peer(step)), device_id_type=MESH_ID)
        return carry

    def greet_near(step, carry):
        pl.semaphore_signal(barrier, 1, device_id=(row, near_peer(step)), device_id_type=MESH_ID)
        return carry

    lax.fori_loop(1, chunk, greet_far, 0)
    lax.fori_loop(1, classes, greet_near, 0)
    pl.semaphore_wait(barrier, chunk + classes - 2)

    def near_out(step):
        target = lax.rem(lane + step, classes)
        return pltpu.make_async_remote_copy(
            part_ref.at[target], near_slots.at[lane], send_near.at[step], recv_near.at[lane],
            device_id=(row, near_peer(step)), device_id_type=MESH_ID,
        )

    def near_in(step):
        source = lax.rem(lane + classes - step, classes)
        return pltpu.make_async_remote_copy(
            part_ref.at[source], near_slots.at[source], send_near.at[step], recv_near.at[source],
            device_id=(row, stride * classes + source), device_id_type=MESH_ID,
        )

    def near_start(step, carry):
        near_out(step).start()
        return carry

    def near_finish(step, total):
        near_out(step).wait_send()
        near_in(step).wait_recv()
        source = lax.rem(lane + classes - step, classes)
        return total + near_slots[source].astype(jnp.float32)

    lax.fori_loop(1, classes, near_start, 0)
    class_sum[...] = lax.fori_loop(1, classes, near_finish, own_ref[lane])

    def far_out(step):
        target = lax.rem(stride + step, chunk)
        return pltpu.make_async_remote_copy(
            class_sum.at[target], far_slots.at[stride], send_far.at[step], recv_far.at[stride],
            device_id=(row, far_peer(step)), device_id_type=MESH_ID,
        )

    def far_in(step):
        source = lax.rem(stride + chunk - step, chunk)
        return pltpu.make_async_remote_copy(
            class_sum.at[source], far_slots.at[source], send_far.at[step], recv_far.at[source],
            device_id=(row, source * classes + lane), device_id_type=MESH_ID,
        )

    def far_start(step, carry):
        far_out(step).start()
        return carry

    def far_finish(step, total):
        far_out(step).wait_send()
        far_in(step).wait_recv()
        source = lax.rem(stride + chunk - step, chunk)
        return total + far_slots[source]

    lax.fori_loop(1, chunk, far_start, 0)
    out_ref[...] = lax.fori_loop(1, chunk, far_finish, class_sum[stride])


def scatter_term(parts):
    classes, chunk = parts.shape[0], parts.shape[1]
    sent = parts.astype(jnp.bfloat16)
    return pl.pallas_call(
        scatter_kernel,
        out_shape=jax.ShapeDtypeStruct(parts.shape[2:], parts.dtype),
        in_specs=[pl.BlockSpec(memory_space=pltpu.VMEM)] * 2,
        out_specs=pl.BlockSpec(memory_space=pltpu.VMEM),
        scratch_shapes=[
            pltpu.VMEM(sent.shape, sent.dtype),
            pltpu.VMEM(parts.shape[1:], parts.dtype),
            pltpu.VMEM(parts.shape[1:], parts.dtype),
            pltpu.SemaphoreType.DMA((classes,)),
            pltpu.SemaphoreType.DMA((classes,)),
            pltpu.SemaphoreType.DMA((chunk,)),
            pltpu.SemaphoreType.DMA((chunk,)),
        ],
        compiler_params=pltpu.CompilerParams(collective_id=1, has_side_effects=True),
    )(sent, parts)


def image_kernel(offs_ref, panel_ref, stiff_ref, triple_ref, out_ref):
    term = pl.program_id(0)
    block = pl.program_id(1)
    block_rows = pl.num_programs(1)
    band = stiff_ref.shape[2]
    width = stiff_ref.shape[-1]
    loads, rows, span = panel_ref.shape
    rim = (span // width - block_rows) // 2

    @pl.when((term == 0) & (block == 0))
    def _():
        out_ref[...] = jnp.zeros_like(out_ref)

    for load in range(loads):
        total = jnp.zeros((rows, width), jnp.float32)
        for slot in range(band):
            place = block + rim + offs_ref[(term * block_rows + block) * band + slot]
            start = pl.multiple_of(place * width, width)
            total += lax.dot_general(
                panel_ref[load, :, pl.ds(start, width)], stiff_ref[0, 0, slot],
                (((1,), (1,)), ((), ())), preferred_element_type=jnp.float32,
            )
        image = total.astype(jnp.bfloat16)
        column = pl.multiple_of((load * block_rows + block) * width, width)
        out_ref[:, pl.ds(column, width)] += jnp.dot(
            triple_ref[0], image, preferred_element_type=jnp.float32
        )


def image_contract(offsets, panel, stiff_blocks, dense):
    term_count, block_rows, band, width, _ = stiff_blocks.shape
    loads, rows, span = panel.shape
    return pl.pallas_call(
        image_kernel,
        out_shape=jax.ShapeDtypeStruct((rows, loads * block_rows * width), jnp.float32),
        grid_spec=pltpu.PrefetchScalarGridSpec(
            num_scalar_prefetch=1,
            grid=(term_count, block_rows),
            in_specs=[
                pl.BlockSpec((loads, rows, span), lambda k, b, offs: (0, 0, 0)),
                pl.BlockSpec((1, 1, band, width, width), lambda k, b, offs: (k, b, 0, 0, 0)),
                pl.BlockSpec((1, rows, rows), lambda k, b, offs: (k, 0, 0)),
            ],
            out_specs=pl.BlockSpec((rows, loads * block_rows * width), lambda k, b, offs: (0, 0)),
        ),
    )(offsets.reshape(-1), panel, stiff_blocks, dense)


def with_halo(block, sides, width):
    for axis, dim in sides:
        count = lax.axis_size(axis)
        forward = [(i, i + 1) for i in range(count - 1)]
        backward = [(target, source) for source, target in forward]
        low = lax.ppermute(
            lax.slice_in_dim(block, block.shape[dim] - width, None, axis=dim), axis, forward
        )
        high = lax.ppermute(lax.slice_in_dim(block, 0, width, axis=dim), axis, backward)
        block = jnp.concatenate([low, block, high], axis=dim)
    return block


def per_device(chaos_field, stiff_blocks, stiff_offsets, triple_blocks, triple_pattern):
    local_rows = chaos_field.shape[0]
    load_count = chaos_field.shape[1]
    cell_count = chaos_field.shape[2]
    term_count = stiff_blocks.shape[0]
    block_width = stiff_blocks.shape[3]
    block_rows = cell_count // block_width
    groups = lax.axis_size("term")
    total_rows = local_rows * groups
    rim_cells = 2 * block_width
    gathered = gather_term(chaos_field.reshape(local_rows * load_count, cell_count))
    panel = gathered.reshape(groups, local_rows, load_count, cell_count).transpose(2, 0, 1, 3)
    panel = panel.reshape(load_count, total_rows, cell_count)
    extended = with_halo(panel, (("space", 2),), rim_cells)
    block_size = triple_blocks.shape[2]
    levels = jnp.arange(total_rows // block_size, dtype=jnp.int32)
    row_hot = (triple_pattern[:, :, 0:1] == levels).astype(jnp.float32)
    col_hot = (triple_pattern[:, :, 1:2] == levels).astype(jnp.float32)
    dense = jnp.einsum("kna,knb,knxy->kaxby", row_hot, col_hot, triple_blocks.astype(jnp.float32))
    order = (groups // CLASSES, CLASSES, local_rows)
    dense = dense.reshape((term_count,) + order + order).transpose(0, 2, 1, 3, 5, 4, 6)
    dense = dense.reshape(term_count, total_rows, total_rows)
    dense = dense.astype(jnp.bfloat16)
    partial = image_contract(stiff_offsets, extended, stiff_blocks, dense)
    parts = partial.reshape(CLASSES, groups // CLASSES, local_rows, load_count * cell_count)
    summed = scatter_term(parts)
    return summed.reshape(local_rows, load_count, cell_count)


def solution(mesh):
    return jax.shard_map(
        per_device,
        mesh=mesh,
        in_specs=(
            P("term", None, "space"),
            P("term", "space", None, None, None),
            P("term", "space", None),
            P("term", None, None, None),
            P("term", None, None),
        ),
        out_specs=P("term", None, "space"),
        check_vma=False,
    )
```

```python
import jax
import jax.numpy as jnp
from jax import lax
from jax.experimental import pallas as pl
from jax.experimental.pallas import tpu as pltpu
from jax.sharding import PartitionSpec as P

MESH_ID = pl.DeviceIdType.MESH


def greet_peers(count):
    me = lax.axis_index("term")
    row = lax.axis_index("space")
    barrier = pltpu.get_barrier_semaphore()

    def greet(step, carry):
        peer = lax.rem(me + step, count)
        pl.semaphore_signal(barrier, 1, device_id=(row, peer), device_id_type=MESH_ID)
        return carry

    lax.fori_loop(1, count, greet, 0)
    pl.semaphore_wait(barrier, count - 1)
    return me, row


CLASSES = 4


def gather_kernel(block_ref, out_ref, local_sem, send_near, recv_near, send_far, recv_far):
    count = out_ref.shape[0]
    chunk = count // CLASSES
    me = lax.axis_index("term")
    row = lax.axis_index("space")
    stride, lane = me // CLASSES, me % CLASSES
    barrier = pltpu.get_barrier_semaphore()

    def far_peer(step):
        return lax.rem(stride + step, chunk) * CLASSES + lane

    def near_peer(step):
        return stride * CLASSES + lax.rem(lane + step, CLASSES)

    def greet_far(step, carry):
        pl.semaphore_signal(barrier, 1, device_id=(row, far_peer(step)), device_id_type=MESH_ID)
        return carry

    def greet_near(step, carry):
        pl.semaphore_signal(barrier, 1, device_id=(row, near_peer(step)), device_id_type=MESH_ID)
        return carry

    lax.fori_loop(1, chunk, greet_far, 0)
    lax.fori_loop(1, CLASSES, greet_near, 0)
    pl.semaphore_wait(barrier, chunk + CLASSES - 2)

    mine = lane * chunk + stride
    local = pltpu.make_async_copy(block_ref, out_ref.at[mine], local_sem)
    local.start()

    def far_out(step):
        return pltpu.make_async_remote_copy(
            block_ref, out_ref.at[mine], send_far.at[step], recv_far.at[stride],
            device_id=(row, far_peer(step)), device_id_type=MESH_ID,
        )

    def far_in(step):
        source = lax.rem(stride + chunk - step, chunk)
        return pltpu.make_async_remote_copy(
            block_ref, out_ref.at[lane * chunk + source], send_far.at[step], recv_far.at[source],
            device_id=(row, source * CLASSES + lane), device_id_type=MESH_ID,
        )

    def far_start(step, carry):
        far_out(step).start()
        return carry

    def far_finish(step, carry):
        far_out(step).wait_send()
        far_in(step).wait_recv()
        return carry

    lax.fori_loop(1, chunk, far_start, 0)
    local.wait()
    lax.fori_loop(1, chunk, far_finish, 0)

    own = out_ref.at[pl.ds(lane * chunk, chunk)]

    def near_out(step):
        return pltpu.make_async_remote_copy(
            own, own, send_near.at[step], recv_near.at[lane],
            device_id=(row, near_peer(step)), device_id_type=MESH_ID,
        )

    def near_in(step):
        source = lax.rem(lane + CLASSES - step, CLASSES)
        theirs = out_ref.at[pl.ds(source * chunk, chunk)]
        return pltpu.make_async_remote_copy(
            theirs, theirs, send_near.at[step], recv_near.at[source],
            device_id=(row, stride * CLASSES + source), device_id_type=MESH_ID,
        )

    def near_start(step, carry):
        near_out(step).start()
        return carry

    def near_finish(step, carry):
        near_out(step).wait_send()
        near_in(step).wait_recv()
        return carry

    lax.fori_loop(1, CLASSES, near_start, 0)
    lax.fori_loop(1, CLASSES, near_finish, 0)


def gather_term(block):
    count = lax.axis_size("term")
    return pl.pallas_call(
        gather_kernel,
        out_shape=jax.ShapeDtypeStruct((count,) + block.shape, block.dtype),
        in_specs=[pl.BlockSpec(memory_space=pltpu.VMEM)],
        out_specs=pl.BlockSpec(memory_space=pltpu.VMEM),
        scratch_shapes=[
            pltpu.SemaphoreType.DMA(()),
            pltpu.SemaphoreType.DMA((CLASSES,)),
            pltpu.SemaphoreType.DMA((CLASSES,)),
            pltpu.SemaphoreType.DMA((count // CLASSES,)),
            pltpu.SemaphoreType.DMA((count // CLASSES,)),
        ],
        compiler_params=pltpu.CompilerParams(collective_id=0, has_side_effects=True),
    )(block)


def scatter_kernel(part_ref, own_ref, out_ref, near_slots, class_sum, far_slots,
                   send_near, recv_near, send_far, recv_far):
    chunk, classes = part_ref.shape[0], part_ref.shape[1]
    me = lax.axis_index("term")
    row = lax.axis_index("space")
    stride, lane = me // classes, me % classes
    barrier = pltpu.get_barrier_semaphore()

    def far_peer(step):
        return lax.rem(stride + step, chunk) * classes + lane

    def near_peer(step):
        return stride * classes + lax.rem(lane + step, classes)

    def greet_far(step, carry):
        pl.semaphore_signal(barrier, 1, device_id=(row, far_peer(step)), device_id_type=MESH_ID)
        return carry

    def greet_near(step, carry):
        pl.semaphore_signal(barrier, 1, device_id=(row, near_peer(step)), device_id_type=MESH_ID)
        return carry

    lax.fori_loop(1, chunk, greet_far, 0)
    lax.fori_loop(1, classes, greet_near, 0)
    pl.semaphore_wait(barrier, chunk + classes - 2)

    def near_out(step):
        target = lax.rem(lane + step, classes)
        return pltpu.make_async_remote_copy(
            part_ref.at[:, target], near_slots.at[lane], send_near.at[step], recv_near.at[lane],
            device_id=(row, near_peer(step)), device_id_type=MESH_ID,
        )

    def near_in(step):
        source = lax.rem(lane + classes - step, classes)
        return pltpu.make_async_remote_copy(
            part_ref.at[:, source], near_slots.at[source], send_near.at[step], recv_near.at[source],
            device_id=(row, stride * classes + source), device_id_type=MESH_ID,
        )

    def near_start(step, carry):
        near_out(step).start()
        return carry

    def near_finish(step, total):
        near_out(step).wait_send()
        near_in(step).wait_recv()
        source = lax.rem(lane + classes - step, classes)
        return total + near_slots[source].astype(jnp.float32)

    lax.fori_loop(1, classes, near_start, 0)
    class_sum[...] = lax.fori_loop(1, classes, near_finish, own_ref[:, lane])

    def far_out(step):
        target = lax.rem(stride + step, chunk)
        return pltpu.make_async_remote_copy(
            class_sum.at[target], far_slots.at[stride], send_far.at[step], recv_far.at[stride],
            device_id=(row, far_peer(step)), device_id_type=MESH_ID,
        )

    def far_in(step):
        source = lax.rem(stride + chunk - step, chunk)
        return pltpu.make_async_remote_copy(
            class_sum.at[source], far_slots.at[source], send_far.at[step], recv_far.at[source],
            device_id=(row, source * classes + lane), device_id_type=MESH_ID,
        )

    def far_start(step, carry):
        far_out(step).start()
        return carry

    def far_finish(step, total):
        far_out(step).wait_send()
        far_in(step).wait_recv()
        source = lax.rem(stride + chunk - step, chunk)
        return total + far_slots[source]

    lax.fori_loop(1, chunk, far_start, 0)
    out_ref[...] = lax.fori_loop(1, chunk, far_finish, class_sum[stride])


def scatter_term(parts):
    chunk, classes = parts.shape[0], parts.shape[1]
    sent = parts.astype(jnp.bfloat16)
    return pl.pallas_call(
        scatter_kernel,
        out_shape=jax.ShapeDtypeStruct(parts.shape[2:], parts.dtype),
        in_specs=[pl.BlockSpec(memory_space=pltpu.VMEM)] * 2,
        out_specs=pl.BlockSpec(memory_space=pltpu.VMEM),
        scratch_shapes=[
            pltpu.VMEM((classes, chunk) + parts.shape[2:], sent.dtype),
            pltpu.VMEM((chunk,) + parts.shape[2:], parts.dtype),
            pltpu.VMEM((chunk,) + parts.shape[2:], parts.dtype),
            pltpu.SemaphoreType.DMA((classes,)),
            pltpu.SemaphoreType.DMA((classes,)),
            pltpu.SemaphoreType.DMA((chunk,)),
            pltpu.SemaphoreType.DMA((chunk,)),
        ],
        compiler_params=pltpu.CompilerParams(collective_id=1, has_side_effects=True),
    )(sent, parts)


def image_kernel(offs_ref, panel_ref, stiff_ref, triple_ref, out_ref):
    term = pl.program_id(0)
    block = pl.program_id(1)
    block_rows = pl.num_programs(1)
    band = stiff_ref.shape[2]
    width = stiff_ref.shape[-1]
    loads, rows, span = panel_ref.shape
    rim = (span // width - block_rows) // 2

    @pl.when((term == 0) & (block == 0))
    def _():
        out_ref[...] = jnp.zeros_like(out_ref)

    for load in range(loads):
        total = jnp.zeros((rows, width), jnp.float32)
        for slot in range(band):
            place = block + rim + offs_ref[(term * block_rows + block) * band + slot]
            start = pl.multiple_of(place * width, width)
            total += lax.dot_general(
                panel_ref[load, :, pl.ds(start, width)], stiff_ref[0, 0, slot],
                (((1,), (1,)), ((), ())), preferred_element_type=jnp.float32,
            )
        image = total.astype(jnp.bfloat16)
        column = pl.multiple_of((load * block_rows + block) * width, width)
        out_ref[:, pl.ds(column, width)] += jnp.dot(
            triple_ref[0], image, preferred_element_type=jnp.float32
        )


def image_contract(offsets, panel, stiff_blocks, dense):
    term_count, block_rows, band, width, _ = stiff_blocks.shape
    loads, rows, span = panel.shape
    return pl.pallas_call(
        image_kernel,
        out_shape=jax.ShapeDtypeStruct((rows, loads * block_rows * width), jnp.float32),
        grid_spec=pltpu.PrefetchScalarGridSpec(
            num_scalar_prefetch=1,
            grid=(term_count, block_rows),
            in_specs=[
                pl.BlockSpec((loads, rows, span), lambda k, b, offs: (0, 0, 0)),
                pl.BlockSpec((1, 1, band, width, width), lambda k, b, offs: (k, b, 0, 0, 0)),
                pl.BlockSpec((1, rows, rows), lambda k, b, offs: (k, 0, 0)),
            ],
            out_specs=pl.BlockSpec((rows, loads * block_rows * width), lambda k, b, offs: (0, 0)),
        ),
    )(offsets.reshape(-1), panel, stiff_blocks, dense)


def with_halo(block, sides, width):
    for axis, dim in sides:
        count = lax.axis_size(axis)
        forward = [(i, i + 1) for i in range(count - 1)]
        backward = [(target, source) for source, target in forward]
        low = lax.ppermute(
            lax.slice_in_dim(block, block.shape[dim] - width, None, axis=dim), axis, forward
        )
        high = lax.ppermute(lax.slice_in_dim(block, 0, width, axis=dim), axis, backward)
        block = jnp.concatenate([low, block, high], axis=dim)
    return block


def per_device(chaos_field, stiff_blocks, stiff_offsets, triple_blocks, triple_pattern):
    local_rows = chaos_field.shape[0]
    load_count = chaos_field.shape[1]
    cell_count = chaos_field.shape[2]
    term_count = stiff_blocks.shape[0]
    block_width = stiff_blocks.shape[3]
    block_rows = cell_count // block_width
    groups = lax.axis_size("term")
    total_rows = local_rows * groups
    rim_cells = 2 * block_width
    gathered = gather_term(chaos_field.reshape(local_rows * load_count, cell_count))
    panel = gathered.reshape(groups, local_rows, load_count, cell_count).transpose(2, 0, 1, 3)
    panel = panel.reshape(load_count, total_rows, cell_count)
    extended = with_halo(panel, (("space", 2),), rim_cells)
    block_size = triple_blocks.shape[2]
    levels = jnp.arange(total_rows // block_size, dtype=jnp.int32)
    row_hot = (triple_pattern[:, :, 0:1] == levels).astype(jnp.float32)
    col_hot = (triple_pattern[:, :, 1:2] == levels).astype(jnp.float32)
    dense = jnp.einsum("kna,knb,knxy->kaxby", row_hot, col_hot, triple_blocks.astype(jnp.float32))
    dense = dense.reshape(term_count, total_rows, groups // CLASSES, CLASSES, local_rows)
    dense = dense.transpose(0, 1, 3, 2, 4).reshape(term_count, total_rows, total_rows)
    dense = dense.astype(jnp.bfloat16)
    partial = image_contract(stiff_offsets, extended, stiff_blocks, dense)
    parts = partial.reshape(groups // CLASSES, CLASSES, local_rows, load_count * cell_count)
    summed = scatter_term(parts)
    return summed.reshape(local_rows, load_count, cell_count)


def solution(mesh):
    return jax.shard_map(
        per_device,
        mesh=mesh,
        in_specs=(
            P("term", None, "space"),
            P("term", "space", None, None, None),
            P("term", "space", None),
            P("term", None, None, None),
            P("term", None, None),
        ),
        out_specs=P("term", None, "space"),
        check_vma=False,
    )
```

```python
import jax
import jax.numpy as jnp
from jax import lax
from jax.experimental import pallas as pl
from jax.experimental.pallas import tpu as pltpu
from jax.sharding import PartitionSpec as P

MESH_ID = pl.DeviceIdType.MESH


CLASSES = 4


def gather_kernel(block_ref, out_ref, local_sem, send_near, recv_near, send_far, recv_far):
    count = out_ref.shape[0]
    chunk = count // CLASSES
    me = lax.axis_index("term")
    row = lax.axis_index("space")
    stride, lane = me // CLASSES, me % CLASSES
    barrier = pltpu.get_barrier_semaphore()

    def far_peer(step):
        return lax.rem(stride + step, chunk) * CLASSES + lane

    def near_peer(step):
        return stride * CLASSES + lax.rem(lane + step, CLASSES)

    def greet_far(step, carry):
        pl.semaphore_signal(barrier, 1, device_id=(row, far_peer(step)), device_id_type=MESH_ID)
        return carry

    def greet_near(step, carry):
        pl.semaphore_signal(barrier, 1, device_id=(row, near_peer(step)), device_id_type=MESH_ID)
        return carry

    lax.fori_loop(1, chunk, greet_far, 0)
    lax.fori_loop(1, CLASSES, greet_near, 0)
    pl.semaphore_wait(barrier, chunk + CLASSES - 2)

    mine = lane * chunk + stride
    local = pltpu.make_async_copy(block_ref, out_ref.at[mine], local_sem)
    local.start()

    def far_out(step):
        return pltpu.make_async_remote_copy(
            block_ref, out_ref.at[mine], send_far.at[step], recv_far.at[stride],
            device_id=(row, far_peer(step)), device_id_type=MESH_ID,
        )

    def far_in(step):
        source = lax.rem(stride + chunk - step, chunk)
        return pltpu.make_async_remote_copy(
            block_ref, out_ref.at[lane * chunk + source], send_far.at[step], recv_far.at[source],
            device_id=(row, source * CLASSES + lane), device_id_type=MESH_ID,
        )

    def far_start(step, carry):
        far_out(step).start()
        return carry

    def far_finish(step, carry):
        far_out(step).wait_send()
        far_in(step).wait_recv()
        return carry

    lax.fori_loop(1, chunk, far_start, 0)
    local.wait()
    lax.fori_loop(1, chunk, far_finish, 0)

    own = out_ref.at[pl.ds(lane * chunk, chunk)]

    def near_out(step):
        return pltpu.make_async_remote_copy(
            own, own, send_near.at[step], recv_near.at[lane],
            device_id=(row, near_peer(step)), device_id_type=MESH_ID,
        )

    def near_in(step):
        source = lax.rem(lane + CLASSES - step, CLASSES)
        theirs = out_ref.at[pl.ds(source * chunk, chunk)]
        return pltpu.make_async_remote_copy(
            theirs, theirs, send_near.at[step], recv_near.at[source],
            device_id=(row, stride * CLASSES + source), device_id_type=MESH_ID,
        )

    def near_start(step, carry):
        near_out(step).start()
        return carry

    def near_finish(step, carry):
        near_out(step).wait_send()
        near_in(step).wait_recv()
        return carry

    lax.fori_loop(1, CLASSES, near_start, 0)
    lax.fori_loop(1, CLASSES, near_finish, 0)


def gather_term(block):
    count = lax.axis_size("term")
    return pl.pallas_call(
        gather_kernel,
        out_shape=jax.ShapeDtypeStruct((count,) + block.shape, block.dtype),
        in_specs=[pl.BlockSpec(memory_space=pltpu.VMEM)],
        out_specs=pl.BlockSpec(memory_space=pltpu.VMEM),
        scratch_shapes=[
            pltpu.SemaphoreType.DMA(()),
            pltpu.SemaphoreType.DMA((CLASSES,)),
            pltpu.SemaphoreType.DMA((CLASSES,)),
            pltpu.SemaphoreType.DMA((count // CLASSES,)),
            pltpu.SemaphoreType.DMA((count // CLASSES,)),
        ],
        compiler_params=pltpu.CompilerParams(collective_id=0, has_side_effects=True),
    )(block)


def scatter_peers(chunk, classes):
    me = lax.axis_index("term")
    row = lax.axis_index("space")
    stride, lane = me // classes, me % classes

    def far_peer(step):
        return lax.rem(stride + step, chunk) * classes + lane

    def near_peer(step):
        return stride * classes + lax.rem(lane + step, classes)

    return row, stride, lane, far_peer, near_peer


def scatter_greet(chunk, classes):
    row, stride, lane, far_peer, near_peer = scatter_peers(chunk, classes)
    barrier = pltpu.get_barrier_semaphore()

    def greet_far(step, carry):
        pl.semaphore_signal(barrier, 1, device_id=(row, far_peer(step)), device_id_type=MESH_ID)
        return carry

    def greet_near(step, carry):
        pl.semaphore_signal(barrier, 1, device_id=(row, near_peer(step)), device_id_type=MESH_ID)
        return carry

    lax.fori_loop(1, chunk, greet_far, 0)
    lax.fori_loop(1, classes, greet_near, 0)


def scatter_stages(part_ref, own_ref, out_ref, near_slots, class_sum, far_slots,
                   send_near, recv_near, send_far, recv_far):
    chunk, classes = part_ref.shape[0], part_ref.shape[1]
    row, stride, lane, far_peer, near_peer = scatter_peers(chunk, classes)
    pl.semaphore_wait(pltpu.get_barrier_semaphore(), chunk + classes - 2)

    def near_out(step):
        target = lax.rem(lane + step, classes)
        return pltpu.make_async_remote_copy(
            part_ref.at[:, target], near_slots.at[lane], send_near.at[step], recv_near.at[lane],
            device_id=(row, near_peer(step)), device_id_type=MESH_ID,
        )

    def near_in(step):
        source = lax.rem(lane + classes - step, classes)
        return pltpu.make_async_remote_copy(
            part_ref.at[:, source], near_slots.at[source], send_near.at[step], recv_near.at[source],
            device_id=(row, stride * classes + source), device_id_type=MESH_ID,
        )

    def near_start(step, carry):
        near_out(step).start()
        return carry

    def near_finish(step, total):
        near_out(step).wait_send()
        near_in(step).wait_recv()
        source = lax.rem(lane + classes - step, classes)
        return total + near_slots[source].astype(jnp.float32)

    lax.fori_loop(1, classes, near_start, 0)
    class_sum[...] = lax.fori_loop(1, classes, near_finish, own_ref[:, lane])

    def far_out(step):
        target = lax.rem(stride + step, chunk)
        return pltpu.make_async_remote_copy(
            class_sum.at[target], far_slots.at[stride], send_far.at[step], recv_far.at[stride],
            device_id=(row, far_peer(step)), device_id_type=MESH_ID,
        )

    def far_in(step):
        source = lax.rem(stride + chunk - step, chunk)
        return pltpu.make_async_remote_copy(
            class_sum.at[source], far_slots.at[source], send_far.at[step], recv_far.at[source],
            device_id=(row, source * classes + lane), device_id_type=MESH_ID,
        )

    def far_start(step, carry):
        far_out(step).start()
        return carry

    def far_finish(step, total):
        far_out(step).wait_send()
        far_in(step).wait_recv()
        source = lax.rem(stride + chunk - step, chunk)
        return total + far_slots[source]

    lax.fori_loop(1, chunk, far_start, 0)
    out_ref[...] = lax.fori_loop(1, chunk, far_finish, class_sum[stride])


def image_kernel(offs_ref, panel_ref, stiff_ref, triple_ref, out_ref, total_ref, sent_ref,
                 near_slots, class_sum, far_slots, send_near, recv_near, send_far, recv_far):
    term = pl.program_id(0)
    block = pl.program_id(1)
    block_rows = pl.num_programs(1)
    band = stiff_ref.shape[2]
    width = stiff_ref.shape[-1]
    chunk, classes, local_rows, columns = total_ref.shape
    rows = panel_ref.shape[1]
    loads = columns // (block_rows * width)
    rim = (panel_ref.shape[0] // loads - block_rows) // 2

    @pl.when((term == 0) & (block == 0))
    def _():
        scatter_greet(chunk, classes)
        total_ref[...] = jnp.zeros_like(total_ref)

    for load in range(loads):
        total = jnp.zeros((rows, width), jnp.float32)
        for slot in range(band):
            place = block + rim + offs_ref[(term * block_rows + block) * band + slot]
            total += lax.dot_general(
                panel_ref[place * loads + load], stiff_ref[0, 0, slot],
                (((1,), (1,)), ((), ())), preferred_element_type=jnp.float32,
            )
        image = total.astype(jnp.bfloat16)
        column = pl.multiple_of((load * block_rows + block) * width, width)
        product = jnp.dot(triple_ref[0], image, preferred_element_type=jnp.float32)
        total_ref[:, :, :, pl.ds(column, width)] += product.reshape(chunk, classes, local_rows, width)

    @pl.when((term == pl.num_programs(0) - 1) & (block == block_rows - 1))
    def _():
        sent_ref[...] = total_ref[...].astype(sent_ref.dtype)
        scatter_stages(sent_ref, total_ref, out_ref, near_slots, class_sum, far_slots,
                       send_near, recv_near, send_far, recv_far)


def image_scatter(offsets, panel, stiff_blocks, dense, local_rows):
    term_count, block_rows, band, width, _ = stiff_blocks.shape
    places, rows, _ = panel.shape
    loads = places // (block_rows + 4)
    columns = loads * block_rows * width
    classes = CLASSES
    chunk = rows // (classes * local_rows)
    shape = (chunk, classes, local_rows, columns)
    return pl.pallas_call(
        image_kernel,
        out_shape=jax.ShapeDtypeStruct((local_rows, columns), jnp.float32),
        grid_spec=pltpu.PrefetchScalarGridSpec(
            num_scalar_prefetch=1,
            grid=(term_count, block_rows),
            in_specs=[
                pl.BlockSpec((places, rows, width), lambda k, b, offs: (0, 0, 0)),
                pl.BlockSpec((1, 1, band, width, width), lambda k, b, offs: (k, b, 0, 0, 0)),
                pl.BlockSpec((1, rows, rows), lambda k, b, offs: (k, 0, 0)),
            ],
            out_specs=pl.BlockSpec((local_rows, columns), lambda k, b, offs: (0, 0)),
            scratch_shapes=[
                pltpu.VMEM(shape, jnp.float32),
                pltpu.VMEM(shape, jnp.bfloat16),
                pltpu.VMEM((classes, chunk, local_rows, columns), jnp.bfloat16),
                pltpu.VMEM((chunk, local_rows, columns), jnp.float32),
                pltpu.VMEM((chunk, local_rows, columns), jnp.float32),
                pltpu.SemaphoreType.DMA((classes,)),
                pltpu.SemaphoreType.DMA((classes,)),
                pltpu.SemaphoreType.DMA((chunk,)),
                pltpu.SemaphoreType.DMA((chunk,)),
            ],
        ),
        compiler_params=pltpu.CompilerParams(collective_id=1, has_side_effects=True),
    )(offsets.reshape(-1), panel, stiff_blocks, dense)


def with_halo(block, sides, width):
    for axis, dim in sides:
        count = lax.axis_size(axis)
        forward = [(i, i + 1) for i in range(count - 1)]
        backward = [(target, source) for source, target in forward]
        low = lax.ppermute(
            lax.slice_in_dim(block, block.shape[dim] - width, None, axis=dim), axis, forward
        )
        high = lax.ppermute(lax.slice_in_dim(block, 0, width, axis=dim), axis, backward)
        block = jnp.concatenate([low, block, high], axis=dim)
    return block


def per_device(chaos_field, stiff_blocks, stiff_offsets, triple_blocks, triple_pattern):
    local_rows = chaos_field.shape[0]
    load_count = chaos_field.shape[1]
    cell_count = chaos_field.shape[2]
    term_count = stiff_blocks.shape[0]
    block_width = stiff_blocks.shape[3]
    block_rows = cell_count // block_width
    groups = lax.axis_size("term")
    total_rows = local_rows * groups
    rim_cells = 2 * block_width
    gathered = gather_term(chaos_field.reshape(local_rows * load_count, cell_count))
    panel = gathered.reshape(groups, local_rows, load_count, block_rows, block_width)
    panel = panel.transpose(3, 2, 0, 1, 4).reshape(block_rows, load_count, total_rows, block_width)
    extended = with_halo(panel, (("space", 0),), rim_cells // block_width)
    extended = extended.reshape(-1, total_rows, block_width)
    block_size = triple_blocks.shape[2]
    levels = jnp.arange(total_rows // block_size, dtype=jnp.int32)
    row_hot = (triple_pattern[:, :, 0:1] == levels).astype(jnp.float32)
    col_hot = (triple_pattern[:, :, 1:2] == levels).astype(jnp.float32)
    dense = jnp.einsum("kna,knb,knxy->kaxby", row_hot, col_hot, triple_blocks.astype(jnp.float32))
    dense = dense.reshape(term_count, total_rows, groups // CLASSES, CLASSES, local_rows)
    dense = dense.transpose(0, 1, 3, 2, 4).reshape(term_count, total_rows, total_rows)
    dense = dense.astype(jnp.bfloat16)
    summed = image_scatter(stiff_offsets, extended, stiff_blocks, dense, local_rows)
    return summed.reshape(local_rows, load_count, cell_count)


def solution(mesh):
    return jax.shard_map(
        per_device,
        mesh=mesh,
        in_specs=(
            P("term", None, "space"),
            P("term", "space", None, None, None),
            P("term", "space", None),
            P("term", None, None, None),
            P("term", None, None),
        ),
        out_specs=P("term", None, "space"),
        check_vma=False,
    )
```

```python
import jax
import jax.numpy as jnp
from jax import lax
from jax.experimental import pallas as pl
from jax.experimental.pallas import tpu as pltpu
from jax.sharding import PartitionSpec as P

MESH_ID = pl.DeviceIdType.MESH


CLASSES = 4


def gather_kernel(block_ref, out_ref, local_sem, send_near, recv_near, send_far, recv_far):
    count = out_ref.shape[0]
    chunk = count // CLASSES
    me = lax.axis_index("term")
    row = lax.axis_index("space")
    stride, lane = me // CLASSES, me % CLASSES
    barrier = pltpu.get_barrier_semaphore()

    def far_peer(step):
        return lax.rem(stride + step, chunk) * CLASSES + lane

    def near_peer(step):
        return stride * CLASSES + lax.rem(lane + step, CLASSES)

    def greet_far(step, carry):
        pl.semaphore_signal(barrier, 1, device_id=(row, far_peer(step)), device_id_type=MESH_ID)
        return carry

    def greet_near(step, carry):
        pl.semaphore_signal(barrier, 1, device_id=(row, near_peer(step)), device_id_type=MESH_ID)
        return carry

    lax.fori_loop(1, chunk, greet_far, 0)
    lax.fori_loop(1, CLASSES, greet_near, 0)
    pl.semaphore_wait(barrier, chunk + CLASSES - 2)

    mine = lane * chunk + stride
    local = pltpu.make_async_copy(block_ref, out_ref.at[mine], local_sem)
    local.start()

    def far_out(step):
        return pltpu.make_async_remote_copy(
            block_ref, out_ref.at[mine], send_far.at[step], recv_far.at[stride],
            device_id=(row, far_peer(step)), device_id_type=MESH_ID,
        )

    def far_in(step):
        source = lax.rem(stride + chunk - step, chunk)
        return pltpu.make_async_remote_copy(
            block_ref, out_ref.at[lane * chunk + source], send_far.at[step], recv_far.at[source],
            device_id=(row, source * CLASSES + lane), device_id_type=MESH_ID,
        )

    def far_start(step, carry):
        far_out(step).start()
        return carry

    def far_finish(step, carry):
        far_out(step).wait_send()
        far_in(step).wait_recv()
        return carry

    lax.fori_loop(1, chunk, far_start, 0)
    local.wait()
    lax.fori_loop(1, chunk, far_finish, 0)

    own = out_ref.at[pl.ds(lane * chunk, chunk)]

    def near_out(step):
        return pltpu.make_async_remote_copy(
            own, own, send_near.at[step], recv_near.at[lane],
            device_id=(row, near_peer(step)), device_id_type=MESH_ID,
        )

    def near_in(step):
        source = lax.rem(lane + CLASSES - step, CLASSES)
        theirs = out_ref.at[pl.ds(source * chunk, chunk)]
        return pltpu.make_async_remote_copy(
            theirs, theirs, send_near.at[step], recv_near.at[source],
            device_id=(row, stride * CLASSES + source), device_id_type=MESH_ID,
        )

    def near_start(step, carry):
        near_out(step).start()
        return carry

    def near_finish(step, carry):
        near_out(step).wait_send()
        near_in(step).wait_recv()
        return carry

    lax.fori_loop(1, CLASSES, near_start, 0)
    lax.fori_loop(1, CLASSES, near_finish, 0)


def gather_term(block):
    count = lax.axis_size("term")
    return pl.pallas_call(
        gather_kernel,
        out_shape=jax.ShapeDtypeStruct((count,) + block.shape, block.dtype),
        in_specs=[pl.BlockSpec(memory_space=pltpu.VMEM)],
        out_specs=pl.BlockSpec(memory_space=pltpu.VMEM),
        scratch_shapes=[
            pltpu.SemaphoreType.DMA(()),
            pltpu.SemaphoreType.DMA((CLASSES,)),
            pltpu.SemaphoreType.DMA((CLASSES,)),
            pltpu.SemaphoreType.DMA((count // CLASSES,)),
            pltpu.SemaphoreType.DMA((count // CLASSES,)),
        ],
        compiler_params=pltpu.CompilerParams(collective_id=0, has_side_effects=True),
    )(block)


def scatter_peers(chunk, classes):
    me = lax.axis_index("term")
    row = lax.axis_index("space")
    stride, lane = me // classes, me % classes

    def far_peer(step):
        return lax.rem(stride + step, chunk) * classes + lane

    def near_peer(step):
        return stride * classes + lax.rem(lane + step, classes)

    return row, stride, lane, far_peer, near_peer


def scatter_greet(chunk, classes):
    row, stride, lane, far_peer, near_peer = scatter_peers(chunk, classes)
    barrier = pltpu.get_barrier_semaphore()

    def greet_far(step, carry):
        pl.semaphore_signal(barrier, 1, device_id=(row, far_peer(step)), device_id_type=MESH_ID)
        return carry

    def greet_near(step, carry):
        pl.semaphore_signal(barrier, 1, device_id=(row, near_peer(step)), device_id_type=MESH_ID)
        return carry

    lax.fori_loop(1, chunk, greet_far, 0)
    lax.fori_loop(1, classes, greet_near, 0)


def scatter_stages(part_ref, own_ref, out_ref, near_slots, class_sum, far_slots,
                   send_near, recv_near, send_far, recv_far):
    chunk, classes = part_ref.shape[0], part_ref.shape[1]
    row, stride, lane, far_peer, near_peer = scatter_peers(chunk, classes)
    pl.semaphore_wait(pltpu.get_barrier_semaphore(), chunk + classes - 2)

    def near_out(step):
        target = lax.rem(lane + step, classes)
        return pltpu.make_async_remote_copy(
            part_ref.at[:, target], near_slots.at[lane], send_near.at[step], recv_near.at[lane],
            device_id=(row, near_peer(step)), device_id_type=MESH_ID,
        )

    def near_in(step):
        source = lax.rem(lane + classes - step, classes)
        return pltpu.make_async_remote_copy(
            part_ref.at[:, source], near_slots.at[source], send_near.at[step], recv_near.at[source],
            device_id=(row, stride * classes + source), device_id_type=MESH_ID,
        )

    def near_start(step, carry):
        near_out(step).start()
        return carry

    def near_finish(step, total):
        near_out(step).wait_send()
        near_in(step).wait_recv()
        source = lax.rem(lane + classes - step, classes)
        return total + near_slots[source].astype(jnp.float32)

    lax.fori_loop(1, classes, near_start, 0)
    class_sum[...] = lax.fori_loop(1, classes, near_finish, own_ref[:, lane])

    def far_out(step):
        target = lax.rem(stride + step, chunk)
        return pltpu.make_async_remote_copy(
            class_sum.at[target], far_slots.at[stride], send_far.at[step], recv_far.at[stride],
            device_id=(row, far_peer(step)), device_id_type=MESH_ID,
        )

    def far_in(step):
        source = lax.rem(stride + chunk - step, chunk)
        return pltpu.make_async_remote_copy(
            class_sum.at[source], far_slots.at[source], send_far.at[step], recv_far.at[source],
            device_id=(row, source * classes + lane), device_id_type=MESH_ID,
        )

    def far_start(step, carry):
        far_out(step).start()
        return carry

    def far_finish(step, total):
        far_out(step).wait_send()
        far_in(step).wait_recv()
        source = lax.rem(stride + chunk - step, chunk)
        return total + far_slots[source]

    lax.fori_loop(1, chunk, far_start, 0)
    out_ref[...] = lax.fori_loop(1, chunk, far_finish, class_sum[stride])


def image_kernel(offs_ref, panel_ref, stiff_ref, triple_ref, out_ref, total_ref, sent_ref,
                 near_slots, class_sum, far_slots, send_near, recv_near, send_far, recv_far):
    term = pl.program_id(0)
    block = pl.program_id(1)
    block_rows = pl.num_programs(1)
    band = stiff_ref.shape[2]
    width = stiff_ref.shape[-1]
    chunk, classes, local_rows, columns = total_ref.shape
    rows = triple_ref.shape[1]
    loads = panel_ref.shape[1] // rows
    rim = (panel_ref.shape[0] - block_rows) // 2

    @pl.when((term == 0) & (block == 0))
    def _():
        scatter_greet(chunk, classes)
        total_ref[...] = jnp.zeros_like(total_ref)

    total = jnp.zeros((loads * rows, width), jnp.float32)
    for slot in range(band):
        place = block + rim + offs_ref[(term * block_rows + block) * band + slot]
        total += lax.dot_general(
            panel_ref[place], stiff_ref[0, 0, slot],
            (((1,), (1,)), ((), ())), preferred_element_type=jnp.float32,
        )
    image = total.astype(jnp.bfloat16)
    for load in range(loads):
        column = pl.multiple_of((load * block_rows + block) * width, width)
        product = jnp.dot(
            triple_ref[0], image[load * rows:(load + 1) * rows], preferred_element_type=jnp.float32
        )
        total_ref[:, :, :, pl.ds(column, width)] += product.reshape(chunk, classes, local_rows, width)

    @pl.when((term == pl.num_programs(0) - 1) & (block == block_rows - 1))
    def _():
        sent_ref[...] = total_ref[...].astype(sent_ref.dtype)
        scatter_stages(sent_ref, total_ref, out_ref, near_slots, class_sum, far_slots,
                       send_near, recv_near, send_far, recv_far)


def image_scatter(offsets, panel, stiff_blocks, dense, local_rows):
    term_count, block_rows, band, width, _ = stiff_blocks.shape
    places, stacked, _ = panel.shape
    rows = dense.shape[1]
    columns = stacked // rows * block_rows * width
    classes = CLASSES
    chunk = rows // (classes * local_rows)
    shape = (chunk, classes, local_rows, columns)
    return pl.pallas_call(
        image_kernel,
        out_shape=jax.ShapeDtypeStruct((local_rows, columns), jnp.float32),
        grid_spec=pltpu.PrefetchScalarGridSpec(
            num_scalar_prefetch=1,
            grid=(term_count, block_rows),
            in_specs=[
                pl.BlockSpec((places, stacked, width), lambda k, b, offs: (0, 0, 0)),
                pl.BlockSpec((1, 1, band, width, width), lambda k, b, offs: (k, b, 0, 0, 0)),
                pl.BlockSpec((1, rows, rows), lambda k, b, offs: (k, 0, 0)),
            ],
            out_specs=pl.BlockSpec((local_rows, columns), lambda k, b, offs: (0, 0)),
            scratch_shapes=[
                pltpu.VMEM(shape, jnp.float32),
                pltpu.VMEM(shape, jnp.bfloat16),
                pltpu.VMEM((classes, chunk, local_rows, columns), jnp.bfloat16),
                pltpu.VMEM((chunk, local_rows, columns), jnp.float32),
                pltpu.VMEM((chunk, local_rows, columns), jnp.float32),
                pltpu.SemaphoreType.DMA((classes,)),
                pltpu.SemaphoreType.DMA((classes,)),
                pltpu.SemaphoreType.DMA((chunk,)),
                pltpu.SemaphoreType.DMA((chunk,)),
            ],
        ),
        compiler_params=pltpu.CompilerParams(collective_id=1, has_side_effects=True),
    )(offsets.reshape(-1), panel, stiff_blocks, dense)


def with_halo(block, sides, width):
    for axis, dim in sides:
        count = lax.axis_size(axis)
        forward = [(i, i + 1) for i in range(count - 1)]
        backward = [(target, source) for source, target in forward]
        low = lax.ppermute(
            lax.slice_in_dim(block, block.shape[dim] - width, None, axis=dim), axis, forward
        )
        high = lax.ppermute(lax.slice_in_dim(block, 0, width, axis=dim), axis, backward)
        block = jnp.concatenate([low, block, high], axis=dim)
    return block


def per_device(chaos_field, stiff_blocks, stiff_offsets, triple_blocks, triple_pattern):
    local_rows = chaos_field.shape[0]
    load_count = chaos_field.shape[1]
    cell_count = chaos_field.shape[2]
    term_count = stiff_blocks.shape[0]
    block_width = stiff_blocks.shape[3]
    block_rows = cell_count // block_width
    groups = lax.axis_size("term")
    total_rows = local_rows * groups
    rim_cells = 2 * block_width
    gathered = gather_term(chaos_field.reshape(local_rows * load_count, cell_count))
    panel = gathered.reshape(groups, local_rows, load_count, block_rows, block_width)
    panel = panel.transpose(3, 2, 0, 1, 4).reshape(block_rows, load_count, total_rows, block_width)
    extended = with_halo(panel, (("space", 0),), rim_cells // block_width)
    extended = extended.reshape(block_rows + 4, load_count * total_rows, block_width)
    block_size = triple_blocks.shape[2]
    levels = jnp.arange(total_rows // block_size, dtype=jnp.int32)
    row_hot = (triple_pattern[:, :, 0:1] == levels).astype(jnp.float32)
    col_hot = (triple_pattern[:, :, 1:2] == levels).astype(jnp.float32)
    dense = jnp.einsum("kna,knb,knxy->kaxby", row_hot, col_hot, triple_blocks.astype(jnp.float32))
    dense = dense.reshape(term_count, total_rows, groups // CLASSES, CLASSES, local_rows)
    dense = dense.transpose(0, 1, 3, 2, 4).reshape(term_count, total_rows, total_rows)
    dense = dense.astype(jnp.bfloat16)
    summed = image_scatter(stiff_offsets, extended, stiff_blocks, dense, local_rows)
    return summed.reshape(local_rows, load_count, cell_count)


def solution(mesh):
    return jax.shard_map(
        per_device,
        mesh=mesh,
        in_specs=(
            P("term", None, "space"),
            P("term", "space", None, None, None),
            P("term", "space", None),
            P("term", None, None, None),
            P("term", None, None),
        ),
        out_specs=P("term", None, "space"),
        check_vma=False,
    )
```

```python
import jax
import jax.numpy as jnp
from jax import lax
from jax.experimental import pallas as pl
from jax.experimental.pallas import tpu as pltpu
from jax.sharding import PartitionSpec as P

MESH_ID = pl.DeviceIdType.MESH


CLASSES = 4
PAIR = 2


def gather_kernel(block_ref, out_ref, local_sem, send_near, recv_near, send_far, recv_far):
    count = out_ref.shape[0]
    chunk = count // CLASSES
    row, stride, lane, far_peer, near_peer = scatter_peers(chunk, CLASSES)
    barrier = pltpu.get_barrier_semaphore()

    def greet_far(step, carry):
        pl.semaphore_signal(barrier, 1, device_id=(row, far_peer(step)), device_id_type=MESH_ID)
        return carry

    def greet_near(step, carry):
        pl.semaphore_signal(barrier, 1, device_id=(row, near_peer(step)), device_id_type=MESH_ID)
        return carry

    lax.fori_loop(1, chunk, greet_far, 0)
    lax.fori_loop(1, CLASSES, greet_near, 0)
    pl.semaphore_wait(barrier, chunk + CLASSES - 2)

    mine = lane * chunk + stride
    local = pltpu.make_async_copy(block_ref, out_ref.at[mine], local_sem)
    local.start()

    def far_out(step):
        return pltpu.make_async_remote_copy(
            block_ref, out_ref.at[mine], send_far.at[step], recv_far.at[stride],
            device_id=(row, far_peer(step)), device_id_type=MESH_ID,
        )

    def far_in(step):
        source = lax.rem(stride + chunk - step, chunk)
        return pltpu.make_async_remote_copy(
            block_ref, out_ref.at[lane * chunk + source], send_far.at[step], recv_far.at[source],
            device_id=(row, term_device(lane, source, chunk)), device_id_type=MESH_ID,
        )

    def far_start(step, carry):
        far_out(step).start()
        return carry

    def far_finish(step, carry):
        far_out(step).wait_send()
        far_in(step).wait_recv()
        return carry

    lax.fori_loop(1, chunk, far_start, 0)
    local.wait()
    lax.fori_loop(1, chunk, far_finish, 0)

    own = out_ref.at[pl.ds(lane * chunk, chunk)]

    def near_out(step):
        return pltpu.make_async_remote_copy(
            own, own, send_near.at[step], recv_near.at[lane],
            device_id=(row, near_peer(step)), device_id_type=MESH_ID,
        )

    def near_in(step):
        source = lax.rem(lane + CLASSES - step, CLASSES)
        theirs = out_ref.at[pl.ds(source * chunk, chunk)]
        return pltpu.make_async_remote_copy(
            theirs, theirs, send_near.at[step], recv_near.at[source],
            device_id=(row, term_device(source, stride, chunk)), device_id_type=MESH_ID,
        )

    def near_start(step, carry):
        near_out(step).start()
        return carry

    def near_finish(step, carry):
        near_out(step).wait_send()
        near_in(step).wait_recv()
        return carry

    lax.fori_loop(1, CLASSES, near_start, 0)
    lax.fori_loop(1, CLASSES, near_finish, 0)


def gather_term(block):
    count = lax.axis_size("term")
    return pl.pallas_call(
        gather_kernel,
        out_shape=jax.ShapeDtypeStruct((count,) + block.shape, block.dtype),
        in_specs=[pl.BlockSpec(memory_space=pltpu.VMEM)],
        out_specs=pl.BlockSpec(memory_space=pltpu.VMEM),
        scratch_shapes=[
            pltpu.SemaphoreType.DMA(()),
            pltpu.SemaphoreType.DMA((CLASSES,)),
            pltpu.SemaphoreType.DMA((CLASSES,)),
            pltpu.SemaphoreType.DMA((count // CLASSES,)),
            pltpu.SemaphoreType.DMA((count // CLASSES,)),
        ],
        compiler_params=pltpu.CompilerParams(collective_id=0, has_side_effects=True),
    )(block)


def term_device(lane, stride, chunk):
    return (lane // PAIR) * (chunk * PAIR) + stride * PAIR + lane % PAIR


def scatter_peers(chunk, classes):
    me = lax.axis_index("term")
    row = lax.axis_index("space")
    ring = chunk * PAIR
    stride = lax.rem(me, ring) // PAIR
    lane = (me // ring) * PAIR + lax.rem(me, PAIR)

    def far_peer(step):
        return term_device(lane, lax.rem(stride + step, chunk), chunk)

    def near_peer(step):
        return term_device(lax.rem(lane + step, classes), stride, chunk)

    return row, stride, lane, far_peer, near_peer


def scatter_greet(chunk, classes):
    row, stride, lane, far_peer, near_peer = scatter_peers(chunk, classes)
    barrier = pltpu.get_barrier_semaphore()

    def greet_far(step, carry):
        pl.semaphore_signal(barrier, 1, device_id=(row, far_peer(step)), device_id_type=MESH_ID)
        return carry

    def greet_near(step, carry):
        pl.semaphore_signal(barrier, 1, device_id=(row, near_peer(step)), device_id_type=MESH_ID)
        return carry

    lax.fori_loop(1, chunk, greet_far, 0)
    lax.fori_loop(1, classes, greet_near, 0)


def scatter_stages(part_ref, own_ref, out_ref, near_slots, class_sum, far_slots,
                   send_near, recv_near, send_far, recv_far):
    chunk, classes = part_ref.shape[1], part_ref.shape[0] * part_ref.shape[2]
    row, stride, lane, far_peer, near_peer = scatter_peers(chunk, classes)
    pl.semaphore_wait(pltpu.get_barrier_semaphore(), chunk + classes - 2)

    def near_out(step):
        target = lax.rem(lane + step, classes)
        return pltpu.make_async_remote_copy(
            part_ref.at[target // PAIR, :, target % PAIR], near_slots.at[lane], send_near.at[step],
            recv_near.at[lane],
            device_id=(row, near_peer(step)), device_id_type=MESH_ID,
        )

    def near_in(step):
        source = lax.rem(lane + classes - step, classes)
        return pltpu.make_async_remote_copy(
            part_ref.at[source // PAIR, :, source % PAIR], near_slots.at[source], send_near.at[step],
            recv_near.at[source],
            device_id=(row, term_device(source, stride, chunk)), device_id_type=MESH_ID,
        )

    def near_start(step, carry):
        near_out(step).start()
        return carry

    def near_finish(step, total):
        near_out(step).wait_send()
        near_in(step).wait_recv()
        source = lax.rem(lane + classes - step, classes)
        return total + near_slots[source].astype(jnp.float32)

    lax.fori_loop(1, classes, near_start, 0)
    class_sum[...] = lax.fori_loop(1, classes, near_finish, own_ref[lane // PAIR, :, lane % PAIR])

    def far_out(step):
        target = lax.rem(stride + step, chunk)
        return pltpu.make_async_remote_copy(
            class_sum.at[target], far_slots.at[stride], send_far.at[step], recv_far.at[stride],
            device_id=(row, far_peer(step)), device_id_type=MESH_ID,
        )

    def far_in(step):
        source = lax.rem(stride + chunk - step, chunk)
        return pltpu.make_async_remote_copy(
            class_sum.at[source], far_slots.at[source], send_far.at[step], recv_far.at[source],
            device_id=(row, term_device(lane, source, chunk)), device_id_type=MESH_ID,
        )

    def far_start(step, carry):
        far_out(step).start()
        return carry

    def far_finish(step, total):
        far_out(step).wait_send()
        far_in(step).wait_recv()
        source = lax.rem(stride + chunk - step, chunk)
        return total + far_slots[source]

    lax.fori_loop(1, chunk, far_start, 0)
    out_ref[...] = lax.fori_loop(1, chunk, far_finish, class_sum[stride])


def image_kernel(offs_ref, panel_ref, stiff_ref, triple_ref, out_ref, total_ref, sent_ref,
                 near_slots, class_sum, far_slots, send_near, recv_near, send_far, recv_far):
    term = pl.program_id(0)
    block = pl.program_id(1)
    block_rows = pl.num_programs(1)
    band = stiff_ref.shape[2]
    width = stiff_ref.shape[-1]
    sides, chunk, _, local_rows, columns = total_ref.shape
    classes = sides * PAIR
    rows = triple_ref.shape[1]
    loads = panel_ref.shape[1] // rows
    rim = (panel_ref.shape[0] - block_rows) // 2

    @pl.when((term == 0) & (block == 0))
    def _():
        scatter_greet(chunk, classes)
        total_ref[...] = jnp.zeros_like(total_ref)

    total = jnp.zeros((loads * rows, width), jnp.float32)
    for slot in range(band):
        place = block + rim + offs_ref[(term * block_rows + block) * band + slot]
        total += lax.dot_general(
            panel_ref[place], stiff_ref[0, 0, slot],
            (((1,), (1,)), ((), ())), preferred_element_type=jnp.float32,
        )
    image = total.astype(jnp.bfloat16)
    for load in range(loads):
        column = pl.multiple_of((load * block_rows + block) * width, width)
        product = jnp.dot(
            triple_ref[0], image[load * rows:(load + 1) * rows], preferred_element_type=jnp.float32
        )
        total_ref[:, :, :, :, pl.ds(column, width)] += product.reshape(
            sides, chunk, PAIR, local_rows, width
        )

    @pl.when((term == pl.num_programs(0) - 1) & (block == block_rows - 1))
    def _():
        sent_ref[...] = total_ref[...].astype(sent_ref.dtype)
        scatter_stages(sent_ref, total_ref, out_ref, near_slots, class_sum, far_slots,
                       send_near, recv_near, send_far, recv_far)


def image_scatter(offsets, panel, stiff_blocks, dense, local_rows):
    term_count, block_rows, band, width, _ = stiff_blocks.shape
    places, stacked, _ = panel.shape
    rows = dense.shape[1]
    columns = stacked // rows * block_rows * width
    classes = CLASSES
    chunk = rows // (classes * local_rows)
    shape = (classes // PAIR, chunk, PAIR, local_rows, columns)
    return pl.pallas_call(
        image_kernel,
        out_shape=jax.ShapeDtypeStruct((local_rows, columns), jnp.float32),
        grid_spec=pltpu.PrefetchScalarGridSpec(
            num_scalar_prefetch=1,
            grid=(term_count, block_rows),
            in_specs=[
                pl.BlockSpec((places, stacked, width), lambda k, b, offs: (0, 0, 0)),
                pl.BlockSpec((1, 1, band, width, width), lambda k, b, offs: (k, b, 0, 0, 0)),
                pl.BlockSpec((1, rows, rows), lambda k, b, offs: (k, 0, 0)),
            ],
            out_specs=pl.BlockSpec((local_rows, columns), lambda k, b, offs: (0, 0)),
            scratch_shapes=[
                pltpu.VMEM(shape, jnp.float32),
                pltpu.VMEM(shape, jnp.bfloat16),
                pltpu.VMEM((classes, chunk, local_rows, columns), jnp.bfloat16),
                pltpu.VMEM((chunk, local_rows, columns), jnp.float32),
                pltpu.VMEM((chunk, local_rows, columns), jnp.float32),
                pltpu.SemaphoreType.DMA((classes,)),
                pltpu.SemaphoreType.DMA((classes,)),
                pltpu.SemaphoreType.DMA((chunk,)),
                pltpu.SemaphoreType.DMA((chunk,)),
            ],
        ),
        compiler_params=pltpu.CompilerParams(collective_id=1, has_side_effects=True),
    )(offsets.reshape(-1), panel, stiff_blocks, dense)


def with_halo(block, sides, width):
    for axis, dim in sides:
        count = lax.axis_size(axis)
        forward = [(i, i + 1) for i in range(count - 1)]
        backward = [(target, source) for source, target in forward]
        low = lax.ppermute(
            lax.slice_in_dim(block, block.shape[dim] - width, None, axis=dim), axis, forward
        )
        high = lax.ppermute(lax.slice_in_dim(block, 0, width, axis=dim), axis, backward)
        block = jnp.concatenate([low, block, high], axis=dim)
    return block


def per_device(chaos_field, stiff_blocks, stiff_offsets, triple_blocks, triple_pattern):
    local_rows = chaos_field.shape[0]
    load_count = chaos_field.shape[1]
    cell_count = chaos_field.shape[2]
    term_count = stiff_blocks.shape[0]
    block_width = stiff_blocks.shape[3]
    block_rows = cell_count // block_width
    groups = lax.axis_size("term")
    total_rows = local_rows * groups
    rim_cells = 2 * block_width
    gathered = gather_term(chaos_field.reshape(local_rows * load_count, cell_count))
    panel = gathered.reshape(groups, local_rows, load_count, block_rows, block_width)
    panel = panel.transpose(3, 2, 0, 1, 4).reshape(block_rows, load_count, total_rows, block_width)
    extended = with_halo(panel, (("space", 0),), rim_cells // block_width)
    extended = extended.reshape(block_rows + 4, load_count * total_rows, block_width)
    block_size = triple_blocks.shape[2]
    levels = jnp.arange(total_rows // block_size, dtype=jnp.int32)
    row_hot = (triple_pattern[:, :, 0:1] == levels).astype(jnp.float32)
    col_hot = (triple_pattern[:, :, 1:2] == levels).astype(jnp.float32)
    dense = jnp.einsum("kna,knb,knxy->kaxby", row_hot, col_hot, triple_blocks.astype(jnp.float32))
    dense = dense.reshape(term_count, total_rows, CLASSES // PAIR, groups // CLASSES, PAIR, local_rows)
    dense = dense.transpose(0, 1, 2, 4, 3, 5).reshape(term_count, total_rows, total_rows)
    dense = dense.astype(jnp.bfloat16)
    summed = image_scatter(stiff_offsets, extended, stiff_blocks, dense, local_rows)
    return summed.reshape(local_rows, load_count, cell_count)


def solution(mesh):
    return jax.shard_map(
        per_device,
        mesh=mesh,
        in_specs=(
            P("term", None, "space"),
            P("term", "space", None, None, None),
            P("term", "space", None),
            P("term", None, None, None),
            P("term", None, None),
        ),
        out_specs=P("term", None, "space"),
        check_vma=False,
    )
```

```python
import jax
import jax.numpy as jnp
from jax import lax
from jax.experimental import pallas as pl
from jax.experimental.pallas import tpu as pltpu
from jax.sharding import PartitionSpec as P

MESH_ID = pl.DeviceIdType.MESH


CLASSES = 4
PAIR = 2


def gather_kernel(block_ref, out_ref, local_sem, send_near, recv_near, send_far, recv_far):
    count = out_ref.shape[0]
    chunk = count // CLASSES
    row, stride, lane, far_peer, near_peer = scatter_peers(chunk, CLASSES)
    barrier = pltpu.get_barrier_semaphore()

    def greet_far(step, carry):
        pl.semaphore_signal(barrier, 1, device_id=(row, far_peer(step)), device_id_type=MESH_ID)
        return carry

    def greet_near(step, carry):
        pl.semaphore_signal(barrier, 1, device_id=(row, near_peer(step)), device_id_type=MESH_ID)
        return carry

    lax.fori_loop(1, chunk, greet_far, 0)
    lax.fori_loop(1, CLASSES, greet_near, 0)
    pl.semaphore_wait(barrier, chunk + CLASSES - 2)

    mine = lane * chunk + stride
    local = pltpu.make_async_copy(block_ref, out_ref.at[mine], local_sem)
    local.start()

    def far_out(step):
        return pltpu.make_async_remote_copy(
            block_ref, out_ref.at[mine], send_far.at[step], recv_far.at[stride],
            device_id=(row, far_peer(step)), device_id_type=MESH_ID,
        )

    def far_in(step):
        source = lax.rem(stride + chunk - step, chunk)
        return pltpu.make_async_remote_copy(
            block_ref, out_ref.at[lane * chunk + source], send_far.at[step], recv_far.at[source],
            device_id=(row, term_device(lane, source, chunk)), device_id_type=MESH_ID,
        )

    def far_start(step, carry):
        far_out(step).start()
        return carry

    def far_finish(step, carry):
        far_out(step).wait_send()
        far_in(step).wait_recv()
        return carry

    lax.fori_loop(1, chunk, far_start, 0)
    local.wait()
    lax.fori_loop(1, chunk, far_finish, 0)

    own = out_ref.at[pl.ds(lane * chunk, chunk)]

    def near_out(step):
        return pltpu.make_async_remote_copy(
            own, own, send_near.at[step], recv_near.at[lane],
            device_id=(row, near_peer(step)), device_id_type=MESH_ID,
        )

    def near_in(step):
        source = lax.rem(lane + CLASSES - step, CLASSES)
        theirs = out_ref.at[pl.ds(source * chunk, chunk)]
        return pltpu.make_async_remote_copy(
            theirs, theirs, send_near.at[step], recv_near.at[source],
            device_id=(row, term_device(source, stride, chunk)), device_id_type=MESH_ID,
        )

    def near_start(step, carry):
        near_out(step).start()
        return carry

    def near_finish(step, carry):
        near_out(step).wait_send()
        near_in(step).wait_recv()
        return carry

    lax.fori_loop(1, CLASSES, near_start, 0)
    lax.fori_loop(1, CLASSES, near_finish, 0)


def gather_term(block):
    count = lax.axis_size("term")
    return pl.pallas_call(
        gather_kernel,
        out_shape=jax.ShapeDtypeStruct((count,) + block.shape, block.dtype),
        in_specs=[pl.BlockSpec(memory_space=pltpu.VMEM)],
        out_specs=pl.BlockSpec(memory_space=pltpu.VMEM),
        scratch_shapes=[
            pltpu.SemaphoreType.DMA(()),
            pltpu.SemaphoreType.DMA((CLASSES,)),
            pltpu.SemaphoreType.DMA((CLASSES,)),
            pltpu.SemaphoreType.DMA((count // CLASSES,)),
            pltpu.SemaphoreType.DMA((count // CLASSES,)),
        ],
        compiler_params=pltpu.CompilerParams(collective_id=0, has_side_effects=True),
    )(block)


def term_device(lane, stride, chunk):
    return (lane // PAIR) * (chunk * PAIR) + stride * PAIR + lane % PAIR


def scatter_peers(chunk, classes):
    me = lax.axis_index("term")
    row = lax.axis_index("space")
    ring = chunk * PAIR
    stride = lax.rem(me, ring) // PAIR
    lane = (me // ring) * PAIR + lax.rem(me, PAIR)

    def far_peer(step):
        return term_device(lane, lax.rem(stride + step, chunk), chunk)

    def near_peer(step):
        return term_device(lax.rem(lane + step, classes), stride, chunk)

    return row, stride, lane, far_peer, near_peer


def scatter_greet(chunk, classes):
    row, stride, lane, far_peer, near_peer = scatter_peers(chunk, classes)
    barrier = pltpu.get_barrier_semaphore()

    def greet_far(step, carry):
        pl.semaphore_signal(barrier, 1, device_id=(row, far_peer(step)), device_id_type=MESH_ID)
        return carry

    def greet_near(step, carry):
        pl.semaphore_signal(barrier, 1, device_id=(row, near_peer(step)), device_id_type=MESH_ID)
        return carry

    lax.fori_loop(1, chunk, greet_far, 0)
    lax.fori_loop(1, classes, greet_near, 0)


def image_kernel(offs_ref, panel_ref, stiff_ref, triple_ref, out_ref, total_ref, sent_ref,
                 near_slots, class_sum, far_slots, send_near, recv_near, send_far, recv_far):
    block = pl.program_id(0)
    term = pl.program_id(1)
    band = stiff_ref.shape[2]
    width = stiff_ref.shape[-1]
    sides, chunk, _, local_rows, columns = total_ref.shape
    classes = sides * PAIR
    rows = triple_ref.shape[1]
    loads = panel_ref.shape[1] // rows
    block_rows = columns // (loads * width)
    term_count = pl.num_programs(1)
    rim = (panel_ref.shape[0] - block_rows) // 2
    half = loads * width
    row, stride, lane, far_peer, near_peer = scatter_peers(chunk, classes)

    @pl.when((term == 0) & (block == 0))
    def _():
        scatter_greet(chunk, classes)
        total_ref[...] = jnp.zeros_like(total_ref)

    total = jnp.zeros((loads * rows, width), jnp.float32)
    for slot in range(band):
        place = block + rim + offs_ref[(term * block_rows + block) * band + slot]
        total += lax.dot_general(
            panel_ref[place], stiff_ref[0, 0, slot],
            (((1,), (1,)), ((), ())), preferred_element_type=jnp.float32,
        )
    image = total.astype(jnp.bfloat16)
    for load in range(loads):
        column = pl.multiple_of((block * loads + load) * width, width)
        product = jnp.dot(
            triple_ref[0], image[load * rows:(load + 1) * rows], preferred_element_type=jnp.float32
        )
        total_ref[:, :, :, :, pl.ds(column, width)] += product.reshape(
            sides, chunk, PAIR, local_rows, width
        )

    def near_copy(step, part, inbound):
        cols = pl.ds(pl.multiple_of(part * half, half), half)
        if inbound:
            source = lax.rem(lane + classes - step, classes)
            return pltpu.make_async_remote_copy(
                sent_ref.at[source // PAIR, :, source % PAIR, :, cols],
                near_slots.at[source, :, :, cols], send_near.at[part, step], recv_near.at[part, source],
                device_id=(row, term_device(source, stride, chunk)), device_id_type=MESH_ID,
            )
        target = lax.rem(lane + step, classes)
        return pltpu.make_async_remote_copy(
            sent_ref.at[target // PAIR, :, target % PAIR, :, cols],
            near_slots.at[lane, :, :, cols], send_near.at[part, step], recv_near.at[part, lane],
            device_id=(row, near_peer(step)), device_id_type=MESH_ID,
        )

    @pl.when(term == term_count - 1)
    def _():
        cols = pl.ds(pl.multiple_of(block * half, half), half)
        sent_ref[:, :, :, :, cols] = total_ref[:, :, :, :, cols].astype(sent_ref.dtype)

        @pl.when(block == 0)
        def _():
            pl.semaphore_wait(pltpu.get_barrier_semaphore(), chunk + classes - 2)

        def near_start(step, carry):
            near_copy(step, block, False).start()
            return carry

        lax.fori_loop(1, classes, near_start, 0)

    @pl.when((term == term_count - 1) & (block == block_rows - 1))
    def _():
        for part in range(block_rows):
            cols = pl.ds(part * half, half)

            def near_finish(step, total):
                near_copy(step, part, False).wait_send()
                near_copy(step, part, True).wait_recv()
                source = lax.rem(lane + classes - step, classes)
                return total + near_slots[source, :, :, cols].astype(jnp.float32)

            own = total_ref[lane // PAIR, :, lane % PAIR, :, cols]
            class_sum[:, :, cols] = lax.fori_loop(1, classes, near_finish, own)

        def far_out(step):
            target = lax.rem(stride + step, chunk)
            return pltpu.make_async_remote_copy(
                class_sum.at[target], far_slots.at[stride], send_far.at[step], recv_far.at[stride],
                device_id=(row, far_peer(step)), device_id_type=MESH_ID,
            )

        def far_in(step):
            source = lax.rem(stride + chunk - step, chunk)
            return pltpu.make_async_remote_copy(
                class_sum.at[source], far_slots.at[source], send_far.at[step], recv_far.at[source],
                device_id=(row, term_device(lane, source, chunk)), device_id_type=MESH_ID,
            )

        def far_start(step, carry):
            far_out(step).start()
            return carry

        def far_finish(step, total):
            far_out(step).wait_send()
            far_in(step).wait_recv()
            source = lax.rem(stride + chunk - step, chunk)
            return total + far_slots[source]

        lax.fori_loop(1, chunk, far_start, 0)
        summed = lax.fori_loop(1, chunk, far_finish, class_sum[stride])
        for part in range(block_rows):
            for load in range(loads):
                source = (part * loads + load) * width
                target = (load * block_rows + part) * width
                out_ref[:, target:target + width] = summed[:, source:source + width]


def image_scatter(offsets, panel, stiff_blocks, dense, local_rows):
    term_count, block_rows, band, width, _ = stiff_blocks.shape
    places, stacked, _ = panel.shape
    rows = dense.shape[1]
    columns = stacked // rows * block_rows * width
    classes = CLASSES
    chunk = rows // (classes * local_rows)
    shape = (classes // PAIR, chunk, PAIR, local_rows, columns)
    return pl.pallas_call(
        image_kernel,
        out_shape=jax.ShapeDtypeStruct((local_rows, columns), jnp.float32),
        grid_spec=pltpu.PrefetchScalarGridSpec(
            num_scalar_prefetch=1,
            grid=(block_rows, term_count),
            in_specs=[
                pl.BlockSpec((places, stacked, width), lambda b, k, offs: (0, 0, 0)),
                pl.BlockSpec((1, 1, band, width, width), lambda b, k, offs: (k, b, 0, 0, 0)),
                pl.BlockSpec((1, rows, rows), lambda b, k, offs: (k, 0, 0)),
            ],
            out_specs=pl.BlockSpec((local_rows, columns), lambda b, k, offs: (0, 0)),
            scratch_shapes=[
                pltpu.VMEM(shape, jnp.float32),
                pltpu.VMEM(shape, jnp.bfloat16),
                pltpu.VMEM((classes, chunk, local_rows, columns), jnp.bfloat16),
                pltpu.VMEM((chunk, local_rows, columns), jnp.float32),
                pltpu.VMEM((chunk, local_rows, columns), jnp.float32),
                pltpu.SemaphoreType.DMA((block_rows, classes)),
                pltpu.SemaphoreType.DMA((block_rows, classes)),
                pltpu.SemaphoreType.DMA((chunk,)),
                pltpu.SemaphoreType.DMA((chunk,)),
            ],
        ),
        compiler_params=pltpu.CompilerParams(collective_id=1, has_side_effects=True),
    )(offsets.reshape(-1), panel, stiff_blocks, dense)


def with_halo(block, sides, width):
    for axis, dim in sides:
        count = lax.axis_size(axis)
        forward = [(i, i + 1) for i in range(count - 1)]
        backward = [(target, source) for source, target in forward]
        low = lax.ppermute(
            lax.slice_in_dim(block, block.shape[dim] - width, None, axis=dim), axis, forward
        )
        high = lax.ppermute(lax.slice_in_dim(block, 0, width, axis=dim), axis, backward)
        block = jnp.concatenate([low, block, high], axis=dim)
    return block


def per_device(chaos_field, stiff_blocks, stiff_offsets, triple_blocks, triple_pattern):
    local_rows = chaos_field.shape[0]
    load_count = chaos_field.shape[1]
    cell_count = chaos_field.shape[2]
    term_count = stiff_blocks.shape[0]
    block_width = stiff_blocks.shape[3]
    block_rows = cell_count // block_width
    groups = lax.axis_size("term")
    total_rows = local_rows * groups
    rim_cells = 2 * block_width
    gathered = gather_term(chaos_field.reshape(local_rows * load_count, cell_count))
    panel = gathered.reshape(groups, local_rows, load_count, block_rows, block_width)
    panel = panel.transpose(3, 2, 0, 1, 4).reshape(block_rows, load_count, total_rows, block_width)
    extended = with_halo(panel, (("space", 0),), rim_cells // block_width)
    extended = extended.reshape(block_rows + 4, load_count * total_rows, block_width)
    block_size = triple_blocks.shape[2]
    levels = jnp.arange(total_rows // block_size, dtype=jnp.int32)
    row_hot = (triple_pattern[:, :, 0:1] == levels).astype(jnp.float32)
    col_hot = (triple_pattern[:, :, 1:2] == levels).astype(jnp.float32)
    dense = jnp.einsum("kna,knb,knxy->kaxby", row_hot, col_hot, triple_blocks.astype(jnp.float32))
    dense = dense.reshape(term_count, total_rows, CLASSES // PAIR, groups // CLASSES, PAIR, local_rows)
    dense = dense.transpose(0, 1, 2, 4, 3, 5).reshape(term_count, total_rows, total_rows)
    dense = dense.astype(jnp.bfloat16)
    summed = image_scatter(stiff_offsets, extended, stiff_blocks, dense, local_rows)
    return summed.reshape(local_rows, load_count, cell_count)


def solution(mesh):
    return jax.shard_map(
        per_device,
        mesh=mesh,
        in_specs=(
            P("term", None, "space"),
            P("term", "space", None, None, None),
            P("term", "space", None),
            P("term", None, None, None),
            P("term", None, None),
        ),
        out_specs=P("term", None, "space"),
        check_vma=False,
    )
```

```python
import jax
import jax.numpy as jnp
from jax import lax
from jax.experimental import pallas as pl
from jax.experimental.pallas import tpu as pltpu
from jax.sharding import PartitionSpec as P

MESH_ID = pl.DeviceIdType.MESH


CLASSES = 4
PAIR = 2


def gather_kernel(block_ref, out_ref, local_sem, send_near, recv_near, send_far, recv_far):
    count = out_ref.shape[0]
    chunk = count // CLASSES
    row, stride, lane, far_peer, near_peer = scatter_peers(chunk, CLASSES)
    barrier = pltpu.get_barrier_semaphore()

    def greet_far(step, carry):
        pl.semaphore_signal(barrier, 1, device_id=(row, far_peer(step)), device_id_type=MESH_ID)
        return carry

    def greet_near(step, carry):
        pl.semaphore_signal(barrier, 1, device_id=(row, near_peer(step)), device_id_type=MESH_ID)
        return carry

    lax.fori_loop(1, chunk, greet_far, 0)
    lax.fori_loop(1, CLASSES, greet_near, 0)
    pl.semaphore_wait(barrier, chunk + CLASSES - 2)

    mine = lane * chunk + stride
    local = pltpu.make_async_copy(block_ref, out_ref.at[mine], local_sem)
    local.start()

    def far_out(step):
        return pltpu.make_async_remote_copy(
            block_ref, out_ref.at[mine], send_far.at[step], recv_far.at[stride],
            device_id=(row, far_peer(step)), device_id_type=MESH_ID,
        )

    def far_in(step):
        source = lax.rem(stride + chunk - step, chunk)
        return pltpu.make_async_remote_copy(
            block_ref, out_ref.at[lane * chunk + source], send_far.at[step], recv_far.at[source],
            device_id=(row, term_device(lane, source, chunk)), device_id_type=MESH_ID,
        )

    def far_start(step, carry):
        far_out(step).start()
        return carry

    def far_finish(step, carry):
        far_out(step).wait_send()
        far_in(step).wait_recv()
        return carry

    lax.fori_loop(1, chunk, far_start, 0)
    local.wait()
    lax.fori_loop(1, chunk, far_finish, 0)

    own = out_ref.at[pl.ds(lane * chunk, chunk)]

    def near_out(step):
        return pltpu.make_async_remote_copy(
            own, own, send_near.at[step], recv_near.at[lane],
            device_id=(row, near_peer(step)), device_id_type=MESH_ID,
        )

    def near_in(step):
        source = lax.rem(lane + CLASSES - step, CLASSES)
        theirs = out_ref.at[pl.ds(source * chunk, chunk)]
        return pltpu.make_async_remote_copy(
            theirs, theirs, send_near.at[step], recv_near.at[source],
            device_id=(row, term_device(source, stride, chunk)), device_id_type=MESH_ID,
        )

    def near_start(step, carry):
        near_out(step).start()
        return carry

    def near_finish(step, carry):
        near_out(step).wait_send()
        near_in(step).wait_recv()
        return carry

    lax.fori_loop(1, CLASSES, near_start, 0)
    lax.fori_loop(1, CLASSES, near_finish, 0)


def gather_term(block):
    count = lax.axis_size("term")
    return pl.pallas_call(
        gather_kernel,
        out_shape=jax.ShapeDtypeStruct((count,) + block.shape, block.dtype),
        in_specs=[pl.BlockSpec(memory_space=pltpu.VMEM)],
        out_specs=pl.BlockSpec(memory_space=pltpu.VMEM),
        scratch_shapes=[
            pltpu.SemaphoreType.DMA(()),
            pltpu.SemaphoreType.DMA((CLASSES,)),
            pltpu.SemaphoreType.DMA((CLASSES,)),
            pltpu.SemaphoreType.DMA((count // CLASSES,)),
            pltpu.SemaphoreType.DMA((count // CLASSES,)),
        ],
        compiler_params=pltpu.CompilerParams(collective_id=0, has_side_effects=True),
    )(block)


def term_device(lane, stride, chunk):
    return (lane // PAIR) * (chunk * PAIR) + stride * PAIR + lane % PAIR


def scatter_peers(chunk, classes):
    me = lax.axis_index("term")
    row = lax.axis_index("space")
    ring = chunk * PAIR
    stride = lax.rem(me, ring) // PAIR
    lane = (me // ring) * PAIR + lax.rem(me, PAIR)

    def far_peer(step):
        return term_device(lane, lax.rem(stride + step, chunk), chunk)

    def near_peer(step):
        return term_device(lax.rem(lane + step, classes), stride, chunk)

    return row, stride, lane, far_peer, near_peer


def scatter_greet(chunk, classes):
    row, stride, lane, far_peer, near_peer = scatter_peers(chunk, classes)
    barrier = pltpu.get_barrier_semaphore()

    def greet_far(step, carry):
        pl.semaphore_signal(barrier, 1, device_id=(row, far_peer(step)), device_id_type=MESH_ID)
        return carry

    def greet_near(step, carry):
        pl.semaphore_signal(barrier, 1, device_id=(row, near_peer(step)), device_id_type=MESH_ID)
        return carry

    lax.fori_loop(1, chunk, greet_far, 0)
    lax.fori_loop(1, classes, greet_near, 0)


def image_kernel(offs_ref, panel_ref, stiff_ref, triple_ref, out_ref, total_ref, far_src,
                 near_slots, class_sum, far_slots, send_near, recv_near, send_far, recv_far):
    block = pl.program_id(0)
    term = pl.program_id(1)
    band = stiff_ref.shape[2]
    width = stiff_ref.shape[-1]
    sides, chunk, _, local_rows, columns = total_ref.shape
    classes = sides * PAIR
    rows = triple_ref.shape[1]
    loads = panel_ref.shape[1] // rows
    block_rows = columns // (loads * width)
    term_count = pl.num_programs(1)
    rim = (panel_ref.shape[0] - block_rows) // 2
    half = loads * width
    row, stride, lane, far_peer, near_peer = scatter_peers(chunk, classes)

    @pl.when((term == 0) & (block == 0))
    def _():
        scatter_greet(chunk, classes)
        total_ref[...] = jnp.zeros_like(total_ref)

    total = jnp.zeros((loads * rows, width), jnp.float32)
    for slot in range(band):
        place = block + rim + offs_ref[(term * block_rows + block) * band + slot]
        total += lax.dot_general(
            panel_ref[place], stiff_ref[0, 0, slot],
            (((1,), (1,)), ((), ())), preferred_element_type=jnp.float32,
        )
    image = total.astype(jnp.bfloat16)
    for load in range(loads):
        column = pl.multiple_of((block * loads + load) * width, width)
        product = jnp.dot(
            triple_ref[0], image[load * rows:(load + 1) * rows], preferred_element_type=jnp.float32
        )
        total_ref[:, :, :, :, pl.ds(column, width)] += product.reshape(
            sides, chunk, PAIR, local_rows, width
        )

    def near_copy(step, part, inbound):
        cols = pl.ds(pl.multiple_of(part * half, half), half)
        if inbound:
            source = lax.rem(lane + classes - step, classes)
            return pltpu.make_async_remote_copy(
                total_ref.at[source // PAIR, :, source % PAIR, :, cols],
                near_slots.at[source, :, :, cols], send_near.at[part, step], recv_near.at[part, source],
                device_id=(row, term_device(source, stride, chunk)), device_id_type=MESH_ID,
            )
        target = lax.rem(lane + step, classes)
        return pltpu.make_async_remote_copy(
            total_ref.at[target // PAIR, :, target % PAIR, :, cols],
            near_slots.at[lane, :, :, cols], send_near.at[part, step], recv_near.at[part, lane],
            device_id=(row, near_peer(step)), device_id_type=MESH_ID,
        )

    @pl.when(term == term_count - 1)
    def _():
        @pl.when(block == 0)
        def _():
            pl.semaphore_wait(pltpu.get_barrier_semaphore(), chunk + classes - 2)

        def near_start(step, carry):
            near_copy(step, block, False).start()
            return carry

        lax.fori_loop(1, classes, near_start, 0)

    @pl.when((term == term_count - 1) & (block == block_rows - 1))
    def _():
        for part in range(block_rows):
            cols = pl.ds(part * half, half)

            def near_finish(step, total):
                near_copy(step, part, False).wait_send()
                near_copy(step, part, True).wait_recv()
                source = lax.rem(lane + classes - step, classes)
                return total + near_slots[source, :, :, cols]

            own = total_ref[lane // PAIR, :, lane % PAIR, :, cols]
            class_sum[:, :, cols] = lax.fori_loop(1, classes, near_finish, own)

        far_src[...] = class_sum[...].astype(far_src.dtype)

        def far_out(step):
            target = lax.rem(stride + step, chunk)
            return pltpu.make_async_remote_copy(
                far_src.at[target], far_slots.at[stride], send_far.at[step], recv_far.at[stride],
                device_id=(row, far_peer(step)), device_id_type=MESH_ID,
            )

        def far_in(step):
            source = lax.rem(stride + chunk - step, chunk)
            return pltpu.make_async_remote_copy(
                far_src.at[source], far_slots.at[source], send_far.at[step], recv_far.at[source],
                device_id=(row, term_device(lane, source, chunk)), device_id_type=MESH_ID,
            )

        def far_start(step, carry):
            far_out(step).start()
            return carry

        def far_finish(step, total):
            far_out(step).wait_send()
            far_in(step).wait_recv()
            source = lax.rem(stride + chunk - step, chunk)
            return total + far_slots[source].astype(jnp.float32)

        lax.fori_loop(1, chunk, far_start, 0)
        summed = lax.fori_loop(1, chunk, far_finish, class_sum[stride])
        for part in range(block_rows):
            for load in range(loads):
                source = (part * loads + load) * width
                target = (load * block_rows + part) * width
                out_ref[:, target:target + width] = summed[:, source:source + width]


def image_scatter(offsets, panel, stiff_blocks, dense, local_rows):
    term_count, block_rows, band, width, _ = stiff_blocks.shape
    places, stacked, _ = panel.shape
    rows = dense.shape[1]
    columns = stacked // rows * block_rows * width
    classes = CLASSES
    chunk = rows // (classes * local_rows)
    shape = (classes // PAIR, chunk, PAIR, local_rows, columns)
    return pl.pallas_call(
        image_kernel,
        out_shape=jax.ShapeDtypeStruct((local_rows, columns), jnp.float32),
        grid_spec=pltpu.PrefetchScalarGridSpec(
            num_scalar_prefetch=1,
            grid=(block_rows, term_count),
            in_specs=[
                pl.BlockSpec((places, stacked, width), lambda b, k, offs: (0, 0, 0)),
                pl.BlockSpec((1, 1, band, width, width), lambda b, k, offs: (k, b, 0, 0, 0)),
                pl.BlockSpec((1, rows, rows), lambda b, k, offs: (k, 0, 0)),
            ],
            out_specs=pl.BlockSpec((local_rows, columns), lambda b, k, offs: (0, 0)),
            scratch_shapes=[
                pltpu.VMEM(shape, jnp.float32),
                pltpu.VMEM((chunk, local_rows, columns), jnp.bfloat16),
                pltpu.VMEM((classes, chunk, local_rows, columns), jnp.float32),
                pltpu.VMEM((chunk, local_rows, columns), jnp.float32),
                pltpu.VMEM((chunk, local_rows, columns), jnp.bfloat16),
                pltpu.SemaphoreType.DMA((block_rows, classes)),
                pltpu.SemaphoreType.DMA((block_rows, classes)),
                pltpu.SemaphoreType.DMA((chunk,)),
                pltpu.SemaphoreType.DMA((chunk,)),
            ],
        ),
        compiler_params=pltpu.CompilerParams(collective_id=1, has_side_effects=True),
    )(offsets.reshape(-1), panel, stiff_blocks, dense)


def with_halo(block, sides, width):
    for axis, dim in sides:
        count = lax.axis_size(axis)
        forward = [(i, i + 1) for i in range(count - 1)]
        backward = [(target, source) for source, target in forward]
        low = lax.ppermute(
            lax.slice_in_dim(block, block.shape[dim] - width, None, axis=dim), axis, forward
        )
        high = lax.ppermute(lax.slice_in_dim(block, 0, width, axis=dim), axis, backward)
        block = jnp.concatenate([low, block, high], axis=dim)
    return block


def per_device(chaos_field, stiff_blocks, stiff_offsets, triple_blocks, triple_pattern):
    local_rows = chaos_field.shape[0]
    load_count = chaos_field.shape[1]
    cell_count = chaos_field.shape[2]
    term_count = stiff_blocks.shape[0]
    block_width = stiff_blocks.shape[3]
    block_rows = cell_count // block_width
    groups = lax.axis_size("term")
    total_rows = local_rows * groups
    rim_cells = 2 * block_width
    gathered = gather_term(chaos_field.reshape(local_rows * load_count, cell_count))
    panel = gathered.reshape(groups, local_rows, load_count, block_rows, block_width)
    panel = panel.transpose(3, 2, 0, 1, 4).reshape(block_rows, load_count, total_rows, block_width)
    extended = with_halo(panel, (("space", 0),), rim_cells // block_width)
    extended = extended.reshape(block_rows + 4, load_count * total_rows, block_width)
    block_size = triple_blocks.shape[2]
    levels = jnp.arange(total_rows // block_size, dtype=jnp.int32)
    row_hot = (triple_pattern[:, :, 0:1] == levels).astype(jnp.float32)
    col_hot = (triple_pattern[:, :, 1:2] == levels).astype(jnp.float32)
    dense = jnp.einsum("kna,knb,knxy->kaxby", row_hot, col_hot, triple_blocks.astype(jnp.float32))
    dense = dense.reshape(term_count, total_rows, CLASSES // PAIR, groups // CLASSES, PAIR, local_rows)
    dense = dense.transpose(0, 1, 2, 4, 3, 5).reshape(term_count, total_rows, total_rows)
    dense = dense.astype(jnp.bfloat16)
    summed = image_scatter(stiff_offsets, extended, stiff_blocks, dense, local_rows)
    return summed.reshape(local_rows, load_count, cell_count)


def solution(mesh):
    return jax.shard_map(
        per_device,
        mesh=mesh,
        in_specs=(
            P("term", None, "space"),
            P("term", "space", None, None, None),
            P("term", "space", None),
            P("term", None, None, None),
            P("term", None, None),
        ),
        out_specs=P("term", None, "space"),
        check_vma=False,
    )
```

```python
import jax
import jax.numpy as jnp
from jax import lax
from jax.experimental import pallas as pl
from jax.experimental.pallas import tpu as pltpu
from jax.sharding import PartitionSpec as P

MESH_ID = pl.DeviceIdType.MESH


CLASSES = 4
PAIR = 2


def gather_kernel(block_ref, out_ref, local_sem, send_near, recv_near, send_far, recv_far):
    count = out_ref.shape[0]
    chunk = count // CLASSES
    row, stride, lane, far_peer, near_peer = scatter_peers(chunk, CLASSES)
    barrier = pltpu.get_barrier_semaphore()

    def greet_far(step, carry):
        pl.semaphore_signal(barrier, 1, device_id=(row, far_peer(step)), device_id_type=MESH_ID)
        return carry

    def greet_near(step, carry):
        pl.semaphore_signal(barrier, 1, device_id=(row, near_peer(step)), device_id_type=MESH_ID)
        return carry

    lax.fori_loop(1, chunk, greet_far, 0)
    lax.fori_loop(1, CLASSES, greet_near, 0)
    pl.semaphore_wait(barrier, chunk + CLASSES - 2)

    mine = lane * chunk + stride
    local = pltpu.make_async_copy(block_ref, out_ref.at[mine], local_sem)
    local.start()

    def far_out(step):
        return pltpu.make_async_remote_copy(
            block_ref, out_ref.at[mine], send_far.at[step], recv_far.at[stride],
            device_id=(row, far_peer(step)), device_id_type=MESH_ID,
        )

    def far_in(step):
        source = lax.rem(stride + chunk - step, chunk)
        return pltpu.make_async_remote_copy(
            block_ref, out_ref.at[lane * chunk + source], send_far.at[step], recv_far.at[source],
            device_id=(row, term_device(lane, source, chunk)), device_id_type=MESH_ID,
        )

    def near_out(held, step):
        slot = out_ref.at[lane * chunk + held]
        return pltpu.make_async_remote_copy(
            slot, slot, send_near.at[held, step], recv_near.at[held, lane],
            device_id=(row, near_peer(step)), device_id_type=MESH_ID,
        )

    def near_in(held, step):
        source = lax.rem(lane + CLASSES - step, CLASSES)
        slot = out_ref.at[source * chunk + held]
        return pltpu.make_async_remote_copy(
            slot, slot, send_near.at[held, step], recv_near.at[held, source],
            device_id=(row, term_device(source, stride, chunk)), device_id_type=MESH_ID,
        )

    def forward(held):
        for step in range(1, CLASSES):
            near_out(held, step).start()

    def far_start(step, carry):
        far_out(step).start()
        return carry

    def far_finish(step, carry):
        far_out(step).wait_send()
        far_in(step).wait_recv()
        forward(lax.rem(stride + chunk - step, chunk))
        return carry

    lax.fori_loop(1, chunk, far_start, 0)
    local.wait()
    forward(stride)
    lax.fori_loop(1, chunk, far_finish, 0)

    def near_finish(held, carry):
        for step in range(1, CLASSES):
            near_out(held, step).wait_send()
            near_in(held, step).wait_recv()
        return carry

    lax.fori_loop(0, chunk, near_finish, 0)


def gather_term(block):
    count = lax.axis_size("term")
    return pl.pallas_call(
        gather_kernel,
        out_shape=jax.ShapeDtypeStruct((count,) + block.shape, block.dtype),
        in_specs=[pl.BlockSpec(memory_space=pltpu.VMEM)],
        out_specs=pl.BlockSpec(memory_space=pltpu.VMEM),
        scratch_shapes=[
            pltpu.SemaphoreType.DMA(()),
            pltpu.SemaphoreType.DMA((count // CLASSES, CLASSES)),
            pltpu.SemaphoreType.DMA((count // CLASSES, CLASSES)),
            pltpu.SemaphoreType.DMA((count // CLASSES,)),
            pltpu.SemaphoreType.DMA((count // CLASSES,)),
        ],
        compiler_params=pltpu.CompilerParams(collective_id=0, has_side_effects=True),
    )(block)


def term_device(lane, stride, chunk):
    return (lane // PAIR) * (chunk * PAIR) + stride * PAIR + lane % PAIR


def scatter_peers(chunk, classes):
    me = lax.axis_index("term")
    row = lax.axis_index("space")
    ring = chunk * PAIR
    stride = lax.rem(me, ring) // PAIR
    lane = (me // ring) * PAIR + lax.rem(me, PAIR)

    def far_peer(step):
        return term_device(lane, lax.rem(stride + step, chunk), chunk)

    def near_peer(step):
        return term_device(lax.rem(lane + step, classes), stride, chunk)

    return row, stride, lane, far_peer, near_peer


def scatter_greet(chunk, classes):
    row, stride, lane, far_peer, near_peer = scatter_peers(chunk, classes)
    barrier = pltpu.get_barrier_semaphore()

    def greet_far(step, carry):
        pl.semaphore_signal(barrier, 1, device_id=(row, far_peer(step)), device_id_type=MESH_ID)
        return carry

    def greet_near(step, carry):
        pl.semaphore_signal(barrier, 1, device_id=(row, near_peer(step)), device_id_type=MESH_ID)
        return carry

    lax.fori_loop(1, chunk, greet_far, 0)
    lax.fori_loop(1, classes, greet_near, 0)


def image_kernel(offs_ref, panel_ref, stiff_ref, triple_ref, out_ref, total_ref, far_src,
                 near_slots, class_sum, far_slots, send_near, recv_near, send_far, recv_far):
    block = pl.program_id(0)
    term = pl.program_id(1)
    band = stiff_ref.shape[2]
    width = stiff_ref.shape[-1]
    sides, chunk, _, local_rows, columns = total_ref.shape
    classes = sides * PAIR
    rows = triple_ref.shape[1]
    loads = panel_ref.shape[1] // rows
    block_rows = columns // (loads * width)
    term_count = pl.num_programs(1)
    rim = (panel_ref.shape[0] - block_rows) // 2
    half = loads * width
    row, stride, lane, far_peer, near_peer = scatter_peers(chunk, classes)

    @pl.when((term == 0) & (block == 0))
    def _():
        scatter_greet(chunk, classes)
        total_ref[...] = jnp.zeros_like(total_ref)

    total = jnp.zeros((loads * rows, width), jnp.float32)
    for slot in range(band):
        place = block + rim + offs_ref[(term * block_rows + block) * band + slot]
        total += lax.dot_general(
            panel_ref[place], stiff_ref[0, 0, slot],
            (((1,), (1,)), ((), ())), preferred_element_type=jnp.float32,
        )
    image = total.astype(jnp.bfloat16)
    for load in range(loads):
        column = pl.multiple_of((block * loads + load) * width, width)
        product = jnp.dot(
            triple_ref[0], image[load * rows:(load + 1) * rows], preferred_element_type=jnp.float32
        )
        total_ref[:, :, :, :, pl.ds(column, width)] += product.reshape(
            sides, chunk, PAIR, local_rows, width
        )

    def near_copy(step, part, inbound):
        cols = pl.ds(pl.multiple_of(part * half, half), half)
        if inbound:
            source = lax.rem(lane + classes - step, classes)
            return pltpu.make_async_remote_copy(
                total_ref.at[source // PAIR, :, source % PAIR, :, cols],
                near_slots.at[source, :, :, cols], send_near.at[part, step], recv_near.at[part, source],
                device_id=(row, term_device(source, stride, chunk)), device_id_type=MESH_ID,
            )
        target = lax.rem(lane + step, classes)
        return pltpu.make_async_remote_copy(
            total_ref.at[target // PAIR, :, target % PAIR, :, cols],
            near_slots.at[lane, :, :, cols], send_near.at[part, step], recv_near.at[part, lane],
            device_id=(row, near_peer(step)), device_id_type=MESH_ID,
        )

    @pl.when(term == term_count - 1)
    def _():
        @pl.when(block == 0)
        def _():
            pl.semaphore_wait(pltpu.get_barrier_semaphore(), chunk + classes - 2)

        def near_start(step, carry):
            near_copy(step, block, False).start()
            return carry

        lax.fori_loop(1, classes, near_start, 0)

    @pl.when((term == term_count - 1) & (block == block_rows - 1))
    def _():
        for part in range(block_rows):
            cols = pl.ds(part * half, half)

            def near_finish(step, total):
                near_copy(step, part, False).wait_send()
                near_copy(step, part, True).wait_recv()
                source = lax.rem(lane + classes - step, classes)
                return total + near_slots[source, :, :, cols]

            own = total_ref[lane // PAIR, :, lane % PAIR, :, cols]
            class_sum[:, :, cols] = lax.fori_loop(1, classes, near_finish, own)

        far_src[...] = class_sum[...].astype(far_src.dtype)

        def far_out(step):
            target = lax.rem(stride + step, chunk)
            return pltpu.make_async_remote_copy(
                far_src.at[target], far_slots.at[stride], send_far.at[step], recv_far.at[stride],
                device_id=(row, far_peer(step)), device_id_type=MESH_ID,
            )

        def far_in(step):
            source = lax.rem(stride + chunk - step, chunk)
            return pltpu.make_async_remote_copy(
                far_src.at[source], far_slots.at[source], send_far.at[step], recv_far.at[source],
                device_id=(row, term_device(lane, source, chunk)), device_id_type=MESH_ID,
            )

        def far_start(step, carry):
            far_out(step).start()
            return carry

        def far_finish(step, total):
            far_out(step).wait_send()
            far_in(step).wait_recv()
            source = lax.rem(stride + chunk - step, chunk)
            return total + far_slots[source].astype(jnp.float32)

        lax.fori_loop(1, chunk, far_start, 0)
        summed = lax.fori_loop(1, chunk, far_finish, class_sum[stride])
        for part in range(block_rows):
            for load in range(loads):
                source = (part * loads + load) * width
                target = (load * block_rows + part) * width
                out_ref[:, target:target + width] = summed[:, source:source + width]


def image_scatter(offsets, panel, stiff_blocks, dense, local_rows):
    term_count, block_rows, band, width, _ = stiff_blocks.shape
    places, stacked, _ = panel.shape
    rows = dense.shape[1]
    columns = stacked // rows * block_rows * width
    classes = CLASSES
    chunk = rows // (classes * local_rows)
    shape = (classes // PAIR, chunk, PAIR, local_rows, columns)
    return pl.pallas_call(
        image_kernel,
        out_shape=jax.ShapeDtypeStruct((local_rows, columns), jnp.float32),
        grid_spec=pltpu.PrefetchScalarGridSpec(
            num_scalar_prefetch=1,
            grid=(block_rows, term_count),
            in_specs=[
                pl.BlockSpec((places, stacked, width), lambda b, k, offs: (0, 0, 0)),
                pl.BlockSpec((1, 1, band, width, width), lambda b, k, offs: (k, b, 0, 0, 0)),
                pl.BlockSpec((1, rows, rows), lambda b, k, offs: (k, 0, 0)),
            ],
            out_specs=pl.BlockSpec((local_rows, columns), lambda b, k, offs: (0, 0)),
            scratch_shapes=[
                pltpu.VMEM(shape, jnp.float32),
                pltpu.VMEM((chunk, local_rows, columns), jnp.bfloat16),
                pltpu.VMEM((classes, chunk, local_rows, columns), jnp.float32),
                pltpu.VMEM((chunk, local_rows, columns), jnp.float32),
                pltpu.VMEM((chunk, local_rows, columns), jnp.bfloat16),
                pltpu.SemaphoreType.DMA((block_rows, classes)),
                pltpu.SemaphoreType.DMA((block_rows, classes)),
                pltpu.SemaphoreType.DMA((chunk,)),
                pltpu.SemaphoreType.DMA((chunk,)),
            ],
        ),
        compiler_params=pltpu.CompilerParams(collective_id=1, has_side_effects=True),
    )(offsets.reshape(-1), panel, stiff_blocks, dense)


def with_halo(block, sides, width):
    for axis, dim in sides:
        count = lax.axis_size(axis)
        forward = [(i, i + 1) for i in range(count - 1)]
        backward = [(target, source) for source, target in forward]
        low = lax.ppermute(
            lax.slice_in_dim(block, block.shape[dim] - width, None, axis=dim), axis, forward
        )
        high = lax.ppermute(lax.slice_in_dim(block, 0, width, axis=dim), axis, backward)
        block = jnp.concatenate([low, block, high], axis=dim)
    return block


def per_device(chaos_field, stiff_blocks, stiff_offsets, triple_blocks, triple_pattern):
    local_rows = chaos_field.shape[0]
    load_count = chaos_field.shape[1]
    cell_count = chaos_field.shape[2]
    term_count = stiff_blocks.shape[0]
    block_width = stiff_blocks.shape[3]
    block_rows = cell_count // block_width
    groups = lax.axis_size("term")
    total_rows = local_rows * groups
    rim_cells = 2 * block_width
    gathered = gather_term(chaos_field.reshape(local_rows * load_count, cell_count))
    panel = gathered.reshape(groups, local_rows, load_count, block_rows, block_width)
    panel = panel.transpose(3, 2, 0, 1, 4).reshape(block_rows, load_count, total_rows, block_width)
    extended = with_halo(panel, (("space", 0),), rim_cells // block_width)
    extended = extended.reshape(block_rows + 4, load_count * total_rows, block_width)
    block_size = triple_blocks.shape[2]
    levels = jnp.arange(total_rows // block_size, dtype=jnp.int32)
    row_hot = (triple_pattern[:, :, 0:1] == levels).astype(jnp.float32)
    col_hot = (triple_pattern[:, :, 1:2] == levels).astype(jnp.float32)
    dense = jnp.einsum("kna,knb,knxy->kaxby", row_hot, col_hot, triple_blocks.astype(jnp.float32))
    dense = dense.reshape(term_count, total_rows, CLASSES // PAIR, groups // CLASSES, PAIR, local_rows)
    dense = dense.transpose(0, 1, 2, 4, 3, 5).reshape(term_count, total_rows, total_rows)
    dense = dense.astype(jnp.bfloat16)
    summed = image_scatter(stiff_offsets, extended, stiff_blocks, dense, local_rows)
    return summed.reshape(local_rows, load_count, cell_count)


def solution(mesh):
    return jax.shard_map(
        per_device,
        mesh=mesh,
        in_specs=(
            P("term", None, "space"),
            P("term", "space", None, None, None),
            P("term", "space", None),
            P("term", None, None, None),
            P("term", None, None),
        ),
        out_specs=P("term", None, "space"),
        check_vma=False,
    )
```

```python
import jax
import jax.numpy as jnp
from jax import lax
from jax.experimental import pallas as pl
from jax.experimental.pallas import tpu as pltpu
from jax.sharding import PartitionSpec as P

MESH_ID = pl.DeviceIdType.MESH


CLASSES = 4
PAIR = 2


def gather_kernel(block_ref, out_ref, local_sem, send_near, recv_near, send_far, recv_far):
    count = out_ref.shape[0]
    chunk = count // CLASSES
    row, stride, lane, far_peer, near_peer = scatter_peers(chunk, CLASSES)
    barrier = pltpu.get_barrier_semaphore()

    def greet_far(step, carry):
        pl.semaphore_signal(barrier, 1, device_id=(row, far_peer(step)), device_id_type=MESH_ID)
        return carry

    def greet_near(step, carry):
        pl.semaphore_signal(barrier, 1, device_id=(row, near_peer(step)), device_id_type=MESH_ID)
        return carry

    lax.fori_loop(1, chunk, greet_far, 0)
    lax.fori_loop(1, CLASSES, greet_near, 0)
    pl.semaphore_wait(barrier, chunk + CLASSES - 2)

    mine = lane * chunk + stride
    local = pltpu.make_async_copy(block_ref, out_ref.at[mine], local_sem)
    local.start()

    def far_out(step):
        return pltpu.make_async_remote_copy(
            block_ref, out_ref.at[mine], send_far.at[step], recv_far.at[stride],
            device_id=(row, far_peer(step)), device_id_type=MESH_ID,
        )

    def far_in(step):
        source = lax.rem(stride + chunk - step, chunk)
        return pltpu.make_async_remote_copy(
            block_ref, out_ref.at[lane * chunk + source], send_far.at[step], recv_far.at[source],
            device_id=(row, term_device(lane, source, chunk)), device_id_type=MESH_ID,
        )

    def far_start(step, carry):
        far_out(step).start()
        return carry

    def far_finish(step, carry):
        far_out(step).wait_send()
        far_in(step).wait_recv()
        return carry

    lax.fori_loop(1, chunk, far_start, 0)
    local.wait()
    lax.fori_loop(1, chunk, far_finish, 0)

    own = out_ref.at[pl.ds(lane * chunk, chunk)]

    def near_out(step):
        return pltpu.make_async_remote_copy(
            own, own, send_near.at[step], recv_near.at[lane],
            device_id=(row, near_peer(step)), device_id_type=MESH_ID,
        )

    def near_in(step):
        source = lax.rem(lane + CLASSES - step, CLASSES)
        theirs = out_ref.at[pl.ds(source * chunk, chunk)]
        return pltpu.make_async_remote_copy(
            theirs, theirs, send_near.at[step], recv_near.at[source],
            device_id=(row, term_device(source, stride, chunk)), device_id_type=MESH_ID,
        )

    def near_start(step, carry):
        near_out(step).start()
        return carry

    def near_finish(step, carry):
        near_out(step).wait_send()
        near_in(step).wait_recv()
        return carry

    lax.fori_loop(1, CLASSES, near_start, 0)
    lax.fori_loop(1, CLASSES, near_finish, 0)


def gather_term(block):
    count = lax.axis_size("term")
    return pl.pallas_call(
        gather_kernel,
        out_shape=jax.ShapeDtypeStruct((count,) + block.shape, block.dtype),
        in_specs=[pl.BlockSpec(memory_space=pltpu.VMEM)],
        out_specs=pl.BlockSpec(memory_space=pltpu.VMEM),
        scratch_shapes=[
            pltpu.SemaphoreType.DMA(()),
            pltpu.SemaphoreType.DMA((CLASSES,)),
            pltpu.SemaphoreType.DMA((CLASSES,)),
            pltpu.SemaphoreType.DMA((count // CLASSES,)),
            pltpu.SemaphoreType.DMA((count // CLASSES,)),
        ],
        compiler_params=pltpu.CompilerParams(collective_id=0, has_side_effects=True),
    )(block)


def term_device(lane, stride, chunk):
    return (lane // PAIR) * (chunk * PAIR) + stride * PAIR + lane % PAIR


def scatter_peers(chunk, classes):
    me = lax.axis_index("term")
    row = lax.axis_index("space")
    ring = chunk * PAIR
    stride = lax.rem(me, ring) // PAIR
    lane = (me // ring) * PAIR + lax.rem(me, PAIR)

    def far_peer(step):
        return term_device(lane, lax.rem(stride + step, chunk), chunk)

    def near_peer(step):
        return term_device(lax.rem(lane + step, classes), stride, chunk)

    return row, stride, lane, far_peer, near_peer


def scatter_greet(chunk, classes):
    row, stride, lane, far_peer, near_peer = scatter_peers(chunk, classes)
    barrier = pltpu.get_barrier_semaphore()

    def greet_far(step, carry):
        pl.semaphore_signal(barrier, 1, device_id=(row, far_peer(step)), device_id_type=MESH_ID)
        return carry

    def greet_near(step, carry):
        pl.semaphore_signal(barrier, 1, device_id=(row, near_peer(step)), device_id_type=MESH_ID)
        return carry

    lax.fori_loop(1, chunk, greet_far, 0)
    lax.fori_loop(1, classes, greet_near, 0)


def image_kernel(offs_ref, panel_ref, stiff_ref, triple_ref, out_ref, total_ref, far_src,
                 near_slots, class_sum, far_slots, send_near, recv_near, send_far, recv_far):
    block = pl.program_id(0)
    term = pl.program_id(1)
    band = stiff_ref.shape[2]
    width = stiff_ref.shape[-1]
    sides, chunk, _, local_rows, columns = total_ref.shape
    classes = sides * PAIR
    rows = triple_ref.shape[1]
    loads = panel_ref.shape[1] // rows
    block_rows = columns // (loads * width)
    term_count = pl.num_programs(1)
    rim = (panel_ref.shape[0] - block_rows) // 2
    half = loads * width
    row, stride, lane, far_peer, near_peer = scatter_peers(chunk, classes)

    @pl.when((term == 0) & (block == 0))
    def _():
        scatter_greet(chunk, classes)
        total_ref[...] = jnp.zeros_like(total_ref)

    total = jnp.zeros((loads * rows, width), jnp.float32)
    for slot in range(band):
        place = block + rim + offs_ref[(term * block_rows + block) * band + slot]
        total += lax.dot_general(
            panel_ref[place], stiff_ref[0, 0, slot],
            (((1,), (1,)), ((), ())), preferred_element_type=jnp.float32,
        )
    image = total.astype(jnp.bfloat16)
    for load in range(loads):
        column = pl.multiple_of((block * loads + load) * width, width)
        product = jnp.dot(
            triple_ref[0], image[load * rows:(load + 1) * rows], preferred_element_type=jnp.float32
        )
        total_ref[:, :, :, :, pl.ds(column, width)] += product.reshape(
            sides, chunk, PAIR, local_rows, width
        )

    def near_copy(step, part, inbound):
        cols = pl.ds(pl.multiple_of(part * half, half), half)
        if inbound:
            source = lax.rem(lane + classes - step, classes)
            return pltpu.make_async_remote_copy(
                total_ref.at[source // PAIR, :, source % PAIR, :, cols],
                near_slots.at[source, :, :, cols], send_near.at[part, step], recv_near.at[part, source],
                device_id=(row, term_device(source, stride, chunk)), device_id_type=MESH_ID,
            )
        target = lax.rem(lane + step, classes)
        return pltpu.make_async_remote_copy(
            total_ref.at[target // PAIR, :, target % PAIR, :, cols],
            near_slots.at[lane, :, :, cols], send_near.at[part, step], recv_near.at[part, lane],
            device_id=(row, near_peer(step)), device_id_type=MESH_ID,
        )

    @pl.when(term == term_count - 1)
    def _():
        @pl.when(block == 0)
        def _():
            pl.semaphore_wait(pltpu.get_barrier_semaphore(), chunk + classes - 2)

        def near_start(step, carry):
            near_copy(step, block, False).start()
            return carry

        lax.fori_loop(1, classes, near_start, 0)

    @pl.when((term == term_count - 1) & (block == block_rows - 1))
    def _():
        for part in range(block_rows):
            cols = pl.ds(part * half, half)

            def near_finish(step, total):
                near_copy(step, part, False).wait_send()
                near_copy(step, part, True).wait_recv()
                source = lax.rem(lane + classes - step, classes)
                return total + near_slots[source, :, :, cols]

            own = total_ref[lane // PAIR, :, lane % PAIR, :, cols]
            class_sum[:, :, cols] = lax.fori_loop(1, classes, near_finish, own)

        far_src[...] = class_sum[...].astype(far_src.dtype)

        def far_out(step):
            target = lax.rem(stride + step, chunk)
            return pltpu.make_async_remote_copy(
                far_src.at[target], far_slots.at[stride], send_far.at[step], recv_far.at[stride],
                device_id=(row, far_peer(step)), device_id_type=MESH_ID,
            )

        def far_in(step):
            source = lax.rem(stride + chunk - step, chunk)
            return pltpu.make_async_remote_copy(
                far_src.at[source], far_slots.at[source], send_far.at[step], recv_far.at[source],
                device_id=(row, term_device(lane, source, chunk)), device_id_type=MESH_ID,
            )

        def far_start(step, carry):
            far_out(step).start()
            return carry

        def far_finish(step, total):
            far_out(step).wait_send()
            far_in(step).wait_recv()
            source = lax.rem(stride + chunk - step, chunk)
            return total + far_slots[source].astype(jnp.float32)

        lax.fori_loop(1, chunk, far_start, 0)
        summed = lax.fori_loop(1, chunk, far_finish, class_sum[stride])
        for part in range(block_rows):
            for load in range(loads):
                source = (part * loads + load) * width
                out_ref[:, load, part * width:(part + 1) * width] = summed[:, source:source + width]


def image_scatter(offsets, panel, stiff_blocks, dense, local_rows):
    term_count, block_rows, band, width, _ = stiff_blocks.shape
    places, stacked, _ = panel.shape
    rows = dense.shape[1]
    columns = stacked // rows * block_rows * width
    classes = CLASSES
    chunk = rows // (classes * local_rows)
    shape = (classes // PAIR, chunk, PAIR, local_rows, columns)
    return pl.pallas_call(
        image_kernel,
        out_shape=jax.ShapeDtypeStruct((local_rows, columns // (block_rows * width), block_rows * width), jnp.float32),
        grid_spec=pltpu.PrefetchScalarGridSpec(
            num_scalar_prefetch=1,
            grid=(block_rows, term_count),
            in_specs=[
                pl.BlockSpec((places, stacked, width), lambda b, k, offs: (0, 0, 0)),
                pl.BlockSpec((1, 1, band, width, width), lambda b, k, offs: (k, b, 0, 0, 0)),
                pl.BlockSpec((1, rows, rows), lambda b, k, offs: (k, 0, 0)),
            ],
            out_specs=pl.BlockSpec(
                (local_rows, columns // (block_rows * width), block_rows * width), lambda b, k, offs: (0, 0, 0)
            ),
            scratch_shapes=[
                pltpu.VMEM(shape, jnp.float32),
                pltpu.VMEM((chunk, local_rows, columns), jnp.bfloat16),
                pltpu.VMEM((classes, chunk, local_rows, columns), jnp.float32),
                pltpu.VMEM((chunk, local_rows, columns), jnp.float32),
                pltpu.VMEM((chunk, local_rows, columns), jnp.bfloat16),
                pltpu.SemaphoreType.DMA((block_rows, classes)),
                pltpu.SemaphoreType.DMA((block_rows, classes)),
                pltpu.SemaphoreType.DMA((chunk,)),
                pltpu.SemaphoreType.DMA((chunk,)),
            ],
        ),
        compiler_params=pltpu.CompilerParams(collective_id=1, has_side_effects=True),
    )(offsets.reshape(-1), panel, stiff_blocks, dense)


def with_halo(block, sides, width):
    for axis, dim in sides:
        count = lax.axis_size(axis)
        forward = [(i, i + 1) for i in range(count - 1)]
        backward = [(target, source) for source, target in forward]
        low = lax.ppermute(
            lax.slice_in_dim(block, block.shape[dim] - width, None, axis=dim), axis, forward
        )
        high = lax.ppermute(lax.slice_in_dim(block, 0, width, axis=dim), axis, backward)
        block = jnp.concatenate([low, block, high], axis=dim)
    return block


def per_device(chaos_field, stiff_blocks, stiff_offsets, triple_blocks, triple_pattern):
    local_rows = chaos_field.shape[0]
    load_count = chaos_field.shape[1]
    cell_count = chaos_field.shape[2]
    term_count = stiff_blocks.shape[0]
    block_width = stiff_blocks.shape[3]
    block_rows = cell_count // block_width
    groups = lax.axis_size("term")
    total_rows = local_rows * groups
    rim_cells = 2 * block_width
    gathered = gather_term(chaos_field.reshape(local_rows * load_count, cell_count))
    panel = gathered.reshape(groups, local_rows, load_count, block_rows, block_width)
    panel = panel.transpose(3, 2, 0, 1, 4).reshape(block_rows, load_count, total_rows, block_width)
    extended = with_halo(panel, (("space", 0),), rim_cells // block_width)
    extended = extended.reshape(block_rows + 4, load_count * total_rows, block_width)
    block_size = triple_blocks.shape[2]
    levels = jnp.arange(total_rows // block_size, dtype=jnp.int32)
    row_hot = (triple_pattern[:, :, 0:1] == levels).astype(jnp.float32)
    col_hot = (triple_pattern[:, :, 1:2] == levels).astype(jnp.float32)
    dense = jnp.einsum("kna,knb,knxy->kaxby", row_hot, col_hot, triple_blocks.astype(jnp.float32))
    dense = dense.reshape(term_count, total_rows, CLASSES // PAIR, groups // CLASSES, PAIR, local_rows)
    dense = dense.transpose(0, 1, 2, 4, 3, 5).reshape(term_count, total_rows, total_rows)
    dense = dense.astype(jnp.bfloat16)
    summed = image_scatter(stiff_offsets, extended, stiff_blocks, dense, local_rows)
    return summed.reshape(local_rows, load_count, cell_count)


def solution(mesh):
    return jax.shard_map(
        per_device,
        mesh=mesh,
        in_specs=(
            P("term", None, "space"),
            P("term", "space", None, None, None),
            P("term", "space", None),
            P("term", None, None, None),
            P("term", None, None),
        ),
        out_specs=P("term", None, "space"),
        check_vma=False,
    )
```

```python
import jax
import jax.numpy as jnp
from jax import lax
from jax.experimental import pallas as pl
from jax.experimental.pallas import tpu as pltpu
from jax.sharding import PartitionSpec as P

MESH_ID = pl.DeviceIdType.MESH


CLASSES = 4
PAIR = 2


def gather_kernel(block_ref, out_ref, local_sem, send_near, recv_near, send_far, recv_far):
    count = out_ref.shape[0]
    chunk = count // CLASSES
    row, stride, lane, far_peer, near_peer = scatter_peers(chunk, CLASSES)
    barrier = pltpu.get_barrier_semaphore()

    def greet_far(step, carry):
        pl.semaphore_signal(barrier, 1, device_id=(row, far_peer(step)), device_id_type=MESH_ID)
        return carry

    def greet_near(step, carry):
        pl.semaphore_signal(barrier, 1, device_id=(row, near_peer(step)), device_id_type=MESH_ID)
        return carry

    lax.fori_loop(1, chunk, greet_far, 0)
    lax.fori_loop(1, CLASSES, greet_near, 0)
    pl.semaphore_wait(barrier, chunk + CLASSES - 2)

    mine = lane * chunk + stride
    local = pltpu.make_async_copy(block_ref, out_ref.at[mine], local_sem)
    local.start()

    def far_out(step):
        return pltpu.make_async_remote_copy(
            block_ref, out_ref.at[mine], send_far.at[step], recv_far.at[stride],
            device_id=(row, far_peer(step)), device_id_type=MESH_ID,
        )

    def far_in(step):
        source = lax.rem(stride + chunk - step, chunk)
        return pltpu.make_async_remote_copy(
            block_ref, out_ref.at[lane * chunk + source], send_far.at[step], recv_far.at[source],
            device_id=(row, term_device(lane, source, chunk)), device_id_type=MESH_ID,
        )

    def far_start(step, carry):
        far_out(step).start()
        return carry

    def far_finish(step, carry):
        far_out(step).wait_send()
        far_in(step).wait_recv()
        return carry

    lax.fori_loop(1, chunk, far_start, 0)
    local.wait()
    lax.fori_loop(1, chunk, far_finish, 0)

    own = out_ref.at[pl.ds(lane * chunk, chunk)]

    def near_out(step):
        return pltpu.make_async_remote_copy(
            own, own, send_near.at[step], recv_near.at[lane],
            device_id=(row, near_peer(step)), device_id_type=MESH_ID,
        )

    def near_in(step):
        source = lax.rem(lane + CLASSES - step, CLASSES)
        theirs = out_ref.at[pl.ds(source * chunk, chunk)]
        return pltpu.make_async_remote_copy(
            theirs, theirs, send_near.at[step], recv_near.at[source],
            device_id=(row, term_device(source, stride, chunk)), device_id_type=MESH_ID,
        )

    def near_start(step, carry):
        near_out(step).start()
        return carry

    def near_finish(step, carry):
        near_out(step).wait_send()
        near_in(step).wait_recv()
        return carry

    lax.fori_loop(1, CLASSES, near_start, 0)
    lax.fori_loop(1, CLASSES, near_finish, 0)


def gather_term(block):
    count = lax.axis_size("term")
    return pl.pallas_call(
        gather_kernel,
        out_shape=jax.ShapeDtypeStruct((count,) + block.shape, block.dtype),
        in_specs=[pl.BlockSpec(memory_space=pltpu.VMEM)],
        out_specs=pl.BlockSpec(memory_space=pltpu.VMEM),
        scratch_shapes=[
            pltpu.SemaphoreType.DMA(()),
            pltpu.SemaphoreType.DMA((CLASSES,)),
            pltpu.SemaphoreType.DMA((CLASSES,)),
            pltpu.SemaphoreType.DMA((count // CLASSES,)),
            pltpu.SemaphoreType.DMA((count // CLASSES,)),
        ],
        compiler_params=pltpu.CompilerParams(collective_id=0, has_side_effects=True),
    )(block)


def term_device(lane, stride, chunk):
    return (lane // PAIR) * (chunk * PAIR) + stride * PAIR + lane % PAIR


def scatter_peers(chunk, classes):
    me = lax.axis_index("term")
    row = lax.axis_index("space")
    ring = chunk * PAIR
    stride = lax.rem(me, ring) // PAIR
    lane = (me // ring) * PAIR + lax.rem(me, PAIR)

    def far_peer(step):
        return term_device(lane, lax.rem(stride + step, chunk), chunk)

    def near_peer(step):
        return term_device(lax.rem(lane + step, classes), stride, chunk)

    return row, stride, lane, far_peer, near_peer


def scatter_greet(chunk, classes):
    row, stride, lane, far_peer, near_peer = scatter_peers(chunk, classes)
    barrier = pltpu.get_barrier_semaphore()

    def greet_far(step, carry):
        pl.semaphore_signal(barrier, 1, device_id=(row, far_peer(step)), device_id_type=MESH_ID)
        return carry

    def greet_near(step, carry):
        pl.semaphore_signal(barrier, 1, device_id=(row, near_peer(step)), device_id_type=MESH_ID)
        return carry

    lax.fori_loop(1, chunk, greet_far, 0)
    lax.fori_loop(1, classes, greet_near, 0)


def image_kernel(offs_ref, panel_ref, stiff_ref, triple_ref, out_ref, total_ref, far_src,
                 near_slots, class_sum, far_slots, send_near, recv_near, send_far, recv_far):
    block = pl.program_id(0)
    term = pl.program_id(1)
    band = stiff_ref.shape[2]
    width = stiff_ref.shape[-1]
    sides, chunk, _, local_rows, columns = total_ref.shape
    classes = sides * PAIR
    rows = triple_ref.shape[1]
    loads = panel_ref.shape[1] // rows
    block_rows = columns // (loads * width)
    term_count = pl.num_programs(1)
    rim = (panel_ref.shape[0] - block_rows) // 2
    half = loads * width
    row, stride, lane, far_peer, near_peer = scatter_peers(chunk, classes)

    @pl.when((term == 0) & (block == 0))
    def _():
        scatter_greet(chunk, classes)
        total_ref[...] = jnp.zeros_like(total_ref)

    total = jnp.zeros((loads * rows, width), jnp.float32)
    for slot in range(band):
        place = block + rim + offs_ref[(term * block_rows + block) * band + slot]
        total += lax.dot_general(
            panel_ref[place], stiff_ref[0, 0, slot],
            (((1,), (1,)), ((), ())), preferred_element_type=jnp.float32,
        )
    image = total.astype(jnp.bfloat16)
    for load in range(loads):
        column = pl.multiple_of((block * loads + load) * width, width)
        product = jnp.dot(
            triple_ref[0], image[load * rows:(load + 1) * rows], preferred_element_type=jnp.float32
        )
        total_ref[:, :, :, :, pl.ds(column, width)] += product.reshape(
            sides, chunk, PAIR, local_rows, width
        )

    def near_copy(step, part, inbound):
        cols = pl.ds(pl.multiple_of(part * half, half), half)
        if inbound:
            source = lax.rem(lane + classes - step, classes)
            return pltpu.make_async_remote_copy(
                total_ref.at[source // PAIR, :, source % PAIR, :, cols],
                near_slots.at[source, :, :, cols], send_near.at[part, step], recv_near.at[part, source],
                device_id=(row, term_device(source, stride, chunk)), device_id_type=MESH_ID,
            )
        target = lax.rem(lane + step, classes)
        return pltpu.make_async_remote_copy(
            total_ref.at[target // PAIR, :, target % PAIR, :, cols],
            near_slots.at[lane, :, :, cols], send_near.at[part, step], recv_near.at[part, lane],
            device_id=(row, near_peer(step)), device_id_type=MESH_ID,
        )

    @pl.when(term == term_count - 1)
    def _():
        @pl.when(block == 0)
        def _():
            pl.semaphore_wait(pltpu.get_barrier_semaphore(), chunk + classes - 2)

        def near_start(step, carry):
            near_copy(step, block, False).start()
            return carry

        lax.fori_loop(1, classes, near_start, 0)

    @pl.when((term == term_count - 1) & (block == block_rows - 1))
    def _():
        def far_copy(step, part, inbound):
            cols = pl.ds(part * half, half)
            if inbound:
                source = lax.rem(stride + chunk - step, chunk)
                return pltpu.make_async_remote_copy(
                    far_src.at[source, :, cols], far_slots.at[source, :, cols],
                    send_far.at[part, step], recv_far.at[part, source],
                    device_id=(row, term_device(lane, source, chunk)), device_id_type=MESH_ID,
                )
            target = lax.rem(stride + step, chunk)
            return pltpu.make_async_remote_copy(
                far_src.at[target, :, cols], far_slots.at[stride, :, cols],
                send_far.at[part, step], recv_far.at[part, stride],
                device_id=(row, far_peer(step)), device_id_type=MESH_ID,
            )

        for part in range(block_rows):
            cols = pl.ds(part * half, half)

            def near_finish(step, total):
                near_copy(step, part, False).wait_send()
                near_copy(step, part, True).wait_recv()
                source = lax.rem(lane + classes - step, classes)
                return total + near_slots[source, :, :, cols]

            own = total_ref[lane // PAIR, :, lane % PAIR, :, cols]
            part_sum = lax.fori_loop(1, classes, near_finish, own)
            class_sum[:, :, cols] = part_sum
            far_src[:, :, cols] = part_sum.astype(far_src.dtype)

            def far_start(step, carry):
                far_copy(step, part, False).start()
                return carry

            lax.fori_loop(1, chunk, far_start, 0)

        for part in range(block_rows):
            cols = pl.ds(part * half, half)

            def far_finish(step, total):
                far_copy(step, part, False).wait_send()
                far_copy(step, part, True).wait_recv()
                source = lax.rem(stride + chunk - step, chunk)
                return total + far_slots[source, :, cols].astype(jnp.float32)

            summed = lax.fori_loop(1, chunk, far_finish, class_sum[stride, :, cols])
            for load in range(loads):
                target = (load * block_rows + part) * width
                out_ref[:, target:target + width] = summed[:, load * width:(load + 1) * width]


def image_scatter(offsets, panel, stiff_blocks, dense, local_rows):
    term_count, block_rows, band, width, _ = stiff_blocks.shape
    places, stacked, _ = panel.shape
    rows = dense.shape[1]
    columns = stacked // rows * block_rows * width
    classes = CLASSES
    chunk = rows // (classes * local_rows)
    shape = (classes // PAIR, chunk, PAIR, local_rows, columns)
    return pl.pallas_call(
        image_kernel,
        out_shape=jax.ShapeDtypeStruct((local_rows, columns), jnp.float32),
        grid_spec=pltpu.PrefetchScalarGridSpec(
            num_scalar_prefetch=1,
            grid=(block_rows, term_count),
            in_specs=[
                pl.BlockSpec((places, stacked, width), lambda b, k, offs: (0, 0, 0)),
                pl.BlockSpec((1, 1, band, width, width), lambda b, k, offs: (k, b, 0, 0, 0)),
                pl.BlockSpec((1, rows, rows), lambda b, k, offs: (k, 0, 0)),
            ],
            out_specs=pl.BlockSpec((local_rows, columns), lambda b, k, offs: (0, 0)),
            scratch_shapes=[
                pltpu.VMEM(shape, jnp.float32),
                pltpu.VMEM((chunk, local_rows, columns), jnp.bfloat16),
                pltpu.VMEM((classes, chunk, local_rows, columns), jnp.float32),
                pltpu.VMEM((chunk, local_rows, columns), jnp.float32),
                pltpu.VMEM((chunk, local_rows, columns), jnp.bfloat16),
                pltpu.SemaphoreType.DMA((block_rows, classes)),
                pltpu.SemaphoreType.DMA((block_rows, classes)),
                pltpu.SemaphoreType.DMA((block_rows, chunk)),
                pltpu.SemaphoreType.DMA((block_rows, chunk)),
            ],
        ),
        compiler_params=pltpu.CompilerParams(collective_id=1, has_side_effects=True),
    )(offsets.reshape(-1), panel, stiff_blocks, dense)


def with_halo(block, sides, width):
    for axis, dim in sides:
        count = lax.axis_size(axis)
        forward = [(i, i + 1) for i in range(count - 1)]
        backward = [(target, source) for source, target in forward]
        low = lax.ppermute(
            lax.slice_in_dim(block, block.shape[dim] - width, None, axis=dim), axis, forward
        )
        high = lax.ppermute(lax.slice_in_dim(block, 0, width, axis=dim), axis, backward)
        block = jnp.concatenate([low, block, high], axis=dim)
    return block


def per_device(chaos_field, stiff_blocks, stiff_offsets, triple_blocks, triple_pattern):
    local_rows = chaos_field.shape[0]
    load_count = chaos_field.shape[1]
    cell_count = chaos_field.shape[2]
    term_count = stiff_blocks.shape[0]
    block_width = stiff_blocks.shape[3]
    block_rows = cell_count // block_width
    groups = lax.axis_size("term")
    total_rows = local_rows * groups
    rim_cells = 2 * block_width
    gathered = gather_term(chaos_field.reshape(local_rows * load_count, cell_count))
    panel = gathered.reshape(groups, local_rows, load_count, block_rows, block_width)
    panel = panel.transpose(3, 2, 0, 1, 4).reshape(block_rows, load_count, total_rows, block_width)
    extended = with_halo(panel, (("space", 0),), rim_cells // block_width)
    extended = extended.reshape(block_rows + 4, load_count * total_rows, block_width)
    block_size = triple_blocks.shape[2]
    levels = jnp.arange(total_rows // block_size, dtype=jnp.int32)
    row_hot = (triple_pattern[:, :, 0:1] == levels).astype(jnp.float32)
    col_hot = (triple_pattern[:, :, 1:2] == levels).astype(jnp.float32)
    dense = jnp.einsum("kna,knb,knxy->kaxby", row_hot, col_hot, triple_blocks.astype(jnp.float32))
    dense = dense.reshape(term_count, total_rows, CLASSES // PAIR, groups // CLASSES, PAIR, local_rows)
    dense = dense.transpose(0, 1, 2, 4, 3, 5).reshape(term_count, total_rows, total_rows)
    dense = dense.astype(jnp.bfloat16)
    summed = image_scatter(stiff_offsets, extended, stiff_blocks, dense, local_rows)
    return summed.reshape(local_rows, load_count, cell_count)


def solution(mesh):
    return jax.shard_map(
        per_device,
        mesh=mesh,
        in_specs=(
            P("term", None, "space"),
            P("term", "space", None, None, None),
            P("term", "space", None),
            P("term", None, None, None),
            P("term", None, None),
        ),
        out_specs=P("term", None, "space"),
        check_vma=False,
    )
```

```python
import jax
import jax.numpy as jnp
from jax import lax
from jax.experimental import pallas as pl
from jax.experimental.pallas import tpu as pltpu
from jax.sharding import PartitionSpec as P

MESH_ID = pl.DeviceIdType.MESH


CLASSES = 4
PAIR = 2


def gather_kernel(block_ref, out_ref, flat_ref, local_sem, send_near, recv_near, send_far, recv_far):
    count = out_ref.shape[0]
    rows, loads, cells = block_ref.shape
    for load in range(loads):
        flat_ref[load * rows:(load + 1) * rows, :] = block_ref[:, load, :]
    chunk = count // CLASSES
    row, stride, lane, far_peer, near_peer = scatter_peers(chunk, CLASSES)
    barrier = pltpu.get_barrier_semaphore()

    def greet_far(step, carry):
        pl.semaphore_signal(barrier, 1, device_id=(row, far_peer(step)), device_id_type=MESH_ID)
        return carry

    def greet_near(step, carry):
        pl.semaphore_signal(barrier, 1, device_id=(row, near_peer(step)), device_id_type=MESH_ID)
        return carry

    lax.fori_loop(1, chunk, greet_far, 0)
    lax.fori_loop(1, CLASSES, greet_near, 0)
    pl.semaphore_wait(barrier, chunk + CLASSES - 2)

    mine = lane * chunk + stride
    local = pltpu.make_async_copy(flat_ref, out_ref.at[mine], local_sem)
    local.start()

    def far_out(step):
        return pltpu.make_async_remote_copy(
            flat_ref, out_ref.at[mine], send_far.at[step], recv_far.at[stride],
            device_id=(row, far_peer(step)), device_id_type=MESH_ID,
        )

    def far_in(step):
        source = lax.rem(stride + chunk - step, chunk)
        return pltpu.make_async_remote_copy(
            flat_ref, out_ref.at[lane * chunk + source], send_far.at[step], recv_far.at[source],
            device_id=(row, term_device(lane, source, chunk)), device_id_type=MESH_ID,
        )

    def far_start(step, carry):
        far_out(step).start()
        return carry

    def far_finish(step, carry):
        far_out(step).wait_send()
        far_in(step).wait_recv()
        return carry

    lax.fori_loop(1, chunk, far_start, 0)
    local.wait()
    lax.fori_loop(1, chunk, far_finish, 0)

    own = out_ref.at[pl.ds(lane * chunk, chunk)]

    def near_out(step):
        return pltpu.make_async_remote_copy(
            own, own, send_near.at[step], recv_near.at[lane],
            device_id=(row, near_peer(step)), device_id_type=MESH_ID,
        )

    def near_in(step):
        source = lax.rem(lane + CLASSES - step, CLASSES)
        theirs = out_ref.at[pl.ds(source * chunk, chunk)]
        return pltpu.make_async_remote_copy(
            theirs, theirs, send_near.at[step], recv_near.at[source],
            device_id=(row, term_device(source, stride, chunk)), device_id_type=MESH_ID,
        )

    def near_start(step, carry):
        near_out(step).start()
        return carry

    def near_finish(step, carry):
        near_out(step).wait_send()
        near_in(step).wait_recv()
        return carry

    lax.fori_loop(1, CLASSES, near_start, 0)
    lax.fori_loop(1, CLASSES, near_finish, 0)


def gather_term(block):
    count = lax.axis_size("term")
    return pl.pallas_call(
        gather_kernel,
        out_shape=jax.ShapeDtypeStruct((count, block.shape[0] * block.shape[1], block.shape[2]), block.dtype),
        in_specs=[pl.BlockSpec(memory_space=pltpu.VMEM)],
        out_specs=pl.BlockSpec(memory_space=pltpu.VMEM),
        scratch_shapes=[
            pltpu.VMEM((block.shape[0] * block.shape[1], block.shape[2]), block.dtype),
            pltpu.SemaphoreType.DMA(()),
            pltpu.SemaphoreType.DMA((CLASSES,)),
            pltpu.SemaphoreType.DMA((CLASSES,)),
            pltpu.SemaphoreType.DMA((count // CLASSES,)),
            pltpu.SemaphoreType.DMA((count // CLASSES,)),
        ],
        compiler_params=pltpu.CompilerParams(collective_id=0, has_side_effects=True),
    )(block)


def term_device(lane, stride, chunk):
    return (lane // PAIR) * (chunk * PAIR) + stride * PAIR + lane % PAIR


def scatter_peers(chunk, classes):
    me = lax.axis_index("term")
    row = lax.axis_index("space")
    ring = chunk * PAIR
    stride = lax.rem(me, ring) // PAIR
    lane = (me // ring) * PAIR + lax.rem(me, PAIR)

    def far_peer(step):
        return term_device(lane, lax.rem(stride + step, chunk), chunk)

    def near_peer(step):
        return term_device(lax.rem(lane + step, classes), stride, chunk)

    return row, stride, lane, far_peer, near_peer


def scatter_greet(chunk, classes):
    row, stride, lane, far_peer, near_peer = scatter_peers(chunk, classes)
    barrier = pltpu.get_barrier_semaphore()

    def greet_far(step, carry):
        pl.semaphore_signal(barrier, 1, device_id=(row, far_peer(step)), device_id_type=MESH_ID)
        return carry

    def greet_near(step, carry):
        pl.semaphore_signal(barrier, 1, device_id=(row, near_peer(step)), device_id_type=MESH_ID)
        return carry

    lax.fori_loop(1, chunk, greet_far, 0)
    lax.fori_loop(1, classes, greet_near, 0)


def image_kernel(offs_ref, panel_ref, stiff_ref, triple_ref, out_ref, total_ref, far_src,
                 near_slots, class_sum, far_slots, send_near, recv_near, send_far, recv_far):
    block = pl.program_id(0)
    term = pl.program_id(1)
    band = stiff_ref.shape[2]
    width = stiff_ref.shape[-1]
    sides, chunk, _, local_rows, columns = total_ref.shape
    classes = sides * PAIR
    rows = triple_ref.shape[1]
    loads = panel_ref.shape[1] // rows
    block_rows = columns // (loads * width)
    term_count = pl.num_programs(1)
    rim = (panel_ref.shape[0] - block_rows) // 2
    half = loads * width
    row, stride, lane, far_peer, near_peer = scatter_peers(chunk, classes)

    @pl.when((term == 0) & (block == 0))
    def _():
        scatter_greet(chunk, classes)
        total_ref[...] = jnp.zeros_like(total_ref)

    total = jnp.zeros((loads * rows, width), jnp.float32)
    for slot in range(band):
        place = block + rim + offs_ref[(term * block_rows + block) * band + slot]
        total += lax.dot_general(
            panel_ref[place], stiff_ref[0, 0, slot],
            (((1,), (1,)), ((), ())), preferred_element_type=jnp.float32,
        )
    image = total.astype(jnp.bfloat16)
    for load in range(loads):
        column = pl.multiple_of((block * loads + load) * width, width)
        product = jnp.dot(
            triple_ref[0], image[load * rows:(load + 1) * rows], preferred_element_type=jnp.float32
        )
        total_ref[:, :, :, :, pl.ds(column, width)] += product.reshape(
            sides, chunk, PAIR, local_rows, width
        )

    def near_copy(step, part, inbound):
        cols = pl.ds(pl.multiple_of(part * half, half), half)
        if inbound:
            source = lax.rem(lane + classes - step, classes)
            return pltpu.make_async_remote_copy(
                total_ref.at[source // PAIR, :, source % PAIR, :, cols],
                near_slots.at[source, :, :, cols], send_near.at[part, step], recv_near.at[part, source],
                device_id=(row, term_device(source, stride, chunk)), device_id_type=MESH_ID,
            )
        target = lax.rem(lane + step, classes)
        return pltpu.make_async_remote_copy(
            total_ref.at[target // PAIR, :, target % PAIR, :, cols],
            near_slots.at[lane, :, :, cols], send_near.at[part, step], recv_near.at[part, lane],
            device_id=(row, near_peer(step)), device_id_type=MESH_ID,
        )

    @pl.when(term == term_count - 1)
    def _():
        @pl.when(block == 0)
        def _():
            pl.semaphore_wait(pltpu.get_barrier_semaphore(), chunk + classes - 2)

        def near_start(step, carry):
            near_copy(step, block, False).start()
            return carry

        lax.fori_loop(1, classes, near_start, 0)

    @pl.when((term == term_count - 1) & (block == block_rows - 1))
    def _():
        for part in range(block_rows):
            cols = pl.ds(part * half, half)

            def near_finish(step, total):
                near_copy(step, part, False).wait_send()
                near_copy(step, part, True).wait_recv()
                source = lax.rem(lane + classes - step, classes)
                return total + near_slots[source, :, :, cols]

            own = total_ref[lane // PAIR, :, lane % PAIR, :, cols]
            class_sum[:, :, cols] = lax.fori_loop(1, classes, near_finish, own)

        far_src[...] = class_sum[...].astype(far_src.dtype)

        def far_out(step):
            target = lax.rem(stride + step, chunk)
            return pltpu.make_async_remote_copy(
                far_src.at[target], far_slots.at[stride], send_far.at[step], recv_far.at[stride],
                device_id=(row, far_peer(step)), device_id_type=MESH_ID,
            )

        def far_in(step):
            source = lax.rem(stride + chunk - step, chunk)
            return pltpu.make_async_remote_copy(
                far_src.at[source], far_slots.at[source], send_far.at[step], recv_far.at[source],
                device_id=(row, term_device(lane, source, chunk)), device_id_type=MESH_ID,
            )

        def far_start(step, carry):
            far_out(step).start()
            return carry

        def far_finish(step, total):
            far_out(step).wait_send()
            far_in(step).wait_recv()
            source = lax.rem(stride + chunk - step, chunk)
            return total + far_slots[source].astype(jnp.float32)

        lax.fori_loop(1, chunk, far_start, 0)
        summed = lax.fori_loop(1, chunk, far_finish, class_sum[stride])
        for part in range(block_rows):
            for load in range(loads):
                source = (part * loads + load) * width
                target = (load * block_rows + part) * width
                out_ref[:, target:target + width] = summed[:, source:source + width]


def image_scatter(offsets, panel, stiff_blocks, dense, local_rows):
    term_count, block_rows, band, width, _ = stiff_blocks.shape
    places, stacked, _ = panel.shape
    rows = dense.shape[1]
    columns = stacked // rows * block_rows * width
    classes = CLASSES
    chunk = rows // (classes * local_rows)
    shape = (classes // PAIR, chunk, PAIR, local_rows, columns)
    return pl.pallas_call(
        image_kernel,
        out_shape=jax.ShapeDtypeStruct((local_rows, columns), jnp.float32),
        grid_spec=pltpu.PrefetchScalarGridSpec(
            num_scalar_prefetch=1,
            grid=(block_rows, term_count),
            in_specs=[
                pl.BlockSpec((places, stacked, width), lambda b, k, offs: (0, 0, 0)),
                pl.BlockSpec((1, 1, band, width, width), lambda b, k, offs: (k, b, 0, 0, 0)),
                pl.BlockSpec((1, rows, rows), lambda b, k, offs: (k, 0, 0)),
            ],
            out_specs=pl.BlockSpec((local_rows, columns), lambda b, k, offs: (0, 0)),
            scratch_shapes=[
                pltpu.VMEM(shape, jnp.float32),
                pltpu.VMEM((chunk, local_rows, columns), jnp.bfloat16),
                pltpu.VMEM((classes, chunk, local_rows, columns), jnp.float32),
                pltpu.VMEM((chunk, local_rows, columns), jnp.float32),
                pltpu.VMEM((chunk, local_rows, columns), jnp.bfloat16),
                pltpu.SemaphoreType.DMA((block_rows, classes)),
                pltpu.SemaphoreType.DMA((block_rows, classes)),
                pltpu.SemaphoreType.DMA((chunk,)),
                pltpu.SemaphoreType.DMA((chunk,)),
            ],
        ),
        compiler_params=pltpu.CompilerParams(collective_id=1, has_side_effects=True),
    )(offsets.reshape(-1), panel, stiff_blocks, dense)


def with_halo(block, sides, width):
    for axis, dim in sides:
        count = lax.axis_size(axis)
        forward = [(i, i + 1) for i in range(count - 1)]
        backward = [(target, source) for source, target in forward]
        low = lax.ppermute(
            lax.slice_in_dim(block, block.shape[dim] - width, None, axis=dim), axis, forward
        )
        high = lax.ppermute(lax.slice_in_dim(block, 0, width, axis=dim), axis, backward)
        block = jnp.concatenate([low, block, high], axis=dim)
    return block


def per_device(chaos_field, stiff_blocks, stiff_offsets, triple_blocks, triple_pattern):
    local_rows = chaos_field.shape[0]
    load_count = chaos_field.shape[1]
    cell_count = chaos_field.shape[2]
    term_count = stiff_blocks.shape[0]
    block_width = stiff_blocks.shape[3]
    block_rows = cell_count // block_width
    groups = lax.axis_size("term")
    total_rows = local_rows * groups
    rim_cells = 2 * block_width
    gathered = gather_term(chaos_field)
    panel = gathered.reshape(groups, load_count, local_rows, block_rows, block_width)
    panel = panel.transpose(3, 1, 0, 2, 4).reshape(block_rows, load_count, total_rows, block_width)
    extended = with_halo(panel, (("space", 0),), rim_cells // block_width)
    extended = extended.reshape(block_rows + 4, load_count * total_rows, block_width)
    block_size = triple_blocks.shape[2]
    levels = jnp.arange(total_rows // block_size, dtype=jnp.int32)
    row_hot = (triple_pattern[:, :, 0:1] == levels).astype(jnp.float32)
    col_hot = (triple_pattern[:, :, 1:2] == levels).astype(jnp.float32)
    dense = jnp.einsum("kna,knb,knxy->kaxby", row_hot, col_hot, triple_blocks.astype(jnp.float32))
    dense = dense.reshape(term_count, total_rows, CLASSES // PAIR, groups // CLASSES, PAIR, local_rows)
    dense = dense.transpose(0, 1, 2, 4, 3, 5).reshape(term_count, total_rows, total_rows)
    dense = dense.astype(jnp.bfloat16)
    summed = image_scatter(stiff_offsets, extended, stiff_blocks, dense, local_rows)
    return summed.reshape(local_rows, load_count, cell_count)


def solution(mesh):
    return jax.shard_map(
        per_device,
        mesh=mesh,
        in_specs=(
            P("term", None, "space"),
            P("term", "space", None, None, None),
            P("term", "space", None),
            P("term", None, None, None),
            P("term", None, None),
        ),
        out_specs=P("term", None, "space"),
        check_vma=False,
    )
```

```python
import jax
import jax.numpy as jnp
from jax import lax
from jax.experimental import pallas as pl
from jax.experimental.pallas import tpu as pltpu
from jax.sharding import PartitionSpec as P

MESH_ID = pl.DeviceIdType.MESH


CLASSES = 4
PAIR = 2


def gather_kernel(block_ref, panel_ref, out_ref, flat_ref, local_sem, send_near, recv_near, send_far,
                  recv_far):
    count = out_ref.shape[0]
    rows, loads, cells = block_ref.shape
    for load in range(loads):
        flat_ref[load * rows:(load + 1) * rows, :] = block_ref[:, load, :]
    chunk = count // CLASSES
    row, stride, lane, far_peer, near_peer = scatter_peers(chunk, CLASSES)
    barrier = pltpu.get_barrier_semaphore()

    def greet_far(step, carry):
        pl.semaphore_signal(barrier, 1, device_id=(row, far_peer(step)), device_id_type=MESH_ID)
        return carry

    def greet_near(step, carry):
        pl.semaphore_signal(barrier, 1, device_id=(row, near_peer(step)), device_id_type=MESH_ID)
        return carry

    lax.fori_loop(1, chunk, greet_far, 0)
    lax.fori_loop(1, CLASSES, greet_near, 0)
    pl.semaphore_wait(barrier, chunk + CLASSES - 2)

    mine = lane * chunk + stride
    local = pltpu.make_async_copy(flat_ref, out_ref.at[mine], local_sem)
    local.start()

    def far_out(step):
        return pltpu.make_async_remote_copy(
            flat_ref, out_ref.at[mine], send_far.at[step], recv_far.at[stride],
            device_id=(row, far_peer(step)), device_id_type=MESH_ID,
        )

    def far_in(step):
        source = lax.rem(stride + chunk - step, chunk)
        return pltpu.make_async_remote_copy(
            flat_ref, out_ref.at[lane * chunk + source], send_far.at[step], recv_far.at[source],
            device_id=(row, term_device(lane, source, chunk)), device_id_type=MESH_ID,
        )

    def far_start(step, carry):
        far_out(step).start()
        return carry

    def far_finish(step, carry):
        far_out(step).wait_send()
        far_in(step).wait_recv()
        return carry

    lax.fori_loop(1, chunk, far_start, 0)
    local.wait()
    lax.fori_loop(1, chunk, far_finish, 0)

    own = out_ref.at[pl.ds(lane * chunk, chunk)]

    def near_out(step):
        return pltpu.make_async_remote_copy(
            own, own, send_near.at[step], recv_near.at[lane],
            device_id=(row, near_peer(step)), device_id_type=MESH_ID,
        )

    def near_in(step):
        source = lax.rem(lane + CLASSES - step, CLASSES)
        theirs = out_ref.at[pl.ds(source * chunk, chunk)]
        return pltpu.make_async_remote_copy(
            theirs, theirs, send_near.at[step], recv_near.at[source],
            device_id=(row, term_device(source, stride, chunk)), device_id_type=MESH_ID,
        )

    def near_start(step, carry):
        near_out(step).start()
        return carry

    def near_finish(step, carry):
        near_out(step).wait_send()
        near_in(step).wait_recv()
        return carry

    lax.fori_loop(1, CLASSES, near_start, 0)
    lax.fori_loop(1, CLASSES, near_finish, 0)

    width = panel_ref.shape[-1]
    for slot in range(count):
        for load in range(loads):
            for block in range(panel_ref.shape[0]):
                panel_ref[block, load, slot * rows:(slot + 1) * rows, :] = out_ref[
                    slot, load * rows:(load + 1) * rows, block * width:(block + 1) * width
                ]


def gather_term(block, width):
    count = lax.axis_size("term")
    return pl.pallas_call(
        gather_kernel,
        out_shape=jax.ShapeDtypeStruct(
            (block.shape[2] // width, block.shape[1], count * block.shape[0], width), block.dtype
        ),
        in_specs=[pl.BlockSpec(memory_space=pltpu.VMEM)],
        out_specs=pl.BlockSpec(memory_space=pltpu.VMEM),
        scratch_shapes=[
            pltpu.VMEM((count, block.shape[0] * block.shape[1], block.shape[2]), block.dtype),
            pltpu.VMEM((block.shape[0] * block.shape[1], block.shape[2]), block.dtype),
            pltpu.SemaphoreType.DMA(()),
            pltpu.SemaphoreType.DMA((CLASSES,)),
            pltpu.SemaphoreType.DMA((CLASSES,)),
            pltpu.SemaphoreType.DMA((count // CLASSES,)),
            pltpu.SemaphoreType.DMA((count // CLASSES,)),
        ],
        compiler_params=pltpu.CompilerParams(collective_id=0, has_side_effects=True),
    )(block)


def term_device(lane, stride, chunk):
    return (lane // PAIR) * (chunk * PAIR) + stride * PAIR + lane % PAIR


def scatter_peers(chunk, classes):
    me = lax.axis_index("term")
    row = lax.axis_index("space")
    ring = chunk * PAIR
    stride = lax.rem(me, ring) // PAIR
    lane = (me // ring) * PAIR + lax.rem(me, PAIR)

    def far_peer(step):
        return term_device(lane, lax.rem(stride + step, chunk), chunk)

    def near_peer(step):
        return term_device(lax.rem(lane + step, classes), stride, chunk)

    return row, stride, lane, far_peer, near_peer


def scatter_greet(chunk, classes):
    row, stride, lane, far_peer, near_peer = scatter_peers(chunk, classes)
    barrier = pltpu.get_barrier_semaphore()

    def greet_far(step, carry):
        pl.semaphore_signal(barrier, 1, device_id=(row, far_peer(step)), device_id_type=MESH_ID)
        return carry

    def greet_near(step, carry):
        pl.semaphore_signal(barrier, 1, device_id=(row, near_peer(step)), device_id_type=MESH_ID)
        return carry

    lax.fori_loop(1, chunk, greet_far, 0)
    lax.fori_loop(1, classes, greet_near, 0)


def image_kernel(offs_ref, panel_ref, stiff_ref, triple_ref, out_ref, total_ref, far_src,
                 near_slots, class_sum, far_slots, send_near, recv_near, send_far, recv_far):
    block = pl.program_id(0)
    term = pl.program_id(1)
    band = stiff_ref.shape[2]
    width = stiff_ref.shape[-1]
    sides, chunk, _, local_rows, columns = total_ref.shape
    classes = sides * PAIR
    rows = triple_ref.shape[1]
    loads = panel_ref.shape[1] // rows
    block_rows = columns // (loads * width)
    term_count = pl.num_programs(1)
    rim = (panel_ref.shape[0] - block_rows) // 2
    half = loads * width
    row, stride, lane, far_peer, near_peer = scatter_peers(chunk, classes)

    @pl.when((term == 0) & (block == 0))
    def _():
        scatter_greet(chunk, classes)
        total_ref[...] = jnp.zeros_like(total_ref)

    total = jnp.zeros((loads * rows, width), jnp.float32)
    for slot in range(band):
        place = block + rim + offs_ref[(term * block_rows + block) * band + slot]
        total += lax.dot_general(
            panel_ref[place], stiff_ref[0, 0, slot],
            (((1,), (1,)), ((), ())), preferred_element_type=jnp.float32,
        )
    image = total.astype(jnp.bfloat16)
    for load in range(loads):
        column = pl.multiple_of((block * loads + load) * width, width)
        product = jnp.dot(
            triple_ref[0], image[load * rows:(load + 1) * rows], preferred_element_type=jnp.float32
        )
        total_ref[:, :, :, :, pl.ds(column, width)] += product.reshape(
            sides, chunk, PAIR, local_rows, width
        )

    def near_copy(step, part, inbound):
        cols = pl.ds(pl.multiple_of(part * half, half), half)
        if inbound:
            source = lax.rem(lane + classes - step, classes)
            return pltpu.make_async_remote_copy(
                total_ref.at[source // PAIR, :, source % PAIR, :, cols],
                near_slots.at[source, :, :, cols], send_near.at[part, step], recv_near.at[part, source],
                device_id=(row, term_device(source, stride, chunk)), device_id_type=MESH_ID,
            )
        target = lax.rem(lane + step, classes)
        return pltpu.make_async_remote_copy(
            total_ref.at[target // PAIR, :, target % PAIR, :, cols],
            near_slots.at[lane, :, :, cols], send_near.at[part, step], recv_near.at[part, lane],
            device_id=(row, near_peer(step)), device_id_type=MESH_ID,
        )

    @pl.when(term == term_count - 1)
    def _():
        @pl.when(block == 0)
        def _():
            pl.semaphore_wait(pltpu.get_barrier_semaphore(), chunk + classes - 2)

        def near_start(step, carry):
            near_copy(step, block, False).start()
            return carry

        lax.fori_loop(1, classes, near_start, 0)

    @pl.when((term == term_count - 1) & (block == block_rows - 1))
    def _():
        for part in range(block_rows):
            cols = pl.ds(part * half, half)

            def near_finish(step, total):
                near_copy(step, part, False).wait_send()
                near_copy(step, part, True).wait_recv()
                source = lax.rem(lane + classes - step, classes)
                return total + near_slots[source, :, :, cols]

            own = total_ref[lane // PAIR, :, lane % PAIR, :, cols]
            class_sum[:, :, cols] = lax.fori_loop(1, classes, near_finish, own)

        far_src[...] = class_sum[...].astype(far_src.dtype)

        def far_out(step):
            target = lax.rem(stride + step, chunk)
            return pltpu.make_async_remote_copy(
                far_src.at[target], far_slots.at[stride], send_far.at[step], recv_far.at[stride],
                device_id=(row, far_peer(step)), device_id_type=MESH_ID,
            )

        def far_in(step):
            source = lax.rem(stride + chunk - step, chunk)
            return pltpu.make_async_remote_copy(
                far_src.at[source], far_slots.at[source], send_far.at[step], recv_far.at[source],
                device_id=(row, term_device(lane, source, chunk)), device_id_type=MESH_ID,
            )

        def far_start(step, carry):
            far_out(step).start()
            return carry

        def far_finish(step, total):
            far_out(step).wait_send()
            far_in(step).wait_recv()
            source = lax.rem(stride + chunk - step, chunk)
            return total + far_slots[source].astype(jnp.float32)

        lax.fori_loop(1, chunk, far_start, 0)
        summed = lax.fori_loop(1, chunk, far_finish, class_sum[stride])
        for part in range(block_rows):
            for load in range(loads):
                source = (part * loads + load) * width
                target = (load * block_rows + part) * width
                out_ref[:, target:target + width] = summed[:, source:source + width]


def image_scatter(offsets, panel, stiff_blocks, dense, local_rows):
    term_count, block_rows, band, width, _ = stiff_blocks.shape
    places, stacked, _ = panel.shape
    rows = dense.shape[1]
    columns = stacked // rows * block_rows * width
    classes = CLASSES
    chunk = rows // (classes * local_rows)
    shape = (classes // PAIR, chunk, PAIR, local_rows, columns)
    return pl.pallas_call(
        image_kernel,
        out_shape=jax.ShapeDtypeStruct((local_rows, columns), jnp.float32),
        grid_spec=pltpu.PrefetchScalarGridSpec(
            num_scalar_prefetch=1,
            grid=(block_rows, term_count),
            in_specs=[
                pl.BlockSpec((places, stacked, width), lambda b, k, offs: (0, 0, 0)),
                pl.BlockSpec((1, 1, band, width, width), lambda b, k, offs: (k, b, 0, 0, 0)),
                pl.BlockSpec((1, rows, rows), lambda b, k, offs: (k, 0, 0)),
            ],
            out_specs=pl.BlockSpec((local_rows, columns), lambda b, k, offs: (0, 0)),
            scratch_shapes=[
                pltpu.VMEM(shape, jnp.float32),
                pltpu.VMEM((chunk, local_rows, columns), jnp.bfloat16),
                pltpu.VMEM((classes, chunk, local_rows, columns), jnp.float32),
                pltpu.VMEM((chunk, local_rows, columns), jnp.float32),
                pltpu.VMEM((chunk, local_rows, columns), jnp.bfloat16),
                pltpu.SemaphoreType.DMA((block_rows, classes)),
                pltpu.SemaphoreType.DMA((block_rows, classes)),
                pltpu.SemaphoreType.DMA((chunk,)),
                pltpu.SemaphoreType.DMA((chunk,)),
            ],
        ),
        compiler_params=pltpu.CompilerParams(collective_id=1, has_side_effects=True),
    )(offsets.reshape(-1), panel, stiff_blocks, dense)


def with_halo(block, sides, width):
    for axis, dim in sides:
        count = lax.axis_size(axis)
        forward = [(i, i + 1) for i in range(count - 1)]
        backward = [(target, source) for source, target in forward]
        low = lax.ppermute(
            lax.slice_in_dim(block, block.shape[dim] - width, None, axis=dim), axis, forward
        )
        high = lax.ppermute(lax.slice_in_dim(block, 0, width, axis=dim), axis, backward)
        block = jnp.concatenate([low, block, high], axis=dim)
    return block


def per_device(chaos_field, stiff_blocks, stiff_offsets, triple_blocks, triple_pattern):
    local_rows = chaos_field.shape[0]
    load_count = chaos_field.shape[1]
    cell_count = chaos_field.shape[2]
    term_count = stiff_blocks.shape[0]
    block_width = stiff_blocks.shape[3]
    block_rows = cell_count // block_width
    groups = lax.axis_size("term")
    total_rows = local_rows * groups
    rim_cells = 2 * block_width
    panel = gather_term(chaos_field, block_width)
    extended = with_halo(panel, (("space", 0),), rim_cells // block_width)
    extended = extended.reshape(block_rows + 4, load_count * total_rows, block_width)
    block_size = triple_blocks.shape[2]
    levels = jnp.arange(total_rows // block_size, dtype=jnp.int32)
    row_hot = (triple_pattern[:, :, 0:1] == levels).astype(jnp.float32)
    col_hot = (triple_pattern[:, :, 1:2] == levels).astype(jnp.float32)
    dense = jnp.einsum("kna,knb,knxy->kaxby", row_hot, col_hot, triple_blocks.astype(jnp.float32))
    dense = dense.reshape(term_count, total_rows, CLASSES // PAIR, groups // CLASSES, PAIR, local_rows)
    dense = dense.transpose(0, 1, 2, 4, 3, 5).reshape(term_count, total_rows, total_rows)
    dense = dense.astype(jnp.bfloat16)
    summed = image_scatter(stiff_offsets, extended, stiff_blocks, dense, local_rows)
    return summed.reshape(local_rows, load_count, cell_count)


def solution(mesh):
    return jax.shard_map(
        per_device,
        mesh=mesh,
        in_specs=(
            P("term", None, "space"),
            P("term", "space", None, None, None),
            P("term", "space", None),
            P("term", None, None, None),
            P("term", None, None),
        ),
        out_specs=P("term", None, "space"),
        check_vma=False,
    )
```

```python
import jax
import jax.numpy as jnp
from jax import lax
from jax.experimental import pallas as pl
from jax.experimental.pallas import tpu as pltpu
from jax.sharding import PartitionSpec as P

MESH_ID = pl.DeviceIdType.MESH


CLASSES = 4
PAIR = 2


def gather_kernel(block_ref, panel_ref, out_ref, flat_ref, local_sem, send_near, recv_near, send_far,
                  recv_far, halo_send, halo_recv):
    count = out_ref.shape[0]
    slabs = lax.axis_size("space")
    rim = (panel_ref.shape[0] - block_ref.shape[2] // panel_ref.shape[-1]) // 2
    rows, loads, cells = block_ref.shape
    for load in range(loads):
        flat_ref[load * rows:(load + 1) * rows, :] = block_ref[:, load, :]
    chunk = count // CLASSES
    row, stride, lane, far_peer, near_peer = scatter_peers(chunk, CLASSES)
    barrier = pltpu.get_barrier_semaphore()

    def greet_far(step, carry):
        pl.semaphore_signal(barrier, 1, device_id=(row, far_peer(step)), device_id_type=MESH_ID)
        return carry

    def greet_near(step, carry):
        pl.semaphore_signal(barrier, 1, device_id=(row, near_peer(step)), device_id_type=MESH_ID)
        return carry

    lax.fori_loop(1, chunk, greet_far, 0)
    lax.fori_loop(1, CLASSES, greet_near, 0)
    me = lax.axis_index("term")
    has_left = row > 0
    has_right = row < slabs - 1

    @pl.when(has_left)
    def _():
        pl.semaphore_signal(barrier, 1, device_id=(row - 1, me), device_id_type=MESH_ID)

    @pl.when(has_right)
    def _():
        pl.semaphore_signal(barrier, 1, device_id=(row + 1, me), device_id_type=MESH_ID)

    pl.semaphore_wait(
        barrier, chunk + CLASSES - 2 + has_left.astype(jnp.int32) + has_right.astype(jnp.int32)
    )

    mine = lane * chunk + stride
    local = pltpu.make_async_copy(flat_ref, out_ref.at[mine], local_sem)
    local.start()

    def far_out(step):
        return pltpu.make_async_remote_copy(
            flat_ref, out_ref.at[mine], send_far.at[step], recv_far.at[stride],
            device_id=(row, far_peer(step)), device_id_type=MESH_ID,
        )

    def far_in(step):
        source = lax.rem(stride + chunk - step, chunk)
        return pltpu.make_async_remote_copy(
            flat_ref, out_ref.at[lane * chunk + source], send_far.at[step], recv_far.at[source],
            device_id=(row, term_device(lane, source, chunk)), device_id_type=MESH_ID,
        )

    def far_start(step, carry):
        far_out(step).start()
        return carry

    def far_finish(step, carry):
        far_out(step).wait_send()
        far_in(step).wait_recv()
        return carry

    lax.fori_loop(1, chunk, far_start, 0)
    local.wait()
    lax.fori_loop(1, chunk, far_finish, 0)

    own = out_ref.at[pl.ds(lane * chunk, chunk)]

    def near_out(step):
        return pltpu.make_async_remote_copy(
            own, own, send_near.at[step], recv_near.at[lane],
            device_id=(row, near_peer(step)), device_id_type=MESH_ID,
        )

    def near_in(step):
        source = lax.rem(lane + CLASSES - step, CLASSES)
        theirs = out_ref.at[pl.ds(source * chunk, chunk)]
        return pltpu.make_async_remote_copy(
            theirs, theirs, send_near.at[step], recv_near.at[source],
            device_id=(row, term_device(source, stride, chunk)), device_id_type=MESH_ID,
        )

    def near_start(step, carry):
        near_out(step).start()
        return carry

    def near_finish(step, carry):
        near_out(step).wait_send()
        near_in(step).wait_recv()
        return carry

    lax.fori_loop(1, CLASSES, near_start, 0)
    lax.fori_loop(1, CLASSES, near_finish, 0)

    width = panel_ref.shape[-1]
    blocks = cells // width
    for slot in range(count):
        for load in range(loads):
            for block in range(blocks):
                panel_ref[rim + block, load, slot * rows:(slot + 1) * rows, :] = out_ref[
                    slot, load * rows:(load + 1) * rows, block * width:(block + 1) * width
                ]
    own = panel_ref.at[pl.ds(rim, blocks)]
    to_left = pltpu.make_async_remote_copy(
        own, panel_ref.at[pl.ds(rim + blocks, rim)], halo_send.at[0], halo_recv.at[0],
        device_id=(row - 1, me), device_id_type=MESH_ID,
    )
    to_right = pltpu.make_async_remote_copy(
        own, panel_ref.at[pl.ds(0, rim)], halo_send.at[1], halo_recv.at[1],
        device_id=(row + 1, me), device_id_type=MESH_ID,
    )

    @pl.when(has_left)
    def _():
        to_left.start()

    @pl.when(has_right)
    def _():
        to_right.start()

    @pl.when(jnp.logical_not(has_left))
    def _():
        panel_ref[pl.ds(0, rim)] = jnp.zeros((rim,) + panel_ref.shape[1:], panel_ref.dtype)

    @pl.when(jnp.logical_not(has_right))
    def _():
        panel_ref[pl.ds(rim + blocks, rim)] = jnp.zeros((rim,) + panel_ref.shape[1:], panel_ref.dtype)

    @pl.when(has_left)
    def _():
        to_left.wait_send()
        to_right.wait_recv()

    @pl.when(has_right)
    def _():
        to_right.wait_send()
        to_left.wait_recv()


def gather_term(block, width):
    count = lax.axis_size("term")
    return pl.pallas_call(
        gather_kernel,
        out_shape=jax.ShapeDtypeStruct(
            (block.shape[2] // width + 4, block.shape[1], count * block.shape[0], width), block.dtype
        ),
        in_specs=[pl.BlockSpec(memory_space=pltpu.VMEM)],
        out_specs=pl.BlockSpec(memory_space=pltpu.VMEM),
        scratch_shapes=[
            pltpu.VMEM((count, block.shape[0] * block.shape[1], block.shape[2]), block.dtype),
            pltpu.VMEM((block.shape[0] * block.shape[1], block.shape[2]), block.dtype),
            pltpu.SemaphoreType.DMA(()),
            pltpu.SemaphoreType.DMA((CLASSES,)),
            pltpu.SemaphoreType.DMA((CLASSES,)),
            pltpu.SemaphoreType.DMA((count // CLASSES,)),
            pltpu.SemaphoreType.DMA((count // CLASSES,)),
            pltpu.SemaphoreType.DMA((2,)),
            pltpu.SemaphoreType.DMA((2,)),
        ],
        compiler_params=pltpu.CompilerParams(collective_id=0, has_side_effects=True),
    )(block)


def term_device(lane, stride, chunk):
    return (lane // PAIR) * (chunk * PAIR) + stride * PAIR + lane % PAIR


def scatter_peers(chunk, classes):
    me = lax.axis_index("term")
    row = lax.axis_index("space")
    ring = chunk * PAIR
    stride = lax.rem(me, ring) // PAIR
    lane = (me // ring) * PAIR + lax.rem(me, PAIR)

    def far_peer(step):
        return term_device(lane, lax.rem(stride + step, chunk), chunk)

    def near_peer(step):
        return term_device(lax.rem(lane + step, classes), stride, chunk)

    return row, stride, lane, far_peer, near_peer


def scatter_greet(chunk, classes):
    row, stride, lane, far_peer, near_peer = scatter_peers(chunk, classes)
    barrier = pltpu.get_barrier_semaphore()

    def greet_far(step, carry):
        pl.semaphore_signal(barrier, 1, device_id=(row, far_peer(step)), device_id_type=MESH_ID)
        return carry

    def greet_near(step, carry):
        pl.semaphore_signal(barrier, 1, device_id=(row, near_peer(step)), device_id_type=MESH_ID)
        return carry

    lax.fori_loop(1, chunk, greet_far, 0)
    lax.fori_loop(1, classes, greet_near, 0)


def image_kernel(offs_ref, panel_ref, stiff_ref, triple_ref, out_ref, total_ref, far_src,
                 near_slots, class_sum, far_slots, send_near, recv_near, send_far, recv_far):
    block = pl.program_id(0)
    term = pl.program_id(1)
    band = stiff_ref.shape[2]
    width = stiff_ref.shape[-1]
    sides, chunk, _, local_rows, columns = total_ref.shape
    classes = sides * PAIR
    rows = triple_ref.shape[1]
    loads = panel_ref.shape[1] // rows
    block_rows = columns // (loads * width)
    term_count = pl.num_programs(1)
    rim = (panel_ref.shape[0] - block_rows) // 2
    half = loads * width
    row, stride, lane, far_peer, near_peer = scatter_peers(chunk, classes)

    @pl.when((term == 0) & (block == 0))
    def _():
        scatter_greet(chunk, classes)
        total_ref[...] = jnp.zeros_like(total_ref)

    total = jnp.zeros((loads * rows, width), jnp.float32)
    for slot in range(band):
        place = block + rim + offs_ref[(term * block_rows + block) * band + slot]
        total += lax.dot_general(
            panel_ref[place], stiff_ref[0, 0, slot],
            (((1,), (1,)), ((), ())), preferred_element_type=jnp.float32,
        )
    image = total.astype(jnp.bfloat16)
    for load in range(loads):
        column = pl.multiple_of((block * loads + load) * width, width)
        product = jnp.dot(
            triple_ref[0], image[load * rows:(load + 1) * rows], preferred_element_type=jnp.float32
        )
        total_ref[:, :, :, :, pl.ds(column, width)] += product.reshape(
            sides, chunk, PAIR, local_rows, width
        )

    def near_copy(step, part, inbound):
        cols = pl.ds(pl.multiple_of(part * half, half), half)
        if inbound:
            source = lax.rem(lane + classes - step, classes)
            return pltpu.make_async_remote_copy(
                total_ref.at[source // PAIR, :, source % PAIR, :, cols],
                near_slots.at[source, :, :, cols], send_near.at[part, step], recv_near.at[part, source],
                device_id=(row, term_device(source, stride, chunk)), device_id_type=MESH_ID,
            )
        target = lax.rem(lane + step, classes)
        return pltpu.make_async_remote_copy(
            total_ref.at[target // PAIR, :, target % PAIR, :, cols],
            near_slots.at[lane, :, :, cols], send_near.at[part, step], recv_near.at[part, lane],
            device_id=(row, near_peer(step)), device_id_type=MESH_ID,
        )

    @pl.when(term == term_count - 1)
    def _():
        @pl.when(block == 0)
        def _():
            pl.semaphore_wait(pltpu.get_barrier_semaphore(), chunk + classes - 2)

        def near_start(step, carry):
            near_copy(step, block, False).start()
            return carry

        lax.fori_loop(1, classes, near_start, 0)

    @pl.when((term == term_count - 1) & (block == block_rows - 1))
    def _():
        for part in range(block_rows):
            cols = pl.ds(part * half, half)

            def near_finish(step, total):
                near_copy(step, part, False).wait_send()
                near_copy(step, part, True).wait_recv()
                source = lax.rem(lane + classes - step, classes)
                return total + near_slots[source, :, :, cols]

            own = total_ref[lane // PAIR, :, lane % PAIR, :, cols]
            class_sum[:, :, cols] = lax.fori_loop(1, classes, near_finish, own)

        far_src[...] = class_sum[...].astype(far_src.dtype)

        def far_out(step):
            target = lax.rem(stride + step, chunk)
            return pltpu.make_async_remote_copy(
                far_src.at[target], far_slots.at[stride], send_far.at[step], recv_far.at[stride],
                device_id=(row, far_peer(step)), device_id_type=MESH_ID,
            )

        def far_in(step):
            source = lax.rem(stride + chunk - step, chunk)
            return pltpu.make_async_remote_copy(
                far_src.at[source], far_slots.at[source], send_far.at[step], recv_far.at[source],
                device_id=(row, term_device(lane, source, chunk)), device_id_type=MESH_ID,
            )

        def far_start(step, carry):
            far_out(step).start()
            return carry

        def far_finish(step, total):
            far_out(step).wait_send()
            far_in(step).wait_recv()
            source = lax.rem(stride + chunk - step, chunk)
            return total + far_slots[source].astype(jnp.float32)

        lax.fori_loop(1, chunk, far_start, 0)
        summed = lax.fori_loop(1, chunk, far_finish, class_sum[stride])
        for part in range(block_rows):
            for load in range(loads):
                source = (part * loads + load) * width
                target = (load * block_rows + part) * width
                out_ref[:, target:target + width] = summed[:, source:source + width]


def image_scatter(offsets, panel, stiff_blocks, dense, local_rows):
    term_count, block_rows, band, width, _ = stiff_blocks.shape
    places, stacked, _ = panel.shape
    rows = dense.shape[1]
    columns = stacked // rows * block_rows * width
    classes = CLASSES
    chunk = rows // (classes * local_rows)
    shape = (classes // PAIR, chunk, PAIR, local_rows, columns)
    return pl.pallas_call(
        image_kernel,
        out_shape=jax.ShapeDtypeStruct((local_rows, columns), jnp.float32),
        grid_spec=pltpu.PrefetchScalarGridSpec(
            num_scalar_prefetch=1,
            grid=(block_rows, term_count),
            in_specs=[
                pl.BlockSpec((places, stacked, width), lambda b, k, offs: (0, 0, 0)),
                pl.BlockSpec((1, 1, band, width, width), lambda b, k, offs: (k, b, 0, 0, 0)),
                pl.BlockSpec((1, rows, rows), lambda b, k, offs: (k, 0, 0)),
            ],
            out_specs=pl.BlockSpec((local_rows, columns), lambda b, k, offs: (0, 0)),
            scratch_shapes=[
                pltpu.VMEM(shape, jnp.float32),
                pltpu.VMEM((chunk, local_rows, columns), jnp.bfloat16),
                pltpu.VMEM((classes, chunk, local_rows, columns), jnp.float32),
                pltpu.VMEM((chunk, local_rows, columns), jnp.float32),
                pltpu.VMEM((chunk, local_rows, columns), jnp.bfloat16),
                pltpu.SemaphoreType.DMA((block_rows, classes)),
                pltpu.SemaphoreType.DMA((block_rows, classes)),
                pltpu.SemaphoreType.DMA((chunk,)),
                pltpu.SemaphoreType.DMA((chunk,)),
            ],
        ),
        compiler_params=pltpu.CompilerParams(collective_id=1, has_side_effects=True),
    )(offsets.reshape(-1), panel, stiff_blocks, dense)


def with_halo(block, sides, width):
    for axis, dim in sides:
        count = lax.axis_size(axis)
        forward = [(i, i + 1) for i in range(count - 1)]
        backward = [(target, source) for source, target in forward]
        low = lax.ppermute(
            lax.slice_in_dim(block, block.shape[dim] - width, None, axis=dim), axis, forward
        )
        high = lax.ppermute(lax.slice_in_dim(block, 0, width, axis=dim), axis, backward)
        block = jnp.concatenate([low, block, high], axis=dim)
    return block


def per_device(chaos_field, stiff_blocks, stiff_offsets, triple_blocks, triple_pattern):
    local_rows = chaos_field.shape[0]
    load_count = chaos_field.shape[1]
    cell_count = chaos_field.shape[2]
    term_count = stiff_blocks.shape[0]
    block_width = stiff_blocks.shape[3]
    block_rows = cell_count // block_width
    groups = lax.axis_size("term")
    total_rows = local_rows * groups
    rim_cells = 2 * block_width
    panel = gather_term(chaos_field, block_width)
    extended = panel.reshape(block_rows + 4, load_count * total_rows, block_width)
    block_size = triple_blocks.shape[2]
    levels = jnp.arange(total_rows // block_size, dtype=jnp.int32)
    row_hot = (triple_pattern[:, :, 0:1] == levels).astype(jnp.float32)
    col_hot = (triple_pattern[:, :, 1:2] == levels).astype(jnp.float32)
    dense = jnp.einsum("kna,knb,knxy->kaxby", row_hot, col_hot, triple_blocks.astype(jnp.float32))
    dense = dense.reshape(term_count, total_rows, CLASSES // PAIR, groups // CLASSES, PAIR, local_rows)
    dense = dense.transpose(0, 1, 2, 4, 3, 5).reshape(term_count, total_rows, total_rows)
    dense = dense.astype(jnp.bfloat16)
    summed = image_scatter(stiff_offsets, extended, stiff_blocks, dense, local_rows)
    return summed.reshape(local_rows, load_count, cell_count)


def solution(mesh):
    return jax.shard_map(
        per_device,
        mesh=mesh,
        in_specs=(
            P("term", None, "space"),
            P("term", "space", None, None, None),
            P("term", "space", None),
            P("term", None, None, None),
            P("term", None, None),
        ),
        out_specs=P("term", None, "space"),
        check_vma=False,
    )
```

```python
import jax
import jax.numpy as jnp
from jax import lax
from jax.experimental import pallas as pl
from jax.experimental.pallas import tpu as pltpu
from jax.sharding import PartitionSpec as P

MESH_ID = pl.DeviceIdType.MESH


CLASSES = 4
PAIR = 2


def gather_kernel(block_ref, panel_ref, out_ref, flat_ref, local_sem, send_near, recv_near, send_far,
                  recv_far, halo_send, halo_recv):
    count = out_ref.shape[0]
    slabs = lax.axis_size("space")
    rim = (panel_ref.shape[0] - block_ref.shape[2] // panel_ref.shape[-1]) // 2
    rows, loads, cells = block_ref.shape
    for load in range(loads):
        flat_ref[load * rows:(load + 1) * rows, :] = block_ref[:, load, :]
    chunk = count // CLASSES
    row, stride, lane, far_peer, near_peer = scatter_peers(chunk, CLASSES)
    barrier = pltpu.get_barrier_semaphore()

    def greet_far(step, carry):
        pl.semaphore_signal(barrier, 1, device_id=(row, far_peer(step)), device_id_type=MESH_ID)
        return carry

    def greet_near(step, carry):
        pl.semaphore_signal(barrier, 1, device_id=(row, near_peer(step)), device_id_type=MESH_ID)
        return carry

    lax.fori_loop(1, chunk, greet_far, 0)
    lax.fori_loop(1, CLASSES, greet_near, 0)
    me = lax.axis_index("term")
    has_left = row > 0
    has_right = row < slabs - 1

    @pl.when(has_left)
    def _():
        pl.semaphore_signal(barrier, 1, device_id=(row - 1, me), device_id_type=MESH_ID)

    @pl.when(has_right)
    def _():
        pl.semaphore_signal(barrier, 1, device_id=(row + 1, me), device_id_type=MESH_ID)

    pl.semaphore_wait(
        barrier, chunk + CLASSES - 2 + has_left.astype(jnp.int32) + has_right.astype(jnp.int32)
    )

    mine = lane * chunk + stride
    local = pltpu.make_async_copy(flat_ref, out_ref.at[mine], local_sem)
    local.start()

    def far_out(step):
        return pltpu.make_async_remote_copy(
            flat_ref, out_ref.at[mine], send_far.at[step], recv_far.at[stride],
            device_id=(row, far_peer(step)), device_id_type=MESH_ID,
        )

    def far_in(step):
        source = lax.rem(stride + chunk - step, chunk)
        return pltpu.make_async_remote_copy(
            flat_ref, out_ref.at[lane * chunk + source], send_far.at[step], recv_far.at[source],
            device_id=(row, term_device(lane, source, chunk)), device_id_type=MESH_ID,
        )

    def far_start(step, carry):
        far_out(step).start()
        return carry

    def far_finish(step, carry):
        far_out(step).wait_send()
        far_in(step).wait_recv()
        return carry

    lax.fori_loop(1, chunk, far_start, 0)
    local.wait()
    lax.fori_loop(1, chunk, far_finish, 0)

    own = out_ref.at[pl.ds(lane * chunk, chunk)]

    def near_out(step):
        return pltpu.make_async_remote_copy(
            own, own, send_near.at[step], recv_near.at[lane],
            device_id=(row, near_peer(step)), device_id_type=MESH_ID,
        )

    def near_in(step):
        source = lax.rem(lane + CLASSES - step, CLASSES)
        theirs = out_ref.at[pl.ds(source * chunk, chunk)]
        return pltpu.make_async_remote_copy(
            theirs, theirs, send_near.at[step], recv_near.at[source],
            device_id=(row, term_device(source, stride, chunk)), device_id_type=MESH_ID,
        )

    def near_start(step, carry):
        near_out(step).start()
        return carry

    def near_finish(step, carry):
        near_out(step).wait_send()
        near_in(step).wait_recv()
        return carry

    lax.fori_loop(1, CLASSES, near_start, 0)
    lax.fori_loop(1, CLASSES, near_finish, 0)

    width = panel_ref.shape[-1]
    blocks = cells // width
    for slot in range(count):
        for load in range(loads):
            for block in range(blocks):
                panel_ref[rim + block, load, slot * rows:(slot + 1) * rows, :] = out_ref[
                    slot, load * rows:(load + 1) * rows, block * width:(block + 1) * width
                ]
    own = panel_ref.at[pl.ds(rim, blocks)]
    to_left = pltpu.make_async_remote_copy(
        own, panel_ref.at[pl.ds(rim + blocks, rim)], halo_send.at[0], halo_recv.at[0],
        device_id=(row - 1, me), device_id_type=MESH_ID,
    )
    to_right = pltpu.make_async_remote_copy(
        own, panel_ref.at[pl.ds(0, rim)], halo_send.at[1], halo_recv.at[1],
        device_id=(row + 1, me), device_id_type=MESH_ID,
    )

    @pl.when(has_left)
    def _():
        to_left.start()

    @pl.when(has_right)
    def _():
        to_right.start()

    @pl.when(jnp.logical_not(has_left))
    def _():
        panel_ref[pl.ds(0, rim)] = jnp.zeros((rim,) + panel_ref.shape[1:], panel_ref.dtype)

    @pl.when(jnp.logical_not(has_right))
    def _():
        panel_ref[pl.ds(rim + blocks, rim)] = jnp.zeros((rim,) + panel_ref.shape[1:], panel_ref.dtype)

    @pl.when(has_left)
    def _():
        to_left.wait_send()
        to_right.wait_recv()

    @pl.when(has_right)
    def _():
        to_right.wait_send()
        to_left.wait_recv()


def gather_term(block, width):
    count = lax.axis_size("term")
    return pl.pallas_call(
        gather_kernel,
        out_shape=jax.ShapeDtypeStruct(
            (block.shape[2] // width + 4, block.shape[1], count * block.shape[0], width), block.dtype
        ),
        in_specs=[pl.BlockSpec(memory_space=pltpu.VMEM)],
        out_specs=pl.BlockSpec(memory_space=pltpu.VMEM),
        scratch_shapes=[
            pltpu.VMEM((count, block.shape[0] * block.shape[1], block.shape[2]), block.dtype),
            pltpu.VMEM((block.shape[0] * block.shape[1], block.shape[2]), block.dtype),
            pltpu.SemaphoreType.DMA(()),
            pltpu.SemaphoreType.DMA((CLASSES,)),
            pltpu.SemaphoreType.DMA((CLASSES,)),
            pltpu.SemaphoreType.DMA((count // CLASSES,)),
            pltpu.SemaphoreType.DMA((count // CLASSES,)),
            pltpu.SemaphoreType.DMA((2,)),
            pltpu.SemaphoreType.DMA((2,)),
        ],
        compiler_params=pltpu.CompilerParams(collective_id=0, has_side_effects=True),
    )(block)


def term_device(lane, stride, chunk):
    return (lane // PAIR) * (chunk * PAIR) + stride * PAIR + lane % PAIR


def scatter_peers(chunk, classes):
    me = lax.axis_index("term")
    row = lax.axis_index("space")
    ring = chunk * PAIR
    stride = lax.rem(me, ring) // PAIR
    lane = (me // ring) * PAIR + lax.rem(me, PAIR)

    def far_peer(step):
        return term_device(lane, lax.rem(stride + step, chunk), chunk)

    def near_peer(step):
        return term_device(lax.rem(lane + step, classes), stride, chunk)

    return row, stride, lane, far_peer, near_peer


def scatter_greet(chunk, classes):
    row, stride, lane, far_peer, near_peer = scatter_peers(chunk, classes)
    barrier = pltpu.get_barrier_semaphore()

    def greet_far(step, carry):
        pl.semaphore_signal(barrier, 1, device_id=(row, far_peer(step)), device_id_type=MESH_ID)
        return carry

    def greet_near(step, carry):
        pl.semaphore_signal(barrier, 1, device_id=(row, near_peer(step)), device_id_type=MESH_ID)
        return carry

    lax.fori_loop(1, chunk, greet_far, 0)
    lax.fori_loop(1, classes, greet_near, 0)


def image_kernel(offs_ref, panel_ref, stiff_ref, triple_ref, out_ref, total_ref, far_src,
                 near_slots, class_sum, far_slots, send_near, recv_near, send_far, recv_far):
    block = pl.program_id(0)
    term = pl.program_id(1)
    band = stiff_ref.shape[2]
    width = stiff_ref.shape[-1]
    sides, chunk, _, local_rows, columns = total_ref.shape
    classes = sides * PAIR
    rows = triple_ref.shape[1]
    loads = panel_ref.shape[1] // rows
    block_rows = columns // (loads * width)
    term_count = pl.num_programs(1)
    rim = (panel_ref.shape[0] - block_rows) // 2
    half = loads * width
    row, stride, lane, far_peer, near_peer = scatter_peers(chunk, classes)

    @pl.when((term == 0) & (block == 0))
    def _():
        scatter_greet(chunk, classes)
        total_ref[...] = jnp.zeros_like(total_ref)

    total = jnp.zeros((loads * rows, width), jnp.float32)
    for slot in range(band):
        place = block + rim + offs_ref[term, block, slot]
        total += lax.dot_general(
            panel_ref[place], stiff_ref[0, 0, slot],
            (((1,), (1,)), ((), ())), preferred_element_type=jnp.float32,
        )
    image = total.astype(jnp.bfloat16)
    for load in range(loads):
        column = pl.multiple_of((block * loads + load) * width, width)
        product = jnp.dot(
            triple_ref[0], image[load * rows:(load + 1) * rows], preferred_element_type=jnp.float32
        )
        total_ref[:, :, :, :, pl.ds(column, width)] += product.reshape(
            sides, chunk, PAIR, local_rows, width
        )

    def near_copy(step, part, inbound):
        cols = pl.ds(pl.multiple_of(part * half, half), half)
        if inbound:
            source = lax.rem(lane + classes - step, classes)
            return pltpu.make_async_remote_copy(
                total_ref.at[source // PAIR, :, source % PAIR, :, cols],
                near_slots.at[source, :, :, cols], send_near.at[part, step], recv_near.at[part, source],
                device_id=(row, term_device(source, stride, chunk)), device_id_type=MESH_ID,
            )
        target = lax.rem(lane + step, classes)
        return pltpu.make_async_remote_copy(
            total_ref.at[target // PAIR, :, target % PAIR, :, cols],
            near_slots.at[lane, :, :, cols], send_near.at[part, step], recv_near.at[part, lane],
            device_id=(row, near_peer(step)), device_id_type=MESH_ID,
        )

    @pl.when(term == term_count - 1)
    def _():
        @pl.when(block == 0)
        def _():
            pl.semaphore_wait(pltpu.get_barrier_semaphore(), chunk + classes - 2)

        def near_start(step, carry):
            near_copy(step, block, False).start()
            return carry

        lax.fori_loop(1, classes, near_start, 0)

    @pl.when((term == term_count - 1) & (block == block_rows - 1))
    def _():
        for part in range(block_rows):
            cols = pl.ds(part * half, half)

            def near_finish(step, total):
                near_copy(step, part, False).wait_send()
                near_copy(step, part, True).wait_recv()
                source = lax.rem(lane + classes - step, classes)
                return total + near_slots[source, :, :, cols]

            own = total_ref[lane // PAIR, :, lane % PAIR, :, cols]
            class_sum[:, :, cols] = lax.fori_loop(1, classes, near_finish, own)

        far_src[...] = class_sum[...].astype(far_src.dtype)

        def far_out(step):
            target = lax.rem(stride + step, chunk)
            return pltpu.make_async_remote_copy(
                far_src.at[target], far_slots.at[stride], send_far.at[step], recv_far.at[stride],
                device_id=(row, far_peer(step)), device_id_type=MESH_ID,
            )

        def far_in(step):
            source = lax.rem(stride + chunk - step, chunk)
            return pltpu.make_async_remote_copy(
                far_src.at[source], far_slots.at[source], send_far.at[step], recv_far.at[source],
                device_id=(row, term_device(lane, source, chunk)), device_id_type=MESH_ID,
            )

        def far_start(step, carry):
            far_out(step).start()
            return carry

        def far_finish(step, total):
            far_out(step).wait_send()
            far_in(step).wait_recv()
            source = lax.rem(stride + chunk - step, chunk)
            return total + far_slots[source].astype(jnp.float32)

        lax.fori_loop(1, chunk, far_start, 0)
        summed = lax.fori_loop(1, chunk, far_finish, class_sum[stride])
        for part in range(block_rows):
            for load in range(loads):
                source = (part * loads + load) * width
                target = (load * block_rows + part) * width
                out_ref[:, target:target + width] = summed[:, source:source + width]


def image_scatter(offsets, panel, stiff_blocks, dense, local_rows):
    term_count, block_rows, band, width, _ = stiff_blocks.shape
    places, stacked, _ = panel.shape
    rows = dense.shape[1]
    columns = stacked // rows * block_rows * width
    classes = CLASSES
    chunk = rows // (classes * local_rows)
    shape = (classes // PAIR, chunk, PAIR, local_rows, columns)
    return pl.pallas_call(
        image_kernel,
        out_shape=jax.ShapeDtypeStruct((local_rows, columns), jnp.float32),
        grid_spec=pltpu.PrefetchScalarGridSpec(
            num_scalar_prefetch=1,
            grid=(block_rows, term_count),
            in_specs=[
                pl.BlockSpec((places, stacked, width), lambda b, k, offs: (0, 0, 0)),
                pl.BlockSpec((1, 1, band, width, width), lambda b, k, offs: (k, b, 0, 0, 0)),
                pl.BlockSpec((1, rows, rows), lambda b, k, offs: (k, 0, 0)),
            ],
            out_specs=pl.BlockSpec((local_rows, columns), lambda b, k, offs: (0, 0)),
            scratch_shapes=[
                pltpu.VMEM(shape, jnp.float32),
                pltpu.VMEM((chunk, local_rows, columns), jnp.bfloat16),
                pltpu.VMEM((classes, chunk, local_rows, columns), jnp.float32),
                pltpu.VMEM((chunk, local_rows, columns), jnp.float32),
                pltpu.VMEM((chunk, local_rows, columns), jnp.bfloat16),
                pltpu.SemaphoreType.DMA((block_rows, classes)),
                pltpu.SemaphoreType.DMA((block_rows, classes)),
                pltpu.SemaphoreType.DMA((chunk,)),
                pltpu.SemaphoreType.DMA((chunk,)),
            ],
        ),
        compiler_params=pltpu.CompilerParams(collective_id=1, has_side_effects=True),
    )(offsets, panel, stiff_blocks, dense)


def with_halo(block, sides, width):
    for axis, dim in sides:
        count = lax.axis_size(axis)
        forward = [(i, i + 1) for i in range(count - 1)]
        backward = [(target, source) for source, target in forward]
        low = lax.ppermute(
            lax.slice_in_dim(block, block.shape[dim] - width, None, axis=dim), axis, forward
        )
        high = lax.ppermute(lax.slice_in_dim(block, 0, width, axis=dim), axis, backward)
        block = jnp.concatenate([low, block, high], axis=dim)
    return block


def per_device(chaos_field, stiff_blocks, stiff_offsets, triple_blocks, triple_pattern):
    local_rows = chaos_field.shape[0]
    load_count = chaos_field.shape[1]
    cell_count = chaos_field.shape[2]
    term_count = stiff_blocks.shape[0]
    block_width = stiff_blocks.shape[3]
    block_rows = cell_count // block_width
    groups = lax.axis_size("term")
    total_rows = local_rows * groups
    rim_cells = 2 * block_width
    panel = gather_term(chaos_field, block_width)
    extended = panel.reshape(block_rows + 4, load_count * total_rows, block_width)
    block_size = triple_blocks.shape[2]
    levels = jnp.arange(total_rows // block_size, dtype=jnp.int32)
    row_hot = (triple_pattern[:, :, 0:1] == levels).astype(jnp.float32)
    col_hot = (triple_pattern[:, :, 1:2] == levels).astype(jnp.float32)
    dense = jnp.einsum("kna,knb,knxy->kaxby", row_hot, col_hot, triple_blocks.astype(jnp.float32))
    dense = dense.reshape(term_count, total_rows, CLASSES // PAIR, groups // CLASSES, PAIR, local_rows)
    dense = dense.transpose(0, 1, 2, 4, 3, 5).reshape(term_count, total_rows, total_rows)
    dense = dense.astype(jnp.bfloat16)
    summed = image_scatter(stiff_offsets, extended, stiff_blocks, dense, local_rows)
    return summed.reshape(local_rows, load_count, cell_count)


def solution(mesh):
    return jax.shard_map(
        per_device,
        mesh=mesh,
        in_specs=(
            P("term", None, "space"),
            P("term", "space", None, None, None),
            P("term", "space", None),
            P("term", None, None, None),
            P("term", None, None),
        ),
        out_specs=P("term", None, "space"),
        check_vma=False,
    )
```
